32 devices in a mesh: tile: 8 (over y, x, core), sec: 4 (over z).
Axes of the slice: x: 2, y: 2, z: 4, core: 2. Of those that a mesh axis runs over, the one named last changes fastest.
Arguments:
- pixels: bfloat16 [8, 64, 1024, 256], P('sec', 'tile'), may hold values from -6 to 6
- pred_features: bfloat16 [64, 1024, 128], P('tile'), may hold values from -6 to 6
- offsets: int32 [8, 2, 64, 1024], P('sec', None, 'tile'), may hold values from -1 to 1
- valid_mask: int32 [8, 64, 1024], P('sec', 'tile'), may hold values 0 or 1
- base_shift: float32 [2, 64, 1024], P(None, 'tile'), may hold values from -6 to 6
- w_hidden: bfloat16 [256, 512], replicated, may hold values from -0.375 to 0.375
- w_feature: bfloat16 [512, 128], replicated, may hold values from -0.25 to 0.25
- feat_gain: float32 [128], replicated, may hold values from 0.25 to 1.75
Outputs:
- displacement: float32 [8, 2, 64, 1024], P('sec', None, 'tile')
The draws below stay inside these ranges and needn't reach their ends.
All inputs are finite; a program needn't handle non-finite values. No bound on the sum of `valid_mask` on one device may be relied on, other than what follows from the above.
Results may differ from the reference program's by a relative error of at most 0.0024.
Values may be sent and summed in bfloat16 or wider, within the bound.
No kernel may reach another device: no remote copies, remote signals or barrier semaphores. Data moves between devices by JAX's collectives and lax.ppermute only.
A program may use at most 128 MiB of HBM per device.

```python
import jax
import jax.numpy as jnp
from jax import lax

PATCH = 256
HID = 512
FEAT = 128
COLS = 1024
ITERS = 8
SECS = 8
ROWS = 64


def with_ends(array, key, least, top_value):
    longest = array.shape.index(max(array.shape))
    spots = []
    for shift in (0, 1):
        where = [jax.random.randint(jax.random.fold_in(key, axis), (), 0, length) for axis, length in enumerate(array.shape)]
        where[longest] = (where[longest] + shift) % array.shape[longest]
        spots.append(tuple(where))
    return array.at[spots[0]].set(least).at[spots[1]].set(top_value)


def levels(stream_key, shape, cuts, smallest, top_value):
    def one(axis_at, shards_of):
        draws = jax.random.uniform(jax.random.fold_in(jax.random.fold_in(stream_key, 6), axis_at), (shards_of,), jnp.float32, smallest / len(cuts), top_value / len(cuts))
        return jnp.repeat(jnp.exp(draws), shape[axis_at] // shards_of).reshape((-1,) + (1,) * (len(shape) - axis_at - 1))

    level = one(*cuts[0])
    for cut in cuts[1:]:
        level = level * one(*cut)
    return level


def bell_draw(own_key, dims, scale, bound, shards=(), held_as=jnp.bfloat16):
    values = jax.random.normal(own_key, dims, jnp.float32) * scale
    if len(shards) > 0:
        values = levels(own_key, dims, shards, -0.22, 0.18) * values
    return jnp.clip(values, min=-bound, max=bound).astype(held_as)


def setup_inputs(seed: int = 0) -> dict:
    streams_of = jax.random.split(jax.random.key(seed), 9)
    pixels = bell_draw(streams_of[0], (SECS, ROWS, COLS, PATCH), 1.0, 6.0, ((0, 4), (1, 8)))
    pred_features = bell_draw(streams_of[1], (ROWS, COLS, FEAT), 1.0, 6.0, ((0, 8),))
    offsets = with_ends(jax.random.randint(streams_of[2], (SECS, 2, ROWS, COLS), -1, 2), jax.random.fold_in(streams_of[2], 1), -1, 1).astype(jnp.int32)
    valid_mask = with_ends((jax.random.randint(streams_of[3], (SECS, ROWS, COLS), 0, 4) < 3).astype(jnp.int32), jax.random.fold_in(streams_of[3], 1), 0, 1)
    base_shift = bell_draw(streams_of[4], (2, ROWS, COLS), 1.0, 6.0, ((1, 8),), jnp.float32)
    w_hidden = bell_draw(streams_of[5], (PATCH, HID), PATCH ** -0.5, 0.375)
    w_feature = bell_draw(streams_of[6], (HID, FEAT), HID ** -0.5, 0.25)
    feat_gain = jnp.clip(1.0 + 0.15 * jax.random.normal(streams_of[7], (FEAT,), jnp.float32), 0.25, 1.75)
    return dict(pixels=pixels, pred_features=pred_features, offsets=offsets, valid_mask=valid_mask, base_shift=base_shift, w_hidden=w_hidden, w_feature=w_feature, feat_gain=feat_gain)


epsilon = 1e-05
step_size = 0.2
stiffness = 0.5

def encode(section_pixels, w_hidden, w_feature, feat_gain):
    flat = section_pixels.reshape(-1, section_pixels.shape[-1])
    hidden = jax.nn.relu(jnp.dot(flat, w_hidden, preferred_element_type=jnp.float32)).astype(jnp.bfloat16)
    pre = jnp.dot(hidden, w_feature, preferred_element_type=jnp.float32)
    scale = lax.rsqrt(lax.optimization_barrier(jnp.mean(pre * pre, axis=-1, keepdims=True)) + epsilon)
    result = (pre * scale * feat_gain).astype(jnp.bfloat16)
    return result.reshape(section_pixels.shape[:-1] + (w_feature.shape[1],))

def flow_field(feature, ref_rows, offsets):
    rows = feature.shape[-3]
    cols = feature.shape[-2]
    padding = [(0, 0)] * (ref_rows.ndim - 2) + [(2, 2), (0, 0)]
    padded = jnp.pad(ref_rows, padding)
    own = feature.astype(jnp.float32)
    scores = {}
    for shift_y in range(-2, 3):
        for shift_x in range(-2, 3):
            window = padded[..., 2 + shift_y:2 + shift_y + rows, 2 + shift_x:2 + shift_x + cols, :]
            scores[shift_y, shift_x] = lax.optimization_barrier(jnp.sum(own * window.astype(jnp.float32), axis=-1)) / own.shape[-1]
    offset_y = offsets[..., 0, :, :]
    offset_x = offsets[..., 1, :, :]
    total = jnp.ones(offset_y.shape, jnp.float32)
    sum_y = jnp.zeros(offset_y.shape, jnp.float32)
    sum_x = jnp.zeros(offset_y.shape, jnp.float32)
    for near_y in (-1, 0, 1):
        for near_x in (-1, 0, 1):
            picked = jnp.zeros(offset_y.shape, jnp.float32)
            for cand_y in (-1, 0, 1):
                for cand_x in (-1, 0, 1):
                    hit = (offset_y == cand_y) & (offset_x == cand_x)
                    picked = picked + jnp.where(hit, scores[cand_y + near_y, cand_x + near_x], 0.0)
            weight = picked * picked
            total = total + weight
            sum_y = sum_y + weight * near_y
            sum_x = sum_x + weight * near_x
    flow_y = offset_y.astype(jnp.float32) + sum_y / total
    flow_x = offset_x.astype(jnp.float32) + sum_x / total
    return jnp.stack([flow_y, flow_x], axis=-3)

def relax_step(padded, flow, weight):
    center = padded[:, :, 1:-1]
    upper = padded[:, :, :-2]
    lower = padded[:, :, 2:]
    sided = jnp.pad(center, ((0, 0), (0, 0), (0, 0), (1, 1)))
    left_side = sided[..., :-2]
    right_side = sided[..., 2:]
    return center + step_size * (upper + lower + left_side + right_side - 4.0 * center + weight * (flow - center))

def reference(pixels, pred_features, offsets, valid_mask, base_shift, w_hidden, w_feature, feat_gain):
    features = lax.map(lambda section: encode(section, w_hidden, w_feature, feat_gain), pixels)
    references = jnp.concatenate([pred_features[None], features[:-1]], axis=0)
    ref_padded = jnp.pad(references, ((0, 0), (2, 2), (0, 0), (0, 0)))

    def one_flow(items):
        return flow_field(items[0], items[1], items[2])
    flow = lax.map(one_flow, (features, ref_padded, offsets))
    weight = stiffness * valid_mask.astype(jnp.float32)[:, None]
    field = jnp.zeros(flow.shape, jnp.float32)
    for step in range(ITERS):
        padded = jnp.pad(field, ((0, 0), (0, 0), (1, 1), (0, 0)))
        field = relax_step(padded, flow, weight)
    return base_shift[None] + jnp.cumsum(field, axis=0)
```

```python
import functools

import jax
import jax.numpy as jnp
from jax import lax
from jax.experimental import pallas as pl
from jax.experimental.pallas import tpu as pltpu
from jax.sharding import PartitionSpec as P

ITERS = 8
REACH = 2
LANES = 128
BASE = 16
PAD = LANES
SEG = 16
EDGE = 16

epsilon = 1e-05
step_size = 0.2
stiffness = 0.5

F32 = jnp.float32
BF16 = jnp.bfloat16
HBM = pl.BlockSpec(memory_space=pl.ANY)
VMEM = pl.BlockSpec(memory_space=pltpu.VMEM)
UNROLL = 8


def hop(value, axis, steps):
    count = lax.axis_size(axis)
    pairs = [(i, i + steps) for i in range(count) if 0 <= i + steps < count]
    return lax.ppermute(value, axis, pairs)


def hop_plane(value, steps):
    tiles = lax.axis_size("tile")
    secs = lax.axis_size("sec")
    pairs = [(i * secs, (i + steps) * secs) for i in range(tiles) if 0 <= i + steps < tiles]
    return lax.ppermute(value, ("tile", "sec"), pairs)


def params(limit=48):
    return pltpu.CompilerParams(vmem_limit_bytes=limit * 1024 * 1024)


def encode_chunk(pix, wh, wf, gain):
    hidden = jnp.maximum(jnp.dot(pix, wh, preferred_element_type=F32), 0.0).astype(BF16)
    pre = jnp.dot(hidden, wf, preferred_element_type=F32)
    mean = jnp.mean(pre * pre, axis=-1, keepdims=True)
    return (pre * lax.rsqrt(mean + epsilon) * gain).astype(BF16)


def chunk_of(width):
    for parts in (2, 3, 4):
        if width % (parts * 16) == 0 and width // parts <= 264:
            return width // parts
    return width


def encode_groups(groups, pix_ref, wh_ref, wf_ref, gain_ref, pix_s, sem):
    copies = []
    at = 0
    for sec, row0, nrows, col0, width, _, _ in groups:
        copy = pltpu.make_async_copy(
            pix_ref.at[sec, row0 : row0 + nrows, col0 : col0 + width, :],
            pix_s.at[at : at + nrows, 0:width, :],
            sem.at[len(copies)],
        )
        copy.start()
        copies.append(copy)
        at += nrows
    at = 0
    for copy, (_, _, nrows, _, width, store, done) in zip(copies, groups):
        copy.wait()
        chunk = chunk_of(width)
        parts = width // chunk

        def body(n, carry, at=at, parts=parts, chunk=chunk, store=store):
            row = n // parts
            offset = pl.multiple_of((n % parts) * chunk, 16)
            value = encode_chunk(
                pix_s[at + row, pl.ds(offset, chunk), :], wh_ref[...], wf_ref[...], gain_ref[...]
            )
            store(row, offset, chunk, value)
            return carry

        lax.fori_loop(0, nrows * parts, body, 0)
        done()
        at += nrows


def store_rows(ref, first):
    def store(row, offset, chunk, value):
        ref[first + row, pl.ds(offset, chunk), :] = value

    return store


def nothing():
    pass


def encode_edge_kernel(half, pix_ref, wh_ref, wf_ref, gain_ref, fwd_ref, pix_s, sem):
    width = fwd_ref.shape[1]
    rows = pix_ref.shape[1]
    groups = [
        (1, 0, REACH, 0, width, store_rows(fwd_ref, 0), nothing),
        (1, rows - REACH, REACH, 0, width, store_rows(fwd_ref, REACH), nothing),
    ]
    encode_groups(groups, pix_ref, wh_ref, wf_ref, gain_ref, pix_s, sem)


def encode_cross_kernel(
    half, pix_ref, wh_ref, wf_ref, gain_ref, off_ref, mask_ref, fwd_ref, bwd_ref, pix_s, sem
):
    width = fwd_ref.shape[1]
    rows, cols = pix_ref.shape[1:3]

    def store_bwd(row, offset, chunk, value):
        at = pl.multiple_of(row * width + offset, 16)
        bwd_ref[pl.ds(at, chunk), :] = value

    groups = [
        (0, 0, rows, cols - width, width, store_bwd, nothing),
        (1, REACH, rows - 2 * REACH, 0, width, store_rows(fwd_ref, 0), nothing),
    ]
    first = half // LANES - 1
    for tile in range(cols // LANES - first):
        lanes = slice((first + tile) * LANES, (first + tile + 1) * LANES)
        extra = jnp.concatenate(
            [off_ref[0, 0, :, lanes], off_ref[0, 1, :, lanes], mask_ref[0, :, lanes], mask_ref[0, :, lanes]], 0
        )
        at = rows * width + tile * 4 * rows
        bwd_ref[at : at + 4 * rows, :] = extra.astype(F32).astype(BF16)
    encode_groups(groups, pix_ref, wh_ref, wf_ref, gain_ref, pix_s, sem)


def encode_border_kernel(
    half, pix_ref, wh_ref, wf_ref, gain_ref, edge_ref, bwd_ref,
    eb_ref, ob_ref, up_ref, down_ref, pix_s, sem, csem,
):
    rows, cols = pix_ref.shape[1:3]
    width = edge_ref.shape[1]
    rest = cols - half
    copies = []

    def copy(src, dst):
        c = pltpu.make_async_copy(src, dst, csem.at[len(copies)])
        c.start()
        copies.append(c)

    for pack, row0, edge0 in ((up_ref, rows - REACH, REACH), (down_ref, 0, 0)):
        for r in range(REACH):
            copy(
                bwd_ref.at[pl.ds((row0 + r) * width + width - rest, rest), :],
                pack.at[r, half : half + rest, :],
            )
            copy(
                edge_ref.at[edge0 + r, half - 2 * EDGE : half, :],
                pack.at[r, cols : cols + 2 * EDGE, :],
            )

    def store_both(ref, first, pack, lead):
        def store(row, offset, chunk, value):
            ref[first + row, pl.ds(offset, chunk), :] = value
            pack[row, pl.ds(pl.multiple_of(lead + offset, 16), chunk), :] = value

        return store

    groups = []
    for pack, row0, first in ((down_ref, 0, 0), (up_ref, rows - REACH, REACH)):
        groups.append((0, row0, REACH, 0, half, store_both(eb_ref, first, pack, 0), nothing))
        groups.append(
            (1, row0, REACH, half, rest, store_both(ob_ref, first, pack, cols + 2 * EDGE), nothing)
        )
    encode_groups(groups, pix_ref, wh_ref, wf_ref, gain_ref, pix_s, sem)
    for c in copies:
        c.wait()


def encode_inner_kernel(half, pix_ref, wh_ref, wf_ref, gain_ref, ei_ref, oi_ref, pix_s, sem):
    rows, cols = pix_ref.shape[1:3]
    inner = rows - 2 * REACH
    groups = [
        (0, REACH, inner, 0, half, store_rows(ei_ref, 0), nothing),
        (1, REACH, inner, half, cols - half, store_rows(oi_ref, 0), nothing),
    ]
    encode_groups(groups, pix_ref, wh_ref, wf_ref, gain_ref, pix_s, sem)


def flops_of(nodes, patch, hid, feat):
    return pl.CostEstimate(
        flops=2 * nodes * hid * (patch + feat), bytes_accessed=nodes * 2 * (patch + feat), transcendentals=nodes
    )


def align(band, first, row, lane):
    band = pltpu.roll(band, (2 * LANES - first - BASE + 2) % LANES, 1)
    for shift in (1, 2, 4):
        band = jnp.where((row & shift) != 0, pltpu.roll(band, LANES - shift, 1), band)
    return band


def score_tile(q_s, ref_s, s_s, r, k, low):
    lane = lax.broadcasted_iota(jnp.int32, (8, LANES), 1)
    row = lax.broadcasted_iota(jnp.int32, (8, LANES), 0)
    span = 2 * REACH + 1
    query = q_s[r, pl.ds(pl.multiple_of(k * LANES + low, 16), LANES - low), :]
    products = []
    for a in range(span):
        start = pl.multiple_of(k * LANES + (PAD - BASE - SEG * a), 16)
        window = ref_s[r + a, pl.ds(start, 2 * LANES), :]
        products.append(
            lax.dot_general(query, window, (((1,), (1,)), ((), ())), preferred_element_type=F32)
        )
    groups = [jnp.zeros((8, LANES), F32)] * (low // 8)
    for i in range(low // 8, LANES // 8):
        at = 8 * i - low
        pieces = []
        for a in range(span):
            s = 8 * i + BASE - 4 + SEG * a
            if s < LANES:
                pieces.append((s, a, 0))
            if s + SEG > LANES:
                pieces.append((max(s, LANES) - LANES, a, LANES))
        band = None
        for s, a, h in sorted(pieces):
            value = products[a][at : at + 8, h : h + LANES]
            band = value if band is None else jnp.where(lane >= s, value, band)
        groups.append(align(band, 8 * i, row, lane))
    turned = jnp.concatenate(groups, 0).T
    s_s[r, :, pl.ds(pl.multiple_of(k * LANES, LANES), LANES)] = turned[: SEG * span]


def score_job(q_s, ref_s, s_s, tiles, low=0):
    rows = q_s.shape[0]
    first = 1 if low else 0
    count = tiles - first

    def body(n, carry):
        score_tile(q_s, ref_s, s_s, n // count, n % count + first, 0)
        return carry

    lax.fori_loop(0, rows * count, body, 0, unroll=UNROLL)
    if low:

        def edge(r, carry):
            score_tile(q_s, ref_s, s_s, r, 0, low)
            return carry

        lax.fori_loop(0, rows, edge, 0, unroll=4)


def flow_tile(s_s, oy, ox, lanes):
    y_low, y_high, x_low, x_high = oy < 0, oy > 0, ox < 0, ox > 0
    feat = F32(1.0 / LANES)
    by_row = {}
    for i in range(3):
        for b in range(5):
            v = [s_s[:, SEG * (i + d) + b, lanes] for d in range(3)]
            by_row[i, b] = jnp.where(y_low, v[0], jnp.where(y_high, v[2], v[1]))
    total = jnp.ones_like(oy)
    sum_y = jnp.zeros_like(oy)
    sum_x = jnp.zeros_like(oy)
    for i in range(3):
        for j in range(3):
            near = jnp.where(
                x_low, by_row[i, j], jnp.where(x_high, by_row[i, j + 2], by_row[i, j + 1])
            )
            near = near * feat
            weight = near * near
            total = total + weight
            if i != 1:
                sum_y = sum_y + weight * (i - 1)
            if j != 1:
                sum_x = sum_x + weight * (j - 1)
    return oy + sum_y / total, ox + sum_x / total


def flows_of(s_s, off_ref, flow_ref, tiles):
    def body(k, carry):
        lanes = pl.ds(pl.multiple_of(k * LANES, LANES), LANES)
        fy, fx = flow_tile(s_s, off_ref[0, :, lanes].astype(F32), off_ref[1, :, lanes].astype(F32), lanes)
        flow_ref[0, :, lanes] = fy
        flow_ref[1, :, lanes] = fx
        return carry

    lax.fori_loop(0, tiles, body, 0)


class Loads:
    def __init__(self, sem, first=0):
        self.sem, self.next, self.open = sem, first, []

    def __call__(self, src, dst):
        copy = pltpu.make_async_copy(src, dst, self.sem.at[self.next])
        copy.start()
        self.next += 1
        self.open.append(copy)

    def wait(self):
        for copy in self.open:
            copy.wait()
        self.open = []


def zero_sides(ref_s, cols):
    side = jnp.zeros((ref_s.shape[0], EDGE, ref_s.shape[2]), BF16)
    ref_s[:, PAD - EDGE : PAD, :] = side
    ref_s[:, PAD + cols : PAD + cols + EDGE, :] = side


def own_scores_kernel(
    half, edge_ref, fwdb_ref, bwd_ref, eb_ref, ei_ref, ob_ref, oi_ref, up_ref, down_ref,
    pred_ref, pup_ref, pdown_ref, off_ref, flow_ref, flow0_ref,
    q_s, ref_s, s_s, q0_s, ref0_s, sem,
):
    rows, cols = q_s.shape[:2]
    width = edge_ref.shape[1]
    rest = cols - half
    last = rows - REACH
    is_first = lax.axis_index("sec") == 0
    base0 = half - LANES
    loads = Loads(sem)
    own = slice(PAD, PAD + half)
    far = slice(PAD + half, PAD + cols)
    for row0, part in ((0, 0), (last, REACH)):
        dst = slice(row0, row0 + REACH)
        ref_dst = slice(row0 + REACH, row0 + 2 * REACH)
        src = slice(part, part + REACH)
        loads(edge_ref.at[src, 0:half, :], q_s.at[dst, 0:half, :])
        loads(ob_ref.at[src], q_s.at[dst, half:cols, :])
        loads(eb_ref.at[src], ref_s.at[ref_dst, own, :])
    loads(fwdb_ref.at[:, 0:half, :], q_s.at[REACH:last, 0:half, :])
    loads(oi_ref, q_s.at[REACH:last, half:cols, :])
    loads(ei_ref, ref_s.at[2 * REACH : rows, own, :])
    for r in range(rows):
        loads(bwd_ref.at[pl.ds(r * width + width - rest, rest), :], ref_s.at[r + REACH, far, :])
    loads(up_ref.at[:, 0:cols, :], ref_s.at[0:REACH, PAD : PAD + cols, :])
    loads(down_ref.at[:, 0:cols, :], ref_s.at[rows + REACH : rows + 2 * REACH, PAD : PAD + cols, :])
    zero_sides(ref_s, cols)
    at = loads.next

    def first_loads():
        loads0 = Loads(sem, at)
        for r in range(rows):
            loads0(
                bwd_ref.at[pl.ds(r * width, width), :],
                q0_s.at[r, LANES + rest - width : LANES + rest, :],
            )
        span = slice(base0, cols)
        to = slice(PAD, PAD + cols - base0)
        loads0(pred_ref.at[:, span, :], ref0_s.at[REACH : rows + REACH, to, :])
        loads0(pup_ref.at[:, span, :], ref0_s.at[0:REACH, to, :])
        loads0(pdown_ref.at[:, span, :], ref0_s.at[rows + REACH : rows + 2 * REACH, to, :])
        return loads0

    @pl.when(is_first)
    def _():
        first_loads().wait()

    loads.wait()
    score_job(q_s, ref_s, s_s, cols // LANES)
    flows_of(s_s, off_ref.at[1], flow_ref, cols // LANES)
    flow0_ref[...] = jnp.zeros_like(flow0_ref)

    @pl.when(is_first)
    def _():
        zero_sides(ref0_s, cols - base0)
        tiles = (cols - base0) // LANES
        score_job(q0_s, ref0_s, s_s, tiles, LANES - EDGE)
        flows_of(s_s, off_ref.at[0, :, :, base0:cols], flow0_ref, tiles)


def back_scores_kernel(
    half, q_ref, edge_ref, fwdb_ref, ob_ref, oi_ref, up_ref, down_ref, flow_ref,
    q_s, ref_s, s_s, off_s, sem,
):
    rows, span = q_s.shape[:2]
    width = edge_ref.shape[1]
    rest = span - LANES
    cols = half + rest
    last = rows - REACH
    loads = Loads(sem)
    for r in range(rows):
        loads(q_ref.at[pl.ds(r * width, width), :], q_s.at[r, span - width : span, :])
    lead = PAD + LANES
    gap = 2 * EDGE
    for row0, part in ((0, 0), (last, REACH)):
        dst = slice(row0 + REACH, row0 + 2 * REACH)
        src = slice(part, part + REACH)
        loads(edge_ref.at[src, half - gap : half, :], ref_s.at[dst, lead - gap : lead, :])
        loads(ob_ref.at[src], ref_s.at[dst, lead : lead + rest, :])
    loads(fwdb_ref.at[:, half - gap : half, :], ref_s.at[2 * REACH : rows, lead - gap : lead, :])
    loads(oi_ref, ref_s.at[2 * REACH : rows, lead : lead + rest, :])
    pack = slice(cols, cols + gap + rest)
    to = slice(lead - gap, lead + rest)
    loads(up_ref.at[:, pack, :], ref_s.at[0:REACH, to, :])
    loads(down_ref.at[:, pack, :], ref_s.at[rows + REACH : rows + 2 * REACH, to, :])
    loads(q_ref.at[rows * width :, :], off_s)
    ref_s[:, lead + rest : lead + rest + EDGE, :] = jnp.zeros((rows + 2 * REACH, EDGE, LANES), BF16)
    loads.wait()
    tiles = span // LANES
    score_job(q_s, ref_s, s_s, tiles, LANES - EDGE)

    def body(k, carry):
        lanes = pl.ds(pl.multiple_of(k * LANES, LANES), LANES)
        extra = off_s[pl.ds(pl.multiple_of(k * 4 * rows, 4 * rows), 4 * rows), :].astype(F32)
        fy, fx = flow_tile(s_s, extra[:rows], extra[rows : 2 * rows], lanes)
        flow_ref[0, :, lanes] = fy
        flow_ref[1, :, lanes] = fx
        flow_ref[2, :, lanes] = extra[2 * rows : 3 * rows]
        return carry

    lax.fori_loop(0, tiles, body, 0)


def pairs_out(pack_ref, at, tops, bottoms):
    for n, (top, bottom) in enumerate(zip(tops, bottoms)):
        pack_ref[at + 16 * n : at + 16 * n + 16, :] = jnp.concatenate([top, bottom], 0).astype(BF16)
    return at + 16 * len(tops)


def front_scores_kernel(
    half, edge_ref, fwdb_ref, up_ref, down_ref, pred_ref, pup_ref, pdown_ref, eb_ref, ei_ref,
    off_ref, mask_ref, flow1_ref, flow0_ref, flow2_ref, flow_ref, pack_ref,
    q_s, ref_s, s_s, sem,
):
    rows = q_s.shape[0]
    cols = off_ref.shape[3]
    width = edge_ref.shape[1]
    last = rows - REACH
    is_first = lax.axis_index("sec") == 0
    loads = Loads(sem)
    for row0, part in ((0, 0), (last, REACH)):
        loads(eb_ref.at[part : part + REACH], q_s.at[row0 : row0 + REACH, :, :])
    loads(ei_ref, q_s.at[REACH:last, :, :])
    at = loads.next
    span = slice(PAD, PAD + width)

    @pl.when(is_first)
    def _():
        mine = Loads(sem, at)
        mine(pred_ref.at[:, 0:width, :], ref_s.at[REACH : rows + REACH, span, :])
        mine(pup_ref.at[:, 0:width, :], ref_s.at[0:REACH, span, :])
        mine(pdown_ref.at[:, 0:width, :], ref_s.at[rows + REACH : rows + 2 * REACH, span, :])
        mine.wait()

    @pl.when(jnp.logical_not(is_first))
    def _():
        mine = Loads(sem, at)
        mine(edge_ref.at[0:REACH], ref_s.at[REACH : 2 * REACH, span, :])
        mine(edge_ref.at[REACH : 2 * REACH], ref_s.at[rows : rows + REACH, span, :])
        mine(fwdb_ref, ref_s.at[2 * REACH : rows, span, :])
        mine(up_ref, ref_s.at[0:REACH, span, :])
        mine(down_ref, ref_s.at[rows + REACH : rows + 2 * REACH, span, :])
        mine.wait()

    loads.wait()
    ref_s[:, PAD - EDGE : PAD, :] = jnp.zeros((rows + 2 * REACH, EDGE, LANES), BF16)
    tiles = half // LANES
    score_job(q_s, ref_s, s_s, tiles)
    flow_ref[:, :, half:cols] = flow0_ref[:, :, LANES:]
    flows_of(s_s, off_ref.at[0], flow_ref, tiles)

    def tiles_of(ref, count):
        return [ref[:, n * LANES : (n + 1) * LANES] for n in range(count)]

    n = 0
    for ref, count in ((flow1_ref, cols // LANES), (flow_ref, cols // LANES), (flow2_ref, flow2_ref.shape[2] // LANES)):
        n = pairs_out(pack_ref, n, tiles_of(ref.at[0], count), tiles_of(ref.at[1], count))
    masks = []
    for ref, count in ((mask_ref.at[1], cols // LANES), (mask_ref.at[0], cols // LANES), (flow2_ref.at[2], flow2_ref.shape[2] // LANES)):
        masks += [m.astype(F32) for m in tiles_of(ref, count)]
    if len(masks) % 2:
        masks.append(masks[-1])
    pairs_out(pack_ref, n, masks[0::2], masks[1::2])


def relax_kernel(
    half, up_ref, down_ref, flow1_ref, flow3_ref, flow2_ref, mask_ref, f1_ref, f3_ref, msg_ref,
    field_s, pull_s, keep_s,
):
    rows, cols = flow1_ref.shape[1:]
    deep = rows + 2 * ITERS
    place = lax.axis_index("tile")
    count = lax.axis_size("tile")
    glob = place * rows + lax.broadcasted_iota(jnp.int32, (deep, LANES), 0) - ITERS
    inside = ((glob >= 0) & (glob < rows * count)).astype(F32)
    widths = (cols, cols, flow2_ref.shape[2])
    tiles = [w // LANES for w in widths]
    flows = (flow1_ref, flow3_ref, flow2_ref)
    own_masks = (mask_ref.at[1], mask_ref.at[0], flow2_ref.at[2])
    starts = [0, tiles[0], tiles[0] + tiles[1]]
    mask_at = 16 * sum(tiles)
    for job in range(3):
        for k in range(tiles[job]):
            lanes = slice(k * LANES, (k + 1) * LANES)
            at = 16 * (starts[job] + k)
            m_at = mask_at + 8 * (starts[job] + k)
            half_at = m_at // 16 * 16
            sub = slice(m_at - half_at, m_at - half_at + 8)
            upper = up_ref[at : at + 16, :].astype(F32)
            lower = down_ref[at : at + 16, :].astype(F32)
            m_up = up_ref[half_at : half_at + 16, :].astype(F32)[sub]
            m_down = down_ref[half_at : half_at + 16, :].astype(F32)[sub]
            weight = stiffness * jnp.concatenate(
                [m_up, own_masks[job][:, lanes].astype(F32), m_down], 0
            )
            keep_s[job, :, lanes] = (step_size - step_size * weight) * inside
            for c in range(2):
                flow = jnp.concatenate(
                    [upper[8 * c : 8 * c + 8], flows[job][c, :, lanes], lower[8 * c : 8 * c + 8]], 0
                )
                pull = step_size * weight * flow * inside
                pull_s[job, c, :, lanes] = pull
                field_s[job, c, :, lanes] = pull
    step = step_size * inside

    def body(n, carry):
        for job in range(3):
            wide = widths[job]
            for c in range(2):
                old = [field_s[job, c, :, k * LANES : (k + 1) * LANES] for k in range(tiles[job])]
                lane = lax.broadcasted_iota(jnp.int32, (deep, LANES), 1)
                nxt = [pltpu.roll(x, LANES - 1, 1) for x in old]
                prv = [pltpu.roll(x, 1, 1) for x in old]
                zero = jnp.zeros_like(old[0])
                for k in range(tiles[job]):
                    lanes = slice(k * LANES, (k + 1) * LANES)
                    right = jnp.where(lane == LANES - 1, nxt[k + 1] if k + 1 < tiles[job] else zero, nxt[k])
                    left = jnp.where(lane == 0, prv[k - 1] if k else zero, prv[k])
                    around = pltpu.roll(old[k], 1, 0) + pltpu.roll(old[k], deep - 1, 0) + left + right
                    field_s[job, c, :, lanes] = (
                        keep_s[job, :, lanes] * old[k] + step * around + pull_s[job, c, :, lanes]
                    )
        return carry

    lax.fori_loop(0, ITERS - 1, body, 0)
    is_first = lax.axis_index("sec") == 0
    seam = half - EDGE // 2
    mine = slice(ITERS, ITERS + rows)
    lead = half - LANES
    for c in range(2):
        for k in range(tiles[0]):
            lanes = slice(k * LANES, (k + 1) * LANES)
            col = lax.broadcasted_iota(jnp.int32, (rows, LANES), 1) + k * LANES
            one = field_s[0, c, mine, lanes]
            front = field_s[1, c, mine, lanes]
            if (k + 1) * LANES > seam:
                front = jnp.where((col < seam) | is_first, front, 0.0)
            total = one + front
            if k * LANES >= lead:
                back = field_s[2, c, mine, k * LANES - lead : (k + 1) * LANES - lead]
                total = total + jnp.where(col >= seam, back, 0.0)
            f1_ref[c, :, lanes] = one
            f3_ref[c, :, lanes] = front
            msg_ref[c, :, lanes] = total.astype(msg_ref.dtype)


def shards(pixels, pred, offsets, mask, base_shift, w_hidden, w_feature, feat_gain):
    secs, rows, cols, patch = pixels.shape
    hid, feat = w_feature.shape
    assert secs == 2 and rows == ITERS and feat == LANES and cols % (2 * LANES) == 0
    half = cols // 2
    rest = cols - half
    width = half + EDGE
    inner = rows - 2 * REACH
    span = rest + LANES
    deep = rows + 2 * REACH
    tail = 4 * rows * (span // LANES)
    gain = feat_gain.reshape(1, feat)
    shape = jax.ShapeDtypeStruct
    weights = (w_hidden, w_feature, gain)
    is_first = lax.axis_index("sec") == 0

    pup = hop_plane(pred[rows - REACH :], 1)
    pdown = hop_plane(pred[:REACH], -1)

    edge = pl.pallas_call(
        functools.partial(encode_edge_kernel, half),
        out_shape=shape((2 * REACH, width, feat), BF16),
        in_specs=[HBM, VMEM, VMEM, VMEM],
        out_specs=VMEM,
        scratch_shapes=[pltpu.VMEM((2 * REACH, width, patch), BF16), pltpu.SemaphoreType.DMA((2,))],
        compiler_params=params(),
        cost_estimate=flops_of(2 * REACH * width, patch, hid, feat),
        name="encode_edge",
    )(pixels, *weights)
    edge_in = hop(edge, "sec", 1)

    fwdb, bwd = pl.pallas_call(
        functools.partial(encode_cross_kernel, half),
        out_shape=(shape((inner, width, feat), BF16), shape((rows * width + tail, feat), BF16)),
        in_specs=[HBM, VMEM, VMEM, VMEM, VMEM, VMEM],
        out_specs=(VMEM, VMEM),
        scratch_shapes=[pltpu.VMEM((rows + inner, width, patch), BF16), pltpu.SemaphoreType.DMA((2,))],
        compiler_params=params(),
        cost_estimate=flops_of((rows + inner) * width, patch, hid, feat),
        name="encode_cross",
    )(pixels, *weights, offsets, mask)
    fwdb_in = hop(fwdb, "sec", 1)
    bwd_in = hop(bwd, "sec", -1)

    pack_cols = cols + 2 * EDGE + rest
    eb, ob, up, down = pl.pallas_call(
        functools.partial(encode_border_kernel, half),
        out_shape=(
            shape((2 * REACH, half, feat), BF16),
            shape((2 * REACH, rest, feat), BF16),
            shape((REACH, pack_cols, feat), BF16),
            shape((REACH, pack_cols, feat), BF16),
        ),
        in_specs=[HBM, VMEM, VMEM, VMEM, HBM, HBM],
        out_specs=(VMEM,) * 4,
        scratch_shapes=[
            pltpu.VMEM((4 * REACH, max(half, rest), patch), BF16),
            pltpu.SemaphoreType.DMA((4,)),
            pltpu.SemaphoreType.DMA((4 * REACH,)),
        ],
        compiler_params=params(),
        cost_estimate=flops_of(2 * REACH * cols, patch, hid, feat),
        name="encode_border",
    )(pixels, *weights, edge, bwd)
    up_in = hop(up, "tile", 1)
    down_in = hop(down, "tile", -1)

    ei, oi = pl.pallas_call(
        functools.partial(encode_inner_kernel, half),
        out_shape=(shape((inner, half, feat), BF16), shape((inner, rest, feat), BF16)),
        in_specs=[HBM, VMEM, VMEM, VMEM],
        out_specs=(VMEM, VMEM),
        scratch_shapes=[pltpu.VMEM((2 * inner, max(half, rest), patch), BF16), pltpu.SemaphoreType.DMA((2,))],
        compiler_params=params(),
        cost_estimate=flops_of(inner * cols, patch, hid, feat),
        name="encode_inner",
    )(pixels, *weights)

    fup_in = hop(edge_in[REACH:], "tile", 1)
    fdown_in = hop(edge_in[:REACH], "tile", -1)

    bands = SEG * (2 * REACH + 1)
    nodes = rows * cols

    def score_cost(part):
        return pl.CostEstimate(flops=int(part * nodes * 12 * 2 * 256 * 128), bytes_accessed=int(part * nodes * 512), transcendentals=0)

    flow1, flow0 = pl.pallas_call(
        functools.partial(own_scores_kernel, half),
        out_shape=(shape((2, rows, cols), F32), shape((2, rows, span), F32)),
        in_specs=[HBM] * 12 + [VMEM],
        out_specs=(VMEM, VMEM),
        scratch_shapes=[
            pltpu.VMEM((rows, cols, feat), BF16),
            pltpu.VMEM((deep, cols + 2 * PAD, feat), BF16),
            pltpu.VMEM((rows, bands, cols), F32),
            pltpu.VMEM((rows, span, feat), BF16),
            pltpu.VMEM((deep, span + 2 * PAD, feat), BF16),
            pltpu.SemaphoreType.DMA((32,)),
        ],
        compiler_params=params(),
        cost_estimate=score_cost(1.0),
        name="own_scores",
    )(edge, fwdb, bwd, eb, ei, ob, oi, up_in, down_in, pred, pup, pdown, offsets)

    flow2 = pl.pallas_call(
        functools.partial(back_scores_kernel, half),
        out_shape=shape((3, rows, span), F32),
        in_specs=[HBM] * 7,
        out_specs=VMEM,
        scratch_shapes=[
            pltpu.VMEM((rows, span, feat), BF16),
            pltpu.VMEM((deep, span + 2 * PAD, feat), BF16),
            pltpu.VMEM((rows, bands, span), F32),
            pltpu.VMEM((tail, feat), BF16),
            pltpu.SemaphoreType.DMA((20,)),
        ],
        compiler_params=params(),
        cost_estimate=score_cost(0.55),
        name="back_scores",
    )(bwd_in, edge, fwdb, ob, oi, up_in, down_in)

    tiles = 2 * (cols // LANES) + span // LANES
    pack_rows = 16 * tiles + 16 * ((tiles + 1) // 2)
    flow3, pack = pl.pallas_call(
        functools.partial(front_scores_kernel, half),
        out_shape=(shape((2, rows, cols), F32), shape((pack_rows, LANES), BF16)),
        in_specs=[HBM] * 9 + [VMEM] * 5,
        out_specs=(VMEM, VMEM),
        scratch_shapes=[
            pltpu.VMEM((rows, half, feat), BF16),
            pltpu.VMEM((deep, half + 3 * PAD, feat), BF16),
            pltpu.VMEM((rows, bands, half), F32),
            pltpu.SemaphoreType.DMA((12,)),
        ],
        compiler_params=params(),
        cost_estimate=score_cost(0.5),
        name="front_scores",
    )(edge_in, fwdb_in, fup_in, fdown_in, pred, pup, pdown, eb, ei, offsets, mask, flow1, flow0, flow2)
    pack_up = hop(pack, "tile", 1)
    pack_down = hop(pack, "tile", -1)

    wide = 24 if rows == 8 else rows + 2 * ITERS
    f1, f3, msg = pl.pallas_call(
        functools.partial(relax_kernel, half),
        out_shape=(shape((2, rows, cols), F32), shape((2, rows, cols), F32), shape((2, rows, cols), BF16)),
        in_specs=[VMEM] * 6,
        out_specs=(VMEM,) * 3,
        scratch_shapes=[
            pltpu.VMEM((3, 2, wide, cols), F32),
            pltpu.VMEM((3, 2, wide, cols), F32),
            pltpu.VMEM((3, wide, cols), F32),
        ],
        compiler_params=params(),
        cost_estimate=pl.CostEstimate(flops=nodes * 24 * 12 * 8, bytes_accessed=nodes * 40, transcendentals=0),
        name="relax",
    )(pack_up, pack_down, flow1, flow3, flow2, mask)

    prefix = base_shift
    for steps in range(1, lax.axis_size("sec")):
        prefix = prefix + hop(msg, "sec", steps).astype(F32)
    first = prefix + f3
    return jnp.stack([first, first + f1], axis=0)


def solution(mesh):
    in_specs = (
        P("sec", "tile", None, None),
        P("tile", None, None),
        P("sec", None, "tile", None),
        P("sec", "tile", None),
        P(None, "tile", None),
        P(),
        P(),
        P(),
    )
    out_specs = P("sec", None, "tile", None)
    return jax.shard_map(shards, mesh=mesh, in_specs=in_specs, out_specs=out_specs, check_vma=False)
```

```python
import functools

import jax
import jax.numpy as jnp
from jax import lax
from jax.experimental import pallas as pl
from jax.experimental.pallas import tpu as pltpu
from jax.sharding import PartitionSpec as P


ITERS = 8
REACH = 2
LANES = 128
BASE = 16
PAD = LANES
SEG = 16
EDGE = 16

epsilon = 1e-05
step_size = 0.2
stiffness = 0.5

F32 = jnp.float32
BF16 = jnp.bfloat16
HBM = pl.BlockSpec(memory_space=pl.ANY)
VMEM = pl.BlockSpec(memory_space=pltpu.VMEM)


def hop(value, axis, steps):
    count = lax.axis_size(axis)
    pairs = [(i, i + steps) for i in range(count) if 0 <= i + steps < count]
    return lax.ppermute(value, axis, pairs)


def hop_plane(value, steps):
    tiles = lax.axis_size("tile")
    secs = lax.axis_size("sec")
    pairs = [(i * secs, (i + steps) * secs) for i in range(tiles) if 0 <= i + steps < tiles]
    return lax.ppermute(value, ("tile", "sec"), pairs)


def params(limit=48):
    return pltpu.CompilerParams(vmem_limit_bytes=limit * 1024 * 1024)


def matmuls(pix, wh, wf):
    hidden = jnp.maximum(jnp.dot(pix, wh, preferred_element_type=F32), 0.0).astype(BF16)
    return jnp.dot(hidden, wf, preferred_element_type=F32)


def normed(pre, gain):
    mean = jnp.mean(pre * pre, axis=-1, keepdims=True)
    return (pre * lax.rsqrt(mean + epsilon) * gain).astype(BF16)


def encode_rows(pieces, store, pix_ref, wh_ref, wf_ref, gain_ref, pix_s, pre_s, sem):
    width = pix_s.shape[1]
    copies = []
    for n, (sec, row, col0) in enumerate(pieces):
        copy = pltpu.make_async_copy(
            pix_ref.at[sec, row, col0 : col0 + width, :], pix_s.at[n], sem.at[n]
        )
        copy.start()
        copies.append(copy)
    steps = len(pieces) // 2

    def finish(n):
        value = normed(pre_s[n % 2], gain_ref[...])
        store(2 * n, value[:width])
        store(2 * n + 1, value[width:])

    for n in range(steps):
        copies[2 * n].wait()
        copies[2 * n + 1].wait()
        pix = pix_s[2 * n : 2 * n + 2].reshape(2 * width, pix_s.shape[2])
        pre_s[n % 2] = matmuls(pix, wh_ref[...], wf_ref[...])
        if n:
            finish(n - 1)
    finish(steps - 1)


def encode_front_kernel(half, pix_ref, wh_ref, wf_ref, gain_ref, fwd_ref, pix_s, pre_s, sem):
    rows = pix_ref.shape[1]

    def store(n, value):
        fwd_ref[n] = value

    pieces = [(1, r, 0) for r in range(rows)]
    encode_rows(pieces, store, pix_ref, wh_ref, wf_ref, gain_ref, pix_s, pre_s, sem)


def encode_back_kernel(
    half, pix_ref, wh_ref, wf_ref, gain_ref, off_ref, mask_ref, bwd_ref, pix_s, pre_s, sem
):
    rows, cols = pix_ref.shape[1:3]
    width = pix_s.shape[1]
    first = half // LANES - 1
    for tile in range(cols // LANES - first):
        lanes = slice((first + tile) * LANES, (first + tile + 1) * LANES)
        extra = jnp.concatenate(
            [off_ref[0, 0, :, lanes], off_ref[0, 1, :, lanes], mask_ref[0, :, lanes], mask_ref[0, :, lanes]], 0
        )
        at = rows * width + tile * 4 * rows
        bwd_ref[at : at + 4 * rows, :] = extra.astype(F32).astype(BF16)

    def store(n, value):
        bwd_ref[n * width : (n + 1) * width, :] = value

    pieces = [(0, r, cols - width) for r in range(rows)]
    encode_rows(pieces, store, pix_ref, wh_ref, wf_ref, gain_ref, pix_s, pre_s, sem)


def border_rows(rows):
    return list(range(REACH)) + list(range(rows - REACH, rows))


def encode_border_kernel(
    half, pix_ref, wh_ref, wf_ref, gain_ref, fwd_ref, bwd_ref,
    border_ref, up_ref, down_ref, pix_s, pre_s, sem, csem,
):
    rows, cols = pix_ref.shape[1:3]
    width = fwd_ref.shape[1]
    copies = []

    def copy(src, dst):
        c = pltpu.make_async_copy(src, dst, csem.at[len(copies)])
        c.start()
        copies.append(c)

    for pack, row0 in ((up_ref, rows - REACH), (down_ref, 0)):
        for r in range(REACH):
            copy(
                bwd_ref.at[pl.ds((row0 + r + 1) * width - half, half), :],
                pack.at[r, half:cols, :],
            )
            copy(
                fwd_ref.at[row0 + r, half - 2 * EDGE : half, :],
                pack.at[r, cols : cols + 2 * EDGE, :],
            )

    def store(n, value):
        border_ref[n] = value
        lead = 0 if n < 2 * REACH else cols + 2 * EDGE
        pack = down_ref if n % (2 * REACH) < REACH else up_ref
        pack[n % REACH, lead : lead + half, :] = value

    pieces = [(0, r, 0) for r in border_rows(rows)] + [(1, r, half) for r in border_rows(rows)]
    encode_rows(pieces, store, pix_ref, wh_ref, wf_ref, gain_ref, pix_s, pre_s, sem)
    for c in copies:
        c.wait()


def encode_inner_kernel(half, pix_ref, wh_ref, wf_ref, gain_ref, inner_ref, pix_s, pre_s, sem):
    rows = pix_ref.shape[1]

    def store(n, value):
        inner_ref[n] = value

    inside = range(REACH, rows - REACH)
    pieces = [(0, r, 0) for r in inside] + [(1, r, half) for r in inside]
    encode_rows(pieces, store, pix_ref, wh_ref, wf_ref, gain_ref, pix_s, pre_s, sem)


def flops_of(nodes, patch, hid, feat):
    return pl.CostEstimate(
        flops=2 * nodes * hid * (patch + feat), bytes_accessed=nodes * 2 * (patch + feat), transcendentals=nodes
    )


def align(band, first, lift, row):
    band = pltpu.roll(band, (2 * LANES - first - BASE + 2 + lift) % LANES, 1)
    for shift in (1, 2, 4):
        band = jnp.where((row & shift) != 0, pltpu.roll(band, LANES - shift, 1), band)
    return band


def score_columns(q_s, ref_s, m_s, s_s, k, low):
    rows = q_s.shape[0]
    span = 2 * REACH + 1
    tall = LANES - low
    lane = lax.broadcasted_iota(jnp.int32, (8, LANES), 1)
    cols = pl.ds(pl.multiple_of(k * LANES + low, 16), tall)
    for rp in range(rows + 2 * REACH):
        j = rp % span
        start = pl.multiple_of(k * LANES + (PAD - BASE - SEG * j), 16)
        window = ref_s[rp, pl.ds(start, 2 * LANES), :]
        first = max(rp - 2 * REACH, 0)
        last = min(rp, rows - 1)
        query = q_s[first : last + 1, cols, :].reshape((last + 1 - first) * tall, q_s.shape[2])
        product = lax.dot_general(
            query, window, (((1,), (1,)), ((), ())), preferred_element_type=F32
        )
        for r in range(first, last + 1):
            for i in range(low // 8, LANES // 8):
                at = (r - first) * tall + 8 * i - low
                s = 8 * i + BASE - 4 + SEG * j
                near = product[at : at + 8, :LANES]
                far = product[at : at + 8, LANES:]
                if s + SEG <= LANES:
                    value, mask = near, (lane >= s) & (lane < s + SEG)
                elif s >= LANES:
                    value, mask = far, (lane >= s - LANES) & (lane < s + SEG - LANES)
                else:
                    value = jnp.where(lane >= s, near, far)
                    mask = (lane >= s) | (lane < s + SEG - LANES)
                dst = m_s.at[r, 8 * i : 8 * i + 8, :]
                if rp == r:
                    dst[...] = value
                else:
                    pltpu.store(dst, value, mask=mask)
        if rp > 2 * REACH and rp % 2:
            score_turn(m_s, s_s, rp - 2 * REACH - 1, k, low)


def score_turn(m_s, s_s, r, k, low):
    span = 2 * REACH + 1
    lane = lax.broadcasted_iota(jnp.int32, (8, LANES), 1)
    row = lax.broadcasted_iota(jnp.int32, (8, LANES), 0)
    groups = [jnp.zeros((8, LANES), F32)] * (low // 8)
    for i in range(low // 8, LANES // 8):
        one = align(m_s[r, 8 * i : 8 * i + 8, :], 8 * i, 0, row)
        two = align(m_s[r + 1, 8 * i : 8 * i + 8, :], 8 * i, 8, row)
        groups.append(jnp.where((lane & 8) != 0, two, one))
    turned = jnp.concatenate(groups, 0).T
    lanes = pl.ds(pl.multiple_of(k * LANES, LANES), LANES)
    for n in range(2):
        for j in range(span):
            a = (j - r - n) % span
            at = SEG * j + 8 * n
            s_s[r + n, SEG * a : SEG * a + 8, lanes] = turned[at : at + 8]


def score_job(q_s, ref_s, m_s, s_s, tiles, low=0):
    first = 1 if low else 0
    if low:
        score_columns(q_s, ref_s, m_s.at[0], s_s, 0, low)
    pairs, odd = (tiles - first) // 2, (tiles - first) % 2

    def body(n, carry):
        for m in range(2):
            score_columns(q_s, ref_s, m_s.at[m], s_s, 2 * n + m + first, 0)
        return carry

    lax.fori_loop(0, pairs, body, 0)
    if odd:
        score_columns(q_s, ref_s, m_s.at[0], s_s, tiles - 1, 0)


def flow_tile(s_s, oy, ox, lanes):
    y_low, y_high, x_low, x_high = oy < 0, oy > 0, ox < 0, ox > 0
    feat = F32(1.0 / LANES)
    by_row = {}
    for i in range(3):
        for b in range(5):
            v = [s_s[:, SEG * (i + d) + b, lanes] for d in range(3)]
            by_row[i, b] = jnp.where(y_low, v[0], jnp.where(y_high, v[2], v[1]))
    total = jnp.ones_like(oy)
    sum_y = jnp.zeros_like(oy)
    sum_x = jnp.zeros_like(oy)
    for i in range(3):
        for j in range(3):
            near = jnp.where(
                x_low, by_row[i, j], jnp.where(x_high, by_row[i, j + 2], by_row[i, j + 1])
            )
            near = near * feat
            weight = near * near
            total = total + weight
            if i != 1:
                sum_y = sum_y + weight * (i - 1)
            if j != 1:
                sum_x = sum_x + weight * (j - 1)
    return oy + sum_y / total, ox + sum_x / total


def flows_of(s_s, off_ref, flow_ref, tiles):
    def body(k, carry):
        lanes = pl.ds(pl.multiple_of(k * LANES, LANES), LANES)
        fy, fx = flow_tile(s_s, off_ref[0, :, lanes].astype(F32), off_ref[1, :, lanes].astype(F32), lanes)
        flow_ref[0, :, lanes] = fy
        flow_ref[1, :, lanes] = fx
        return carry

    lax.fori_loop(0, tiles, body, 0)


class Loads:
    def __init__(self, sem, first=0):
        self.sem, self.next, self.open = sem, first, []

    def __call__(self, src, dst):
        copy = pltpu.make_async_copy(src, dst, self.sem.at[self.next])
        copy.start()
        self.next += 1
        self.open.append(copy)

    def wait(self):
        for copy in self.open:
            copy.wait()
        self.open = []


def zero_sides(ref_s, cols):
    side = jnp.zeros((ref_s.shape[0], EDGE, ref_s.shape[2]), BF16)
    ref_s[:, PAD - EDGE : PAD, :] = side
    ref_s[:, PAD + cols : PAD + cols + EDGE, :] = side


def load_left(loads, border_ref, inner_ref, ref, row0, lanes, section):
    inner = inner_ref.shape[0] // 2
    at = section * 2 * REACH
    loads(border_ref.at[at : at + REACH], ref.at[row0 : row0 + REACH, lanes, :])
    loads(
        inner_ref.at[section * inner : (section + 1) * inner],
        ref.at[row0 + REACH : row0 + REACH + inner, lanes, :],
    )
    loads(
        border_ref.at[at + REACH : at + 2 * REACH],
        ref.at[row0 + REACH + inner : row0 + 2 * REACH + inner, lanes, :],
    )


def own_scores_kernel(
    half, fwd_ref, bwd_ref, border_ref, inner_ref, up_ref, down_ref,
    pred_ref, pup_ref, pdown_ref, off_ref, flow_ref, flow0_ref,
    q_s, ref_s, s_s, q0_s, ref0_s, m_s, sem,
):
    rows, cols = q_s.shape[:2]
    width = fwd_ref.shape[1]
    is_first = lax.axis_index("sec") == 0
    base0 = half - LANES
    loads = Loads(sem)
    loads(fwd_ref.at[:, 0:half, :], q_s.at[:, 0:half, :])
    load_left(loads, border_ref, inner_ref, q_s, 0, slice(half, cols), 1)
    load_left(loads, border_ref, inner_ref, ref_s, REACH, slice(PAD, PAD + half), 0)
    for r in range(rows):
        loads(
            bwd_ref.at[pl.ds((r + 1) * width - half, half), :],
            ref_s.at[r + REACH, PAD + half : PAD + cols, :],
        )
    loads(up_ref.at[:, 0:cols, :], ref_s.at[0:REACH, PAD : PAD + cols, :])
    loads(down_ref.at[:, 0:cols, :], ref_s.at[rows + REACH : rows + 2 * REACH, PAD : PAD + cols, :])
    zero_sides(ref_s, cols)
    at = loads.next
    loads.wait()
    flow0_ref[...] = jnp.zeros_like(flow0_ref)

    @pl.when(is_first)
    def _():
        loads0 = Loads(sem, at)
        for r in range(rows):
            loads0(
                bwd_ref.at[pl.ds(r * width, width), :],
                q0_s.at[r, LANES + half - width : LANES + half, :],
            )
        span = slice(base0, cols)
        to = slice(PAD, PAD + cols - base0)
        loads0(pred_ref.at[:, span, :], ref0_s.at[REACH : rows + REACH, to, :])
        loads0(pup_ref.at[:, span, :], ref0_s.at[0:REACH, to, :])
        loads0(pdown_ref.at[:, span, :], ref0_s.at[rows + REACH : rows + 2 * REACH, to, :])
        zero_sides(ref0_s, cols - base0)
        tiles = (cols - base0) // LANES
        loads0.wait()
        score_job(q0_s, ref0_s, m_s, s_s, tiles, LANES - EDGE)
        flows_of(s_s, off_ref.at[0, :, :, base0:cols], flow0_ref, tiles)

    score_job(q_s, ref_s, m_s, s_s, cols // LANES)
    flows_of(s_s, off_ref.at[1], flow_ref, cols // LANES)


def back_scores_kernel(
    half, q_ref, fwd_ref, border_ref, inner_ref, up_ref, down_ref, flow_ref,
    q_s, ref_s, s_s, off_s, m_s, sem,
):
    rows, span = q_s.shape[:2]
    width = fwd_ref.shape[1]
    cols = 2 * half
    lead = PAD + LANES
    gap = 2 * EDGE
    loads = Loads(sem)
    for r in range(rows):
        loads(q_ref.at[pl.ds(r * width, width), :], q_s.at[r, span - width : span, :])
    loads(fwd_ref.at[:, half - gap : half, :], ref_s.at[REACH : rows + REACH, lead - gap : lead, :])
    load_left(loads, border_ref, inner_ref, ref_s, REACH, slice(lead, lead + half), 1)
    pack = slice(cols, cols + gap + half)
    to = slice(lead - gap, lead + half)
    loads(up_ref.at[:, pack, :], ref_s.at[0:REACH, to, :])
    loads(down_ref.at[:, pack, :], ref_s.at[rows + REACH : rows + 2 * REACH, to, :])
    loads(q_ref.at[rows * width :, :], off_s)
    ref_s[:, lead + half : lead + half + EDGE, :] = jnp.zeros((rows + 2 * REACH, EDGE, LANES), BF16)
    loads.wait()
    tiles = span // LANES
    score_job(q_s, ref_s, m_s, s_s, tiles, LANES - EDGE)

    def body(k, carry):
        lanes = pl.ds(pl.multiple_of(k * LANES, LANES), LANES)
        extra = off_s[pl.ds(pl.multiple_of(k * 4 * rows, 4 * rows), 4 * rows), :].astype(F32)
        fy, fx = flow_tile(s_s, extra[:rows], extra[rows : 2 * rows], lanes)
        flow_ref[0, :, lanes] = fy
        flow_ref[1, :, lanes] = fx
        flow_ref[2, :, lanes] = extra[2 * rows : 3 * rows]
        return carry

    lax.fori_loop(0, tiles, body, 0)


def pairs_out(pack_ref, at, tops, bottoms):
    for n, (top, bottom) in enumerate(zip(tops, bottoms)):
        pack_ref[at + 16 * n : at + 16 * n + 16, :] = jnp.concatenate([top, bottom], 0).astype(BF16)
    return at + 16 * len(tops)


def front_scores_kernel(
    half, fwd_ref, up_ref, down_ref, pred_ref, pup_ref, pdown_ref, border_ref, inner_ref,
    off_ref, mask_ref, flow1_ref, flow0_ref, flow2_ref, flow_ref, pack_ref,
    q_s, ref_s, s_s, m_s, sem,
):
    rows = q_s.shape[0]
    cols = off_ref.shape[3]
    width = fwd_ref.shape[1]
    is_first = lax.axis_index("sec") == 0
    loads = Loads(sem)
    load_left(loads, border_ref, inner_ref, q_s, 0, slice(0, half), 0)
    at = loads.next
    span = slice(PAD, PAD + width)
    below = slice(rows + REACH, rows + 2 * REACH)

    @pl.when(is_first)
    def _():
        mine = Loads(sem, at)
        mine(pred_ref.at[:, 0:width, :], ref_s.at[REACH : rows + REACH, span, :])
        mine(pup_ref.at[:, 0:width, :], ref_s.at[0:REACH, span, :])
        mine(pdown_ref.at[:, 0:width, :], ref_s.at[below, span, :])
        mine.wait()

    @pl.when(jnp.logical_not(is_first))
    def _():
        mine = Loads(sem, at)
        mine(fwd_ref, ref_s.at[REACH : rows + REACH, span, :])
        mine(up_ref, ref_s.at[0:REACH, span, :])
        mine(down_ref, ref_s.at[below, span, :])
        mine.wait()

    loads.wait()
    ref_s[:, PAD - EDGE : PAD, :] = jnp.zeros((rows + 2 * REACH, EDGE, LANES), BF16)
    tiles = half // LANES
    score_job(q_s, ref_s, m_s, s_s, tiles)
    flow_ref[:, :, half:cols] = flow0_ref[:, :, LANES:]
    flows_of(s_s, off_ref.at[0], flow_ref, tiles)

    def tiles_of(ref, count):
        return [ref[:, n * LANES : (n + 1) * LANES] for n in range(count)]

    n = 0
    for ref, count in ((flow1_ref, cols // LANES), (flow_ref, cols // LANES), (flow2_ref, flow2_ref.shape[2] // LANES)):
        n = pairs_out(pack_ref, n, tiles_of(ref.at[0], count), tiles_of(ref.at[1], count))
    masks = []
    for ref, count in ((mask_ref.at[1], cols // LANES), (mask_ref.at[0], cols // LANES), (flow2_ref.at[2], flow2_ref.shape[2] // LANES)):
        masks += [m.astype(F32) for m in tiles_of(ref, count)]
    if len(masks) % 2:
        masks.append(masks[-1])
    pairs_out(pack_ref, n, masks[0::2], masks[1::2])


def relax_kernel(
    half, up_ref, down_ref, flow1_ref, flow3_ref, flow2_ref, mask_ref, f1_ref, f3_ref, msg_ref,
    field_s, pull_s, keep_s,
):
    rows, cols = flow1_ref.shape[1:]
    deep = rows + 2 * ITERS
    place = lax.axis_index("tile")
    count = lax.axis_size("tile")
    glob = place * rows + lax.broadcasted_iota(jnp.int32, (deep, LANES), 0) - ITERS
    inside = ((glob >= 0) & (glob < rows * count)).astype(F32)
    widths = (cols, cols, flow2_ref.shape[2])
    tiles = [w // LANES for w in widths]
    flows = (flow1_ref, flow3_ref, flow2_ref)
    own_masks = (mask_ref.at[1], mask_ref.at[0], flow2_ref.at[2])
    starts = [0, tiles[0], tiles[0] + tiles[1]]
    mask_at = 16 * sum(tiles)
    for job in range(3):
        for k in range(tiles[job]):
            lanes = slice(k * LANES, (k + 1) * LANES)
            at = 16 * (starts[job] + k)
            m_at = mask_at + 8 * (starts[job] + k)
            half_at = m_at // 16 * 16
            sub = slice(m_at - half_at, m_at - half_at + 8)
            upper = up_ref[at : at + 16, :].astype(F32)
            lower = down_ref[at : at + 16, :].astype(F32)
            m_up = up_ref[half_at : half_at + 16, :].astype(F32)[sub]
            m_down = down_ref[half_at : half_at + 16, :].astype(F32)[sub]
            weight = stiffness * jnp.concatenate(
                [m_up, own_masks[job][:, lanes].astype(F32), m_down], 0
            )
            keep_s[job, :, lanes] = (step_size - step_size * weight) * inside
            for c in range(2):
                flow = jnp.concatenate(
                    [upper[8 * c : 8 * c + 8], flows[job][c, :, lanes], lower[8 * c : 8 * c + 8]], 0
                )
                pull = step_size * weight * flow * inside
                pull_s[job, c, :, lanes] = pull
                field_s[job, c, :, lanes] = pull
    step = step_size * inside

    def body(n, carry):
        for job in range(3):
            for c in range(2):
                old = [field_s[job, c, :, k * LANES : (k + 1) * LANES] for k in range(tiles[job])]
                lane = lax.broadcasted_iota(jnp.int32, (deep, LANES), 1)
                nxt = [pltpu.roll(x, LANES - 1, 1) for x in old]
                prv = [pltpu.roll(x, 1, 1) for x in old]
                zero = jnp.zeros_like(old[0])
                for k in range(tiles[job]):
                    lanes = slice(k * LANES, (k + 1) * LANES)
                    right = jnp.where(lane == LANES - 1, nxt[k + 1] if k + 1 < tiles[job] else zero, nxt[k])
                    left = jnp.where(lane == 0, prv[k - 1] if k else zero, prv[k])
                    around = pltpu.roll(old[k], 1, 0) + pltpu.roll(old[k], deep - 1, 0) + left + right
                    field_s[job, c, :, lanes] = (
                        keep_s[job, :, lanes] * old[k] + step * around + pull_s[job, c, :, lanes]
                    )
        return carry

    lax.fori_loop(0, ITERS - 1, body, 0)
    is_first = lax.axis_index("sec") == 0
    seam = half - EDGE // 2
    mine = slice(ITERS, ITERS + rows)
    lead = half - LANES
    for c in range(2):
        for k in range(tiles[0]):
            lanes = slice(k * LANES, (k + 1) * LANES)
            col = lax.broadcasted_iota(jnp.int32, (rows, LANES), 1) + k * LANES
            one = field_s[0, c, mine, lanes]
            front = field_s[1, c, mine, lanes]
            if (k + 1) * LANES > seam:
                front = jnp.where((col < seam) | is_first, front, 0.0)
            total = one + front
            if k * LANES >= lead:
                back = field_s[2, c, mine, k * LANES - lead : (k + 1) * LANES - lead]
                total = total + jnp.where(col >= seam, back, 0.0)
            f1_ref[c, :, lanes] = one
            f3_ref[c, :, lanes] = front
            msg_ref[c, :, lanes] = total.astype(msg_ref.dtype)


def shards(pixels, pred, offsets, mask, base_shift, w_hidden, w_feature, feat_gain):
    secs, rows, cols, patch = pixels.shape
    hid, feat = w_feature.shape
    assert secs == 2 and rows == ITERS and feat == LANES and cols % (2 * LANES) == 0
    half = cols // 2
    width = half + EDGE
    inner = rows - 2 * REACH
    span = half + LANES
    deep = rows + 2 * REACH
    tail = 4 * rows * (span // LANES)
    gain = feat_gain.reshape(1, feat)
    shape = jax.ShapeDtypeStruct
    weights = (w_hidden, w_feature, gain)

    def encode(kernel, outs, extra, extra_specs, wide, more=()):
        return pl.pallas_call(
            functools.partial(kernel, half),
            out_shape=outs,
            in_specs=[HBM, VMEM, VMEM, VMEM] + extra_specs,
            out_specs=jax.tree.map(lambda _: VMEM, outs),
            scratch_shapes=[
                pltpu.VMEM((rows, wide, patch), BF16),
                pltpu.VMEM((2, 2 * wide, feat), F32),
                pltpu.SemaphoreType.DMA((rows,)),
                *more,
            ],
            compiler_params=params(),
            cost_estimate=flops_of(rows * wide, patch, hid, feat),
        )(pixels, *weights, *extra)

    pup = hop_plane(pred[rows - REACH :], 1)
    pdown = hop_plane(pred[:REACH], -1)
    fwd = encode(encode_front_kernel, shape((rows, width, feat), BF16), (), [], width)
    fwd_in = hop(fwd, "sec", 1)
    bwd = encode(
        encode_back_kernel, shape((rows * width + tail, feat), BF16),
        (offsets, mask), [VMEM, VMEM], width,
    )
    bwd_in = hop(bwd, "sec", -1)
    pack_cols = cols + 2 * EDGE + half
    border, up, down = encode(
        encode_border_kernel,
        (
            shape((4 * REACH, half, feat), BF16),
            shape((REACH, pack_cols, feat), BF16),
            shape((REACH, pack_cols, feat), BF16),
        ),
        (fwd, bwd), [HBM, HBM], half, (pltpu.SemaphoreType.DMA((4 * REACH,)),),
    )
    up_in = hop(up, "tile", 1)
    down_in = hop(down, "tile", -1)
    inside = encode(encode_inner_kernel, shape((2 * inner, half, feat), BF16), (), [], half)
    fup_in = hop(fwd_in[rows - REACH :], "tile", 1)
    fdown_in = hop(fwd_in[:REACH], "tile", -1)

    bands = SEG * (2 * REACH + 1)
    nodes = rows * cols

    def score_cost(part):
        return pl.CostEstimate(flops=int(part * nodes * 12 * 2 * 256 * 128), bytes_accessed=int(part * nodes * 512), transcendentals=0)

    flow1, flow0 = pl.pallas_call(
        functools.partial(own_scores_kernel, half),
        out_shape=(shape((2, rows, cols), F32), shape((2, rows, span), F32)),
        in_specs=[HBM] * 9 + [VMEM],
        out_specs=(VMEM, VMEM),
        scratch_shapes=[
            pltpu.VMEM((rows, cols, feat), BF16),
            pltpu.VMEM((deep, cols + 2 * PAD, feat), BF16),
            pltpu.VMEM((rows, bands, cols), F32),
            pltpu.VMEM((rows, span, feat), BF16),
            pltpu.VMEM((deep, span + 2 * PAD, feat), BF16),
            pltpu.VMEM((2, rows, LANES, LANES), F32),
            pltpu.SemaphoreType.DMA((32,)),
        ],
        compiler_params=params(),
        cost_estimate=score_cost(1.0),
        name="own_scores",
    )(fwd, bwd, border, inside, up_in, down_in, pred, pup, pdown, offsets)

    flow2 = pl.pallas_call(
        functools.partial(back_scores_kernel, half),
        out_shape=shape((3, rows, span), F32),
        in_specs=[HBM] * 6,
        out_specs=VMEM,
        scratch_shapes=[
            pltpu.VMEM((rows, span, feat), BF16),
            pltpu.VMEM((deep, span + 2 * PAD, feat), BF16),
            pltpu.VMEM((rows, bands, span), F32),
            pltpu.VMEM((tail, feat), BF16),
            pltpu.VMEM((2, rows, LANES, LANES), F32),
            pltpu.SemaphoreType.DMA((20,)),
        ],
        compiler_params=params(),
        cost_estimate=score_cost(0.55),
        name="back_scores",
    )(bwd_in, fwd, border, inside, up_in, down_in)

    tiles = 2 * (cols // LANES) + span // LANES
    pack_rows = 16 * tiles + 16 * ((tiles + 1) // 2)
    flow3, pack = pl.pallas_call(
        functools.partial(front_scores_kernel, half),
        out_shape=(shape((2, rows, cols), F32), shape((pack_rows, LANES), BF16)),
        in_specs=[HBM] * 8 + [VMEM] * 5,
        out_specs=(VMEM, VMEM),
        scratch_shapes=[
            pltpu.VMEM((rows, half, feat), BF16),
            pltpu.VMEM((deep, half + 3 * PAD, feat), BF16),
            pltpu.VMEM((rows, bands, half), F32),
            pltpu.VMEM((2, rows, LANES, LANES), F32),
            pltpu.SemaphoreType.DMA((12,)),
        ],
        compiler_params=params(),
        cost_estimate=score_cost(0.5),
        name="front_scores",
    )(fwd_in, fup_in, fdown_in, pred, pup, pdown, border, inside, offsets, mask, flow1, flow0, flow2)
    pack_up = hop(pack, "tile", 1)
    pack_down = hop(pack, "tile", -1)

    wide = rows + 2 * ITERS
    f1, f3, msg = pl.pallas_call(
        functools.partial(relax_kernel, half),
        out_shape=(shape((2, rows, cols), F32), shape((2, rows, cols), F32), shape((2, rows, cols), BF16)),
        in_specs=[VMEM] * 6,
        out_specs=(VMEM,) * 3,
        scratch_shapes=[
            pltpu.VMEM((3, 2, wide, cols), F32),
            pltpu.VMEM((3, 2, wide, cols), F32),
            pltpu.VMEM((3, wide, cols), F32),
        ],
        compiler_params=params(),
        cost_estimate=pl.CostEstimate(flops=nodes * 24 * 12 * 8, bytes_accessed=nodes * 40, transcendentals=0),
        name="relax",
    )(pack_up, pack_down, flow1, flow3, flow2, mask)

    prefix = base_shift
    for steps in range(1, lax.axis_size("sec")):
        prefix = prefix + hop(msg, "sec", steps).astype(F32)
    first = prefix + f3
    return jnp.stack([first, first + f1], axis=0)


def solution(mesh):
    in_specs = (
        P("sec", "tile", None, None),
        P("tile", None, None),
        P("sec", None, "tile", None),
        P("sec", "tile", None),
        P(None, "tile", None),
        P(),
        P(),
        P(),
    )
    out_specs = P("sec", None, "tile", None)
    return jax.shard_map(shards, mesh=mesh, in_specs=in_specs, out_specs=out_specs, check_vma=False)
```

```python
import functools

import jax
import jax.numpy as jnp
from jax import lax
from jax.experimental import pallas as pl
from jax.experimental.pallas import tpu as pltpu
from jax.sharding import PartitionSpec as P


ITERS = 8
REACH = 2
LANES = 128
BASE = 16
PAD = LANES
SEG = 16
EDGE = 16

epsilon = 1e-05
step_size = 0.2
stiffness = 0.5

F32 = jnp.float32
BF16 = jnp.bfloat16
HBM = pl.BlockSpec(memory_space=pltpu.HBM)
VMEM = pl.BlockSpec(memory_space=pltpu.VMEM)


def hop(value, axis, steps):
    count = lax.axis_size(axis)
    pairs = [(i, i + steps) for i in range(count) if 0 <= i + steps < count]
    return lax.ppermute(value, axis, pairs)


def hop_plane(value, steps):
    tiles = lax.axis_size("tile")
    secs = lax.axis_size("sec")
    pairs = [(i * secs, (i + steps) * secs) for i in range(tiles) if 0 <= i + steps < tiles]
    return lax.ppermute(value, ("tile", "sec"), pairs)


def params(limit):
    return pltpu.CompilerParams(vmem_limit_bytes=limit * 1024 * 1024)


def matmuls(pix, wh, wf):
    hidden = jnp.maximum(jnp.dot(pix, wh, preferred_element_type=F32), 0.0).astype(BF16)
    return jnp.dot(hidden, wf, preferred_element_type=F32)


def normed(pre, gain):
    mean = jnp.mean(pre * pre, axis=-1, keepdims=True)
    return (pre * lax.rsqrt(mean + epsilon) * gain).astype(BF16)


def encode_steps(pix_of, count, width, store, wh_ref, wf_ref, gain_ref, pre_s):
    steps = count // 2

    def finish(n):
        value = normed(pre_s[n % 2], gain_ref[...])
        store(2 * n, value[:width])
        store(2 * n + 1, value[width:])

    for n in range(steps):
        pre_s[n % 2] = matmuls(pix_of(2 * n), wh_ref[...], wf_ref[...])
        if n:
            finish(n - 1)
    finish(steps - 1)


def border_rows(rows):
    return list(range(REACH)) + list(range(rows - REACH, rows))


def inner_rows(rows):
    return list(range(REACH, rows - REACH))


def pieces_of(kind, rows, far):
    border, inner = border_rows(rows), inner_rows(rows)
    if kind == "front":
        return [(1, r, 0) for r in range(rows)]
    if kind == "border":
        return [(0, r, far) for r in border] + [(0, r, 0) for r in border] + [(1, r, far) for r in border]
    if kind == "back":
        return [(0, r, far) for r in inner]
    return [(0, r, 0) for r in inner] + [(1, r, far) for r in inner]


def fetch(pieces, pix_ref, dst_ref, sem):
    width = dst_ref.shape[1]
    copies = []
    for n, (sec, row, col0) in enumerate(pieces):
        copy = pltpu.make_async_copy(
            pix_ref.at[sec, row, col0 : col0 + width, :], dst_ref.at[n], sem.at[n]
        )
        copy.start()
        copies.append(copy)
    return copies


def pair_of(ref, n):
    width, patch = ref.shape[1:]
    return ref[n : n + 2].reshape(2 * width, patch)


def zero_sides(ref, cols):
    side = jnp.zeros((ref.shape[0], EDGE, ref.shape[2]), BF16)
    ref[:, PAD - EDGE : PAD, :] = side
    ref[:, PAD + cols : PAD + cols + EDGE, :] = side


def put_left(ref, row, value, half):
    ref[row + REACH, PAD : PAD + half, :] = value[:half]


def put_right(ref, row, value, half):
    ref[row + REACH, PAD + half : PAD + 2 * half, :] = value[value.shape[0] - half :]


def encode_front_kernel(
    half, pix_ref, wh_in, wf_in, gain_in, pred_ref,
    front_ref, odd_ref, next_ref, wh_ref, wf_ref, gain_ref, top_ref, bottom_ref,
    pix_s, pre_s, sem, next_sem, more_sem,
):
    rows, cols = pix_ref.shape[1:3]
    width = front_ref.shape[1]
    far = cols - width
    constants = [(wh_in, wh_ref), (wf_in, wf_ref), (gain_in, gain_ref)]
    start_all(constants, more_sem)
    copies = fetch(pieces_of("front", rows, far), pix_ref, pix_s, sem)
    edges = [(pred_ref.at[0:REACH], top_ref), (pred_ref.at[rows - REACH : rows], bottom_ref)]
    start_all(edges, more_sem.at[len(constants) :])
    following = fetch(pieces_of("border", rows, far), pix_ref, next_ref, next_sem)
    zero_sides(odd_ref, cols)
    wait_all(constants, more_sem)

    def pix_of(n):
        copies[n].wait()
        copies[n + 1].wait()
        return pair_of(pix_s, n)

    def store(n, value):
        front_ref[n] = value
        put_left(odd_ref, n, value, half)

    encode_steps(pix_of, len(copies), width, store, wh_ref, wf_ref, gain_ref, pre_s)
    wait_all(edges, more_sem.at[len(constants) :])
    for copy in following:
        copy.wait()


def encode_border_kernel(
    half, pix_ref, wh_ref, wf_ref, gain_ref, own_ref, odd_in, off_ref, mask_ref,
    odd_ref, even_ref, back_ref, up_ref, down_ref, next_ref, pre_s, next_sem,
):
    rows, cols = pix_ref.shape[1:3]
    width = own_ref.shape[1]
    border = border_rows(rows)
    following = fetch(pieces_of("back", rows, cols - width), pix_ref, next_ref, next_sem)
    zero_sides(even_ref, cols)
    first = half // LANES - 1
    for tile in range(cols // LANES - first):
        lanes = slice((first + tile) * LANES, (first + tile + 1) * LANES)
        extra = jnp.concatenate(
            [off_ref[0, 0, :, lanes], off_ref[0, 1, :, lanes], mask_ref[0, :, lanes], mask_ref[0, :, lanes]], 0
        )
        at = rows * width + tile * 4 * rows
        back_ref[at : at + 4 * rows, :] = extra.astype(F32).astype(BF16)

    def store(n, value):
        part, m = divmod(n, len(border))
        row = border[m]
        pack = down_ref if m < REACH else up_ref
        if part == 0:
            back_ref[row * width : (row + 1) * width, :] = value
            put_right(even_ref, row, value, half)
            pack[m % REACH, half:cols, :] = value[width - half :]
        elif part == 1:
            put_left(even_ref, row, value, half)
            pack[m % REACH, 0:half, :] = value[:half]
        else:
            put_right(odd_ref, row, value, half)
            pack[m % REACH, cols : cols + width, :] = value

    encode_steps(lambda n: pair_of(own_ref, n), own_ref.shape[0], width, store, wh_ref, wf_ref, gain_ref, pre_s)
    for copy in following:
        copy.wait()


def encode_back_kernel(
    half, pix_ref, wh_ref, wf_ref, gain_ref, own_ref, even_in, back_in,
    even_ref, back_ref, next_ref, pre_s, next_sem,
):
    rows, cols = pix_ref.shape[1:3]
    width = own_ref.shape[1]
    inner = inner_rows(rows)
    following = fetch(pieces_of("inner", rows, cols - width), pix_ref, next_ref, next_sem)

    def store(n, value):
        back_ref[inner[n] * width : (inner[n] + 1) * width, :] = value
        put_right(even_ref, inner[n], value, half)

    encode_steps(lambda n: pair_of(own_ref, n), own_ref.shape[0], width, store, wh_ref, wf_ref, gain_ref, pre_s)
    for copy in following:
        copy.wait()


def encode_inner_kernel(
    half, wh_ref, wf_ref, gain_ref, own_ref, odd_in, even_in, odd_ref, even_ref, pre_s
):
    width = own_ref.shape[1]
    rows = odd_ref.shape[0] - 2 * REACH
    inner = inner_rows(rows)

    def store(n, value):
        part, m = divmod(n, len(inner))
        if part == 0:
            put_left(even_ref, inner[m], value, half)
        else:
            put_right(odd_ref, inner[m], value, half)

    encode_steps(lambda n: pair_of(own_ref, n), own_ref.shape[0], width, store, wh_ref, wf_ref, gain_ref, pre_s)


def flops_of(nodes, patch, hid, feat):
    return pl.CostEstimate(
        flops=2 * nodes * hid * (patch + feat), bytes_accessed=nodes * 2 * (patch + feat), transcendentals=nodes
    )


def align(band, first, lift, row):
    band = pltpu.roll(band, (2 * LANES - first - BASE + 2 + lift) % LANES, 1)
    for shift in (1, 2, 4):
        band = jnp.where((row & shift) != 0, pltpu.roll(band, LANES - shift, 1), band)
    return band


def score_columns(query_of, window_of, rows, m_s, s_s, k, low):
    span = 2 * REACH + 1
    tall = LANES - low
    lane = lax.broadcasted_iota(jnp.int32, (8, LANES), 1)
    for rp in range(rows[0], rows[1] + 2 * REACH):
        j = rp % span
        window = window_of(rp, k, SEG * j)
        first = max(rp - 2 * REACH, rows[0])
        last = min(rp, rows[1] - 1)
        parts = [query_of(r, k, low) for r in range(first, last + 1)]
        query = jnp.concatenate(parts, 0) if len(parts) > 1 else parts[0]
        product = lax.dot_general(
            query, window, (((1,), (1,)), ((), ())), preferred_element_type=F32
        )
        for r in range(first, last + 1):
            for i in range(low // 8, LANES // 8):
                at = (r - first) * tall + 8 * i - low
                s = 8 * i + BASE - 4 + SEG * j
                near = product[at : at + 8, :LANES]
                far = product[at : at + 8, LANES:]
                if s + SEG <= LANES:
                    value, mask = near, (lane >= s) & (lane < s + SEG)
                elif s >= LANES:
                    value, mask = far, (lane >= s - LANES) & (lane < s + SEG - LANES)
                else:
                    value = jnp.where(lane >= s, near, far)
                    mask = (lane >= s) | (lane < s + SEG - LANES)
                dst = m_s.at[r, 8 * i : 8 * i + 8, :]
                if rp == r:
                    dst[...] = value
                else:
                    pltpu.store(dst, value, mask=mask)
        if rp > rows[0] + 2 * REACH and rp % 2:
            score_turn(m_s, s_s, rp - 2 * REACH - 1, k, low)


def score_turn(m_s, s_s, r, k, low):
    span = 2 * REACH + 1
    lane = lax.broadcasted_iota(jnp.int32, (8, LANES), 1)
    row = lax.broadcasted_iota(jnp.int32, (8, LANES), 0)
    groups = [jnp.zeros((8, LANES), F32)] * (low // 8)
    for i in range(low // 8, LANES // 8):
        one = align(m_s[r, 8 * i : 8 * i + 8, :], 8 * i, 0, row)
        two = align(m_s[r + 1, 8 * i : 8 * i + 8, :], 8 * i, 8, row)
        groups.append(jnp.where((lane & 8) != 0, two, one))
    turned = jnp.concatenate(groups, 0).T
    lanes = pl.ds(pl.multiple_of(k * LANES, LANES), LANES)
    for n in range(2):
        for j in range(span):
            a = (j - r - n) % span
            at = SEG * j + 8 * n
            s_s[r + n, SEG * a : SEG * a + 8, lanes] = turned[at : at + 8]


def score_job(query_of, window_of, m_s, s_s, tiles, low=0, blocks=None):
    blocks = blocks or ((0, s_s.shape[0]),)
    first = 1 if low else 0

    def columns(m, k, low):
        for rows in blocks:
            score_columns(query_of, window_of, rows, m_s.at[m], s_s, k, low)

    if low:
        columns(0, 0, low)
    pairs, odd = (tiles - first) // 2, (tiles - first) % 2

    def body(n, carry):
        for m in range(2):
            columns(m, 2 * n + m + first, 0)
        return carry

    lax.fori_loop(0, pairs, body, 0)
    if odd:
        columns(0, tiles - 1, 0)


def padded_query(ref, tile0=0):
    def query_of(r, k, low):
        at = pl.multiple_of((k + tile0) * LANES + PAD + low, 16)
        return ref[r + REACH, pl.ds(at, LANES - low), :]

    return query_of


def padded_window(ref, halo=None, tile0=0):
    rows = ref.shape[0] - 2 * REACH

    def window_of(rp, k, shift):
        at = pl.multiple_of((k + tile0) * LANES + (PAD - BASE) - shift, 16)
        if halo is not None and rp < REACH:
            return halo[rp, pl.ds(at, 2 * LANES), :]
        if halo is not None and rp >= rows + REACH:
            return halo[rp - rows, pl.ds(at, 2 * LANES), :]
        return ref[rp, pl.ds(at, 2 * LANES), :]

    return window_of


def flow_tile(s_s, oy, ox, lanes):
    y_low, y_high, x_low, x_high = oy < 0, oy > 0, ox < 0, ox > 0
    feat = F32(1.0 / LANES)
    by_row = {}
    for i in range(3):
        for b in range(5):
            v = [s_s[:, SEG * (i + d) + b, lanes] for d in range(3)]
            by_row[i, b] = jnp.where(y_low, v[0], jnp.where(y_high, v[2], v[1]))
    total = jnp.ones_like(oy)
    sum_y = jnp.zeros_like(oy)
    sum_x = jnp.zeros_like(oy)
    for i in range(3):
        for j in range(3):
            near = jnp.where(
                x_low, by_row[i, j], jnp.where(x_high, by_row[i, j + 2], by_row[i, j + 1])
            )
            near = near * feat
            weight = near * near
            total = total + weight
            if i != 1:
                sum_y = sum_y + weight * (i - 1)
            if j != 1:
                sum_x = sum_x + weight * (j - 1)
    return oy + sum_y / total, ox + sum_x / total


def flows_of(s_s, off_ref, flow_ref, tiles):
    def body(k, carry):
        lanes = pl.ds(pl.multiple_of(k * LANES, LANES), LANES)
        fy, fx = flow_tile(s_s, off_ref[0, :, lanes].astype(F32), off_ref[1, :, lanes].astype(F32), lanes)
        flow_ref[0, :, lanes] = fy
        flow_ref[1, :, lanes] = fx
        return carry

    lax.fori_loop(0, tiles, body, 0)


def copies_of(pairs, sem):
    return [pltpu.make_async_copy(src, dst, sem.at[n]) for n, (src, dst) in enumerate(pairs)]


def start_all(pairs, sem):
    for copy in copies_of(pairs, sem):
        copy.start()


def wait_all(pairs, sem):
    for copy in copies_of(pairs, sem):
        copy.wait()


def near_scores_kernel(
    half, even_ref, odd_ref, pred_ref, pup_ref, pdown_ref, off_ref,
    s_s, flow0_ref, ref0_s, s0_s, m_s, sem,
):
    rows = odd_ref.shape[0] - 2 * REACH
    cols = 2 * half
    far = half - 2 * EDGE
    is_first = lax.axis_index("sec") == 0
    tile0 = half // LANES - 1
    tiles = cols // LANES - tile0
    to = slice(PAD + far, PAD + cols)
    before = [
        (pred_ref.at[:, far:cols, :], ref0_s.at[REACH : rows + REACH, to, :]),
        (pup_ref.at[:, far:cols, :], ref0_s.at[0:REACH, to, :]),
        (pdown_ref.at[:, far:cols, :], ref0_s.at[rows + REACH : rows + 2 * REACH, to, :]),
    ]

    @pl.when(is_first)
    def _():
        start_all(before, sem)

    flow0_ref[...] = jnp.zeros_like(flow0_ref)
    score_job(
        padded_query(odd_ref), padded_window(even_ref), m_s, s_s, cols // LANES, 0, ((REACH, rows - REACH),)
    )

    @pl.when(is_first)
    def _():
        zero_sides(ref0_s, cols)
        wait_all(before, sem)
        score_job(
            padded_query(even_ref, tile0), padded_window(ref0_s, None, tile0), m_s, s0_s, tiles, LANES - EDGE
        )
        flows_of(s0_s, off_ref.at[0, :, :, tile0 * LANES : cols], flow0_ref, tiles)


def own_scores_kernel(
    half, even_ref, odd_ref, up_ref, down_ref, off_ref, s_in, s_s, flow_ref, halo_s, m_s, sem
):
    rows = odd_ref.shape[0] - 2 * REACH
    cols = 2 * half
    halos = [
        (up_ref.at[:, 0:cols, :], halo_s.at[0:REACH, PAD : PAD + cols, :]),
        (down_ref.at[:, 0:cols, :], halo_s.at[REACH : 2 * REACH, PAD : PAD + cols, :]),
    ]
    start_all(halos, sem)
    zero_sides(halo_s, cols)
    wait_all(halos, sem)
    score_job(
        padded_query(odd_ref), padded_window(even_ref, halo_s), m_s, s_s, cols // LANES, 0,
        ((0, REACH), (rows - REACH, rows)),
    )
    flows_of(s_s, off_ref.at[1], flow_ref, cols // LANES)


def pairs_out(pack_ref, at, tops, bottoms):
    for n, (top, bottom) in enumerate(zip(tops, bottoms)):
        pack_ref[at + 16 * n : at + 16 * n + 16, :] = jnp.concatenate([top, bottom], 0).astype(BF16)
    return at + 16 * len(tops)


def cross_scores_kernel(
    half, back_ref, odd_ref, up_ref, down_ref, front_ref, fup_ref, fdown_ref,
    pred_ref, pup_ref, pdown_ref, even_ref, off_ref, mask_ref, flow1_ref, flow0_ref,
    flow2_ref, flow_ref, pack_ref, halo_s, ref_s, s_s, m_s, sem, sem0,
):
    rows = odd_ref.shape[0] - 2 * REACH
    cols = 2 * half
    width = front_ref.shape[1]
    far = cols - width
    is_first = lax.axis_index("sec") == 0
    tile0 = half // LANES - 1
    tiles = cols // LANES - tile0
    pack = slice(cols, cols + width)
    to = slice(PAD + far, PAD + cols)
    span = slice(PAD, PAD + width)
    above, below = slice(0, REACH), slice(rows + REACH, rows + 2 * REACH)
    halos = [
        (up_ref.at[:, pack, :], halo_s.at[0:REACH, to, :]),
        (down_ref.at[:, pack, :], halo_s.at[REACH : 2 * REACH, to, :]),
    ]
    before = [
        (pred_ref.at[:, 0:width, :], ref_s.at[REACH : rows + REACH, span, :]),
        (pup_ref.at[:, 0:width, :], ref_s.at[above, span, :]),
        (pdown_ref.at[:, 0:width, :], ref_s.at[below, span, :]),
    ]
    passed = [
        (front_ref, ref_s.at[REACH : rows + REACH, span, :]),
        (fup_ref, ref_s.at[above, span, :]),
        (fdown_ref, ref_s.at[below, span, :]),
    ]
    start_all(halos, sem)

    @pl.when(is_first)
    def _():
        start_all(before, sem0)

    @pl.when(jnp.logical_not(is_first))
    def _():
        start_all(passed, sem0)

    zero_sides(halo_s, cols)
    wait_all(halos, sem)

    def query_of(r, k, low):
        at = (k + tile0) * LANES + low - far
        size = LANES - low
        return back_ref[pl.ds(pl.multiple_of(at + r * width, 16), size), :]

    score_job(query_of, padded_window(odd_ref, halo_s, tile0), m_s, s_s, tiles, LANES - EDGE)

    def body(k, carry):
        lanes = pl.ds(pl.multiple_of(k * LANES, LANES), LANES)
        extra = back_ref[pl.ds(pl.multiple_of(k * 4 * rows + rows * width, 4 * rows), 4 * rows), :].astype(F32)
        fy, fx = flow_tile(s_s, extra[:rows], extra[rows : 2 * rows], lanes)
        flow2_ref[0, :, lanes] = fy
        flow2_ref[1, :, lanes] = fx
        flow2_ref[2, :, lanes] = extra[2 * rows : 3 * rows]
        return carry

    lax.fori_loop(0, tiles, body, 0)

    @pl.when(is_first)
    def _():
        wait_all(before, sem0)

    @pl.when(jnp.logical_not(is_first))
    def _():
        wait_all(passed, sem0)

    ref_s[:, PAD - EDGE : PAD, :] = jnp.zeros((rows + 2 * REACH, EDGE, LANES), BF16)
    tiles = half // LANES
    score_job(padded_query(even_ref), padded_window(ref_s), m_s, s_s, tiles)
    flow_ref[:, :, half:cols] = flow0_ref[:, :, LANES:]
    flows_of(s_s, off_ref.at[0], flow_ref, tiles)

    def tiles_of(ref, count):
        return [ref[:, n * LANES : (n + 1) * LANES] for n in range(count)]

    n = 0
    for ref, count in ((flow1_ref, cols // LANES), (flow_ref, cols // LANES), (flow2_ref, flow2_ref.shape[2] // LANES)):
        n = pairs_out(pack_ref, n, tiles_of(ref.at[0], count), tiles_of(ref.at[1], count))
    masks = []
    for ref, count in ((mask_ref.at[1], cols // LANES), (mask_ref.at[0], cols // LANES), (flow2_ref.at[2], flow2_ref.shape[2] // LANES)):
        masks += [m.astype(F32) for m in tiles_of(ref, count)]
    if len(masks) % 2:
        masks.append(masks[-1])
    pairs_out(pack_ref, n, masks[0::2], masks[1::2])


def relax_kernel(
    half, up_ref, down_ref, flow1_ref, flow3_ref, flow2_ref, mask_ref, f1_ref, f3_ref, msg_ref,
    field_s, pull_s, keep_s,
):
    rows, cols = flow1_ref.shape[1:]
    deep = rows + 2 * ITERS
    place = lax.axis_index("tile")
    count = lax.axis_size("tile")
    glob = place * rows + lax.broadcasted_iota(jnp.int32, (deep, LANES), 0) - ITERS
    inside = ((glob >= 0) & (glob < rows * count)).astype(F32)
    widths = (cols, cols, flow2_ref.shape[2])
    tiles = [w // LANES for w in widths]
    flows = (flow1_ref, flow3_ref, flow2_ref)
    own_masks = (mask_ref.at[1], mask_ref.at[0], flow2_ref.at[2])
    starts = [0, tiles[0], tiles[0] + tiles[1]]
    mask_at = 16 * sum(tiles)
    for job in range(3):
        for k in range(tiles[job]):
            lanes = slice(k * LANES, (k + 1) * LANES)
            at = 16 * (starts[job] + k)
            m_at = mask_at + 8 * (starts[job] + k)
            half_at = m_at // 16 * 16
            sub = slice(m_at - half_at, m_at - half_at + 8)
            upper = up_ref[at : at + 16, :].astype(F32)
            lower = down_ref[at : at + 16, :].astype(F32)
            m_up = up_ref[half_at : half_at + 16, :].astype(F32)[sub]
            m_down = down_ref[half_at : half_at + 16, :].astype(F32)[sub]
            weight = stiffness * jnp.concatenate(
                [m_up, own_masks[job][:, lanes].astype(F32), m_down], 0
            )
            keep_s[job, :, lanes] = (step_size - step_size * weight) * inside
            for c in range(2):
                flow = jnp.concatenate(
                    [upper[8 * c : 8 * c + 8], flows[job][c, :, lanes], lower[8 * c : 8 * c + 8]], 0
                )
                pull = step_size * weight * flow * inside
                pull_s[job, c, :, lanes] = pull
                field_s[job, c, :, lanes] = pull
    step = step_size * inside

    def body(n, carry):
        for job in range(3):
            for c in range(2):
                old = [field_s[job, c, :, k * LANES : (k + 1) * LANES] for k in range(tiles[job])]
                lane = lax.broadcasted_iota(jnp.int32, (deep, LANES), 1)
                nxt = [pltpu.roll(x, LANES - 1, 1) for x in old]
                prv = [pltpu.roll(x, 1, 1) for x in old]
                zero = jnp.zeros_like(old[0])
                for k in range(tiles[job]):
                    lanes = slice(k * LANES, (k + 1) * LANES)
                    right = jnp.where(lane == LANES - 1, nxt[k + 1] if k + 1 < tiles[job] else zero, nxt[k])
                    left = jnp.where(lane == 0, prv[k - 1] if k else zero, prv[k])
                    around = pltpu.roll(old[k], 1, 0) + pltpu.roll(old[k], deep - 1, 0) + left + right
                    field_s[job, c, :, lanes] = (
                        keep_s[job, :, lanes] * old[k] + step * around + pull_s[job, c, :, lanes]
                    )
        return carry

    lax.fori_loop(0, ITERS - 1, body, 0)
    is_first = lax.axis_index("sec") == 0
    seam = half - EDGE // 2
    mine = slice(ITERS, ITERS + rows)
    lead = half - LANES
    for c in range(2):
        for k in range(tiles[0]):
            lanes = slice(k * LANES, (k + 1) * LANES)
            col = lax.broadcasted_iota(jnp.int32, (rows, LANES), 1) + k * LANES
            one = field_s[0, c, mine, lanes]
            front = field_s[1, c, mine, lanes]
            if (k + 1) * LANES > seam:
                front = jnp.where((col < seam) | is_first, front, 0.0)
            total = one + front
            if k * LANES >= lead:
                back = field_s[2, c, mine, k * LANES - lead : (k + 1) * LANES - lead]
                total = total + jnp.where(col >= seam, back, 0.0)
            f1_ref[c, :, lanes] = one
            f3_ref[c, :, lanes] = front
            msg_ref[c, :, lanes] = total.astype(msg_ref.dtype)


def shards(pixels, pred, offsets, mask, base_shift, w_hidden, w_feature, feat_gain):
    secs, rows, cols, patch = pixels.shape
    hid, feat = w_feature.shape
    assert secs == 2 and rows == ITERS and feat == LANES and cols % (2 * LANES) == 0
    half = cols // 2
    width = half + 2 * EDGE
    inner = rows - 2 * REACH
    span = half + LANES
    deep = rows + 2 * REACH
    tail = 4 * rows * (span // LANES)
    full = cols + 2 * PAD
    gain = feat_gain.reshape(1, feat)
    shape = jax.ShapeDtypeStruct
    padded = shape((deep, full, feat), BF16)
    pre = pltpu.VMEM((2, 2 * width, feat), F32)

    dma = pltpu.SemaphoreType.DMA

    def call(kernel, ins, in_specs, outs, scratch, cost, limit, aliases=None):
        return pl.pallas_call(
            functools.partial(kernel, half),
            out_shape=outs,
            in_specs=in_specs,
            out_specs=tuple(VMEM for _ in outs),
            scratch_shapes=scratch,
            input_output_aliases=aliases or {},
            compiler_params=params(limit),
            cost_estimate=cost,
        )(*ins)

    def pixels_for(kind):
        return shape((len(pieces_of(kind, rows, 0)), width, patch), BF16)

    def encode_cost(kind):
        return flops_of(len(pieces_of(kind, rows, 0)) * width, patch, hid, feat)

    pixels, w_hidden, w_feature, gain, pred = (
        pltpu.with_memory_space_constraint(x, pltpu.HBM) for x in (pixels, w_hidden, w_feature, gain, pred)
    )
    edges = shape((REACH, cols, feat), BF16)
    front, odd, pix, wh, wf, gain, top, bottom = call(
        encode_front_kernel,
        (pixels, w_hidden, w_feature, gain, pred), [HBM] * 5,
        (
            shape((rows, width, feat), BF16), padded, pixels_for("border"),
            shape(w_hidden.shape, BF16), shape(w_feature.shape, BF16), shape(gain.shape, F32), edges, edges,
        ),
        [pltpu.VMEM((rows, width, patch), BF16), pre, dma((rows,)), dma((6 * REACH,)), dma((5,))],
        encode_cost("front"), 12,
    )
    weights = (wh, wf, gain)
    front_in = hop(front, "sec", 1)
    pup = hop_plane(bottom, 1)
    pdown = hop_plane(top, -1)
    pack = shape((REACH, cols + width, feat), BF16)
    odd, even, back, up, down, pix = call(
        encode_border_kernel,
        (pixels, *weights, pix, odd, offsets, mask), [HBM] + [VMEM] * 7,
        (padded, padded, shape((rows * width + tail, feat), BF16), pack, pack, pixels_for("back")),
        [pre, dma((inner,))], encode_cost("border"), 12, {5: 0},
    )
    up_in = hop(up, "tile", 1)
    down_in = hop(down, "tile", -1)
    even, back, pix = call(
        encode_back_kernel,
        (pixels, *weights, pix, even, back), [HBM] + [VMEM] * 6,
        (padded, shape(back.shape, BF16), pixels_for("inner")),
        [pre, dma((2 * inner,))], encode_cost("back"), 12, {5: 0, 6: 1},
    )
    back_in = hop(back, "sec", -1)
    odd, even = call(
        encode_inner_kernel, (*weights, pix, odd, even), [VMEM] * 6,
        (padded, padded), [pre], encode_cost("inner"), 12, {4: 0, 5: 1},
    )

    bands = SEG * (2 * REACH + 1)
    nodes = rows * cols

    def score_cost(part):
        return pl.CostEstimate(
            flops=int(part * nodes * 2560 * LANES), bytes_accessed=int(part * nodes * 512), transcendentals=0
        )

    halo = pltpu.VMEM((2 * REACH, full, feat), BF16)
    grids = pltpu.VMEM((rows, bands, cols), F32)
    turning = pltpu.VMEM((2, rows, LANES, LANES), F32)
    whole = pltpu.VMEM((deep, full, feat), BF16)
    flow0_shape = shape((2, rows, span), F32)
    scores, flow0 = call(
        near_scores_kernel, (even, odd, pred, pup, pdown, offsets),
        [VMEM] * 2 + [HBM] + [VMEM] * 3, (shape((rows, bands, cols), F32), flow0_shape),
        [whole, pltpu.VMEM((rows, bands, span), F32), turning, dma((3,))], score_cost(0.5), 16,
    )
    fup_in = hop(front_in[rows - REACH :], "tile", 1)
    fdown_in = hop(front_in[:REACH], "tile", -1)
    _, flow1 = call(
        own_scores_kernel, (even, odd, up_in, down_in, offsets, scores), [VMEM] * 6,
        (shape(scores.shape, F32), shape((2, rows, cols), F32)),
        [halo, turning, dma((2,))], score_cost(0.5), 12, {5: 0},
    )

    tiles = 2 * (cols // LANES) + span // LANES
    pack_rows = 16 * tiles + 16 * ((tiles + 1) // 2)
    flow2, flow3, pack = call(
        cross_scores_kernel,
        (
            back_in, odd, up_in, down_in, front_in, fup_in, fdown_in,
            pred, pup, pdown, even, offsets, mask, flow1, flow0,
        ),
        [VMEM] * 7 + [HBM] + [VMEM] * 7,
        (shape((3, rows, span), F32), shape((2, rows, cols), F32), shape((pack_rows, LANES), BF16)),
        [halo, whole, grids, turning, dma((2,)), dma((3,))], score_cost(1.0), 20,
    )
    pack_up = hop(pack, "tile", 1)
    pack_down = hop(pack, "tile", -1)

    wide = rows + 2 * ITERS
    f1, f3, msg = pl.pallas_call(
        functools.partial(relax_kernel, half),
        out_shape=(shape((2, rows, cols), F32), shape((2, rows, cols), F32), shape((2, rows, cols), BF16)),
        in_specs=[VMEM] * 6,
        out_specs=(VMEM,) * 3,
        scratch_shapes=[
            pltpu.VMEM((3, 2, wide, cols), F32),
            pltpu.VMEM((3, 2, wide, cols), F32),
            pltpu.VMEM((3, wide, cols), F32),
        ],
        compiler_params=params(12),
        cost_estimate=pl.CostEstimate(flops=nodes * 24 * 12 * 8, bytes_accessed=nodes * 40, transcendentals=0),
        name="relax",
    )(pack_up, pack_down, flow1, flow3, flow2, mask)

    prefix = base_shift
    for steps in range(1, lax.axis_size("sec")):
        prefix = prefix + hop(msg, "sec", steps).astype(F32)
    first = prefix + f3
    return jnp.stack([first, first + f1], axis=0)


def solution(mesh):
    in_specs = (
        P("sec", "tile", None, None),
        P("tile", None, None),
        P("sec", None, "tile", None),
        P("sec", "tile", None),
        P(None, "tile", None),
        P(),
        P(),
        P(),
    )
    out_specs = P("sec", None, "tile", None)
    return jax.shard_map(shards, mesh=mesh, in_specs=in_specs, out_specs=out_specs, check_vma=False)
```

```python
import functools

import jax
import jax.numpy as jnp
from jax import lax
from jax.experimental import pallas as pl
from jax.experimental.pallas import tpu as pltpu
from jax.sharding import PartitionSpec as P


ITERS = 8
REACH = 2
LANES = 128
BASE = 16
PAD = LANES
SEG = 16
EDGE = 16

epsilon = 1e-05
step_size = 0.2
stiffness = 0.5

F32 = jnp.float32
BF16 = jnp.bfloat16
HBM = pl.BlockSpec(memory_space=pltpu.HBM)
VMEM = pl.BlockSpec(memory_space=pltpu.VMEM)


def hop(value, axis, steps):
    count = lax.axis_size(axis)
    pairs = [(i, i + steps) for i in range(count) if 0 <= i + steps < count]
    return lax.ppermute(value, axis, pairs)


def hop_plane(value, steps):
    tiles = lax.axis_size("tile")
    secs = lax.axis_size("sec")
    pairs = [(i * secs, (i + steps) * secs) for i in range(tiles) if 0 <= i + steps < tiles]
    return lax.ppermute(value, ("tile", "sec"), pairs)


def params(limit):
    return pltpu.CompilerParams(vmem_limit_bytes=limit * 1024 * 1024)


def matmuls(pix, wh, wf):
    hidden = jnp.maximum(jnp.dot(pix, wh, preferred_element_type=F32), 0.0).astype(BF16)
    return jnp.dot(hidden, wf, preferred_element_type=F32)


def normed(pre, gain):
    mean = jnp.mean(pre * pre, axis=-1, keepdims=True)
    return (pre * lax.rsqrt(mean + epsilon) * gain).astype(BF16)


def encode_steps(pix_of, count, width, store, wh_ref, wf_ref, gain_ref, pre_s):
    steps = count // 2

    def finish(n):
        value = normed(pre_s[n % 2], gain_ref[...])
        store(2 * n, value[:width])
        store(2 * n + 1, value[width:])

    for n in range(steps):
        pre_s[n % 2] = matmuls(pix_of(2 * n), wh_ref[...], wf_ref[...])
        if n:
            finish(n - 1)
    finish(steps - 1)


def border_rows(rows):
    return list(range(REACH)) + list(range(rows - REACH, rows))


def inner_rows(rows):
    return list(range(REACH, rows - REACH))


def pieces_of(kind, rows, far):
    border, inner = border_rows(rows), inner_rows(rows)
    if kind == "front":
        return [(1, r, 0) for r in range(rows)]
    if kind == "border":
        return [(0, r, far) for r in border] + [(0, r, 0) for r in border] + [(1, r, far) for r in border]
    if kind == "back":
        return [(0, r, far) for r in inner]
    return [(0, r, 0) for r in inner] + [(1, r, far) for r in inner]


def pixel_pair(pix_ref, pieces, n, width):
    rows = [pix_ref[sec, row, col0 : col0 + width, :] for sec, row, col0 in pieces[n : n + 2]]
    return jnp.concatenate(rows, 0)


def zero_sides(ref, cols):
    side = jnp.zeros((ref.shape[0], EDGE, ref.shape[2]), BF16)
    ref[:, PAD - EDGE : PAD, :] = side
    ref[:, PAD + cols : PAD + cols + EDGE, :] = side


def put_left(ref, row, value, half):
    ref[row + REACH, PAD : PAD + half, :] = value[:half]


def put_right(ref, row, value, half):
    ref[row + REACH, PAD + half : PAD + 2 * half, :] = value[value.shape[0] - half :]


def encode_front_kernel(
    half, pix_ref, wh_in, wf_in, gain_in, pred_ref,
    front_ref, odd_ref, wh_ref, wf_ref, gain_ref, top_ref, bottom_ref,
    pix_s, pre_s, sem, more_sem,
):
    rows, cols = pix_ref.shape[1:3]
    width = front_ref.shape[1]
    pieces = pieces_of("front", rows, cols - width)
    loads = [
        (pix_ref.at[sec, row, col0 : col0 + width, :], pix_s.at[n])
        for n, (sec, row, col0) in enumerate(pieces)
    ]
    copies = copies_of(loads, sem)
    constants = copies_of([(wh_in, wh_ref), (wf_in, wf_ref), (gain_in, gain_ref)], more_sem)
    edges = [(pred_ref.at[0:REACH], top_ref), (pred_ref.at[rows - REACH : rows], bottom_ref)]
    edge_sem = more_sem.at[len(constants) :]
    is_first = lax.axis_index("sec") == 0
    for copy in copies[:2] + constants + copies[2:4]:
        copy.start()

    @pl.when(is_first)
    def _():
        start_all(edges, edge_sem)

    zero_sides(odd_ref, cols)
    for copy in constants:
        copy.wait()

    def pix_of(n):
        for copy in copies[n + 4 : n + 6]:
            copy.start()
        copies[n].wait()
        copies[n + 1].wait()
        return pix_s[n : n + 2].reshape(2 * width, pix_s.shape[2])

    def store(n, value):
        front_ref[n] = value
        put_left(odd_ref, n, value, half)

    encode_steps(pix_of, len(pieces), width, store, wh_ref, wf_ref, gain_ref, pre_s)

    @pl.when(is_first)
    def _():
        wait_all(edges, edge_sem)


def encode_border_kernel(
    half, pix_ref, wh_ref, wf_ref, gain_ref, odd_in, off_ref, mask_ref,
    odd_ref, even_ref, back_ref, up_ref, down_ref, pre_s,
):
    rows, cols = pix_ref.shape[1:3]
    width = up_ref.shape[1] - cols
    border = border_rows(rows)
    pieces = pieces_of("border", rows, cols - width)
    zero_sides(even_ref, cols)
    first = half // LANES - 1
    for tile in range(cols // LANES - first):
        lanes = slice((first + tile) * LANES, (first + tile + 1) * LANES)
        extra = jnp.concatenate(
            [off_ref[0, 0, :, lanes], off_ref[0, 1, :, lanes], mask_ref[0, :, lanes], mask_ref[0, :, lanes]], 0
        )
        at = rows * width + tile * 4 * rows
        back_ref[at : at + 4 * rows, :] = extra.astype(F32).astype(BF16)

    def store(n, value):
        part, m = divmod(n, len(border))
        row = border[m]
        pack = down_ref if m < REACH else up_ref
        if part == 0:
            back_ref[row * width : (row + 1) * width, :] = value
            put_right(even_ref, row, value, half)
            pack[m % REACH, half:cols, :] = value[width - half :]
        elif part == 1:
            put_left(even_ref, row, value, half)
            pack[m % REACH, 0:half, :] = value[:half]
        else:
            put_right(odd_ref, row, value, half)
            pack[m % REACH, cols : cols + width, :] = value

    encode_steps(
        lambda n: pixel_pair(pix_ref, pieces, n, width), len(pieces), width, store, wh_ref, wf_ref, gain_ref, pre_s
    )


def encode_back_kernel(half, pix_ref, wh_ref, wf_ref, gain_ref, even_in, back_in, even_ref, back_ref, pre_s):
    rows, cols = pix_ref.shape[1:3]
    width = pre_s.shape[1] // 2
    inner = inner_rows(rows)
    pieces = pieces_of("back", rows, cols - width)

    def store(n, value):
        back_ref[inner[n] * width : (inner[n] + 1) * width, :] = value
        put_right(even_ref, inner[n], value, half)

    encode_steps(
        lambda n: pixel_pair(pix_ref, pieces, n, width), len(pieces), width, store, wh_ref, wf_ref, gain_ref, pre_s
    )


def encode_inner_kernel(half, pix_ref, wh_ref, wf_ref, gain_ref, odd_in, even_in, odd_ref, even_ref, pre_s):
    rows, cols = pix_ref.shape[1:3]
    width = pre_s.shape[1] // 2
    inner = inner_rows(rows)
    pieces = pieces_of("inner", rows, cols - width)

    def store(n, value):
        part, m = divmod(n, len(inner))
        if part == 0:
            put_left(even_ref, inner[m], value, half)
        else:
            put_right(odd_ref, inner[m], value, half)

    encode_steps(
        lambda n: pixel_pair(pix_ref, pieces, n, width), len(pieces), width, store, wh_ref, wf_ref, gain_ref, pre_s
    )


def flops_of(nodes, patch, hid, feat):
    return pl.CostEstimate(
        flops=2 * nodes * hid * (patch + feat), bytes_accessed=nodes * 2 * (patch + feat), transcendentals=nodes
    )


def align(band, first, lift, row):
    band = pltpu.roll(band, (2 * LANES - first - BASE + 2 + lift) % LANES, 1)
    return jnp.where((row & 4) != 0, pltpu.roll(band, LANES - 4, 1), band)


def settle(band, row):
    for shift in (2, 1):
        band = jnp.where((row & shift) != 0, pltpu.roll(band, LANES - shift, 1), band)
    return band


def score_columns(query_of, window_of, rows, m_s, s_s, k, low):
    span = 2 * REACH + 1
    tall = LANES - low
    lane = lax.broadcasted_iota(jnp.int32, (8, LANES), 1)
    for rp in range(rows[0], rows[1] + 2 * REACH):
        j = rp % span
        window = window_of(rp, k, SEG * j)
        first = max(rp - 2 * REACH, rows[0])
        last = min(rp, rows[1] - 1)
        parts = [query_of(r, k, low) for r in range(first, last + 1)]
        query = jnp.concatenate(parts, 0) if len(parts) > 1 else parts[0]
        product = lax.dot_general(
            query, window, (((1,), (1,)), ((), ())), preferred_element_type=F32
        )
        for r in range(first, last + 1):
            for i in range(low // 8, LANES // 8):
                at = (r - first) * tall + 8 * i - low
                s = 8 * i + BASE - 4 + SEG * j
                near = product[at : at + 8, :LANES]
                far = product[at : at + 8, LANES:]
                if s + SEG <= LANES:
                    value, mask = near, (lane >= s) & (lane < s + SEG)
                elif s >= LANES:
                    value, mask = far, (lane >= s - LANES) & (lane < s + SEG - LANES)
                else:
                    value = jnp.where(lane >= s, near, far)
                    mask = (lane >= s) | (lane < s + SEG - LANES)
                dst = m_s.at[r, 8 * i : 8 * i + 8, :]
                if rp == r:
                    dst[...] = value
                else:
                    pltpu.store(dst, value, mask=mask)
        if rp > rows[0] + 2 * REACH and rp % 2:
            score_turn(m_s, s_s, rp - 2 * REACH - 1, k, low)


def score_turn(m_s, s_s, r, k, low):
    span = 2 * REACH + 1
    lane = lax.broadcasted_iota(jnp.int32, (8, LANES), 1)
    row = lax.broadcasted_iota(jnp.int32, (8, LANES), 0)
    groups = [jnp.zeros((8, LANES), F32)] * (low // 8)
    for i in range(low // 8, LANES // 8):
        one = align(m_s[r, 8 * i : 8 * i + 8, :], 8 * i, 0, row)
        two = align(m_s[r + 1, 8 * i : 8 * i + 8, :], 8 * i, 8, row)
        groups.append(settle(jnp.where((lane & 8) != 0, two, one), row))
    turned = jnp.concatenate(groups, 0).T
    lanes = pl.ds(pl.multiple_of(k * LANES, LANES), LANES)
    for n in range(2):
        for j in range(span):
            a = (j - r - n) % span
            at = SEG * j + 8 * n
            s_s[r + n, SEG * a : SEG * a + 8, lanes] = turned[at : at + 8]


def score_job(query_of, window_of, m_s, s_s, tiles, low=0, blocks=None):
    blocks = blocks or ((0, s_s.shape[0]),)
    first = 1 if low else 0

    def columns(m, k, low):
        for rows in blocks:
            score_columns(query_of, window_of, rows, m_s.at[m], s_s, k, low)

    if low:
        columns(0, 0, low)
    step = m_s.shape[0]
    whole, odd = (tiles - first) // step, (tiles - first) % step

    def body(n, carry):
        for m in range(step):
            columns(m, step * n + m + first, 0)
        return carry

    lax.fori_loop(0, whole, body, 0)
    for m in range(odd):
        columns(m, tiles - odd + m, 0)


def padded_query(ref, tile0=0):
    def query_of(r, k, low):
        at = pl.multiple_of((k + tile0) * LANES + PAD + low, 16)
        return ref[r + REACH, pl.ds(at, LANES - low), :]

    return query_of


def padded_window(ref, halo=None, tile0=0):
    rows = ref.shape[0] - 2 * REACH

    def window_of(rp, k, shift):
        at = pl.multiple_of((k + tile0) * LANES + (PAD - BASE) - shift, 16)
        if halo is not None and rp < REACH:
            return halo[rp, pl.ds(at, 2 * LANES), :]
        if halo is not None and rp >= rows + REACH:
            return halo[rp - rows, pl.ds(at, 2 * LANES), :]
        return ref[rp, pl.ds(at, 2 * LANES), :]

    return window_of


def flow_tile(s_s, oy, ox, lanes):
    y_low, y_high, x_low, x_high = oy < 0, oy > 0, ox < 0, ox > 0
    feat = F32(1.0 / LANES)
    by_row = {}
    for i in range(3):
        for b in range(5):
            v = [s_s[:, SEG * (i + d) + b, lanes] for d in range(3)]
            by_row[i, b] = jnp.where(y_low, v[0], jnp.where(y_high, v[2], v[1]))
    total = jnp.ones_like(oy)
    sum_y = jnp.zeros_like(oy)
    sum_x = jnp.zeros_like(oy)
    for i in range(3):
        for j in range(3):
            near = jnp.where(
                x_low, by_row[i, j], jnp.where(x_high, by_row[i, j + 2], by_row[i, j + 1])
            )
            near = near * feat
            weight = near * near
            total = total + weight
            if i != 1:
                sum_y = sum_y + weight * (i - 1)
            if j != 1:
                sum_x = sum_x + weight * (j - 1)
    return oy + sum_y / total, ox + sum_x / total


def flows_of(s_s, off_ref, flow_ref, tiles):
    def body(k, carry):
        lanes = pl.ds(pl.multiple_of(k * LANES, LANES), LANES)
        fy, fx = flow_tile(s_s, off_ref[0, :, lanes].astype(F32), off_ref[1, :, lanes].astype(F32), lanes)
        flow_ref[0, :, lanes] = fy
        flow_ref[1, :, lanes] = fx
        return carry

    lax.fori_loop(0, tiles, body, 0)


def copies_of(pairs, sem):
    return [pltpu.make_async_copy(src, dst, sem.at[n]) for n, (src, dst) in enumerate(pairs)]


def start_all(pairs, sem):
    for copy in copies_of(pairs, sem):
        copy.start()


def wait_all(pairs, sem):
    for copy in copies_of(pairs, sem):
        copy.wait()


def near_scores_kernel(
    half, even_ref, odd_ref, pred_ref, pup_ref, pdown_ref, off_ref,
    s_s, flow0_ref, ref0_s, s0_s, m_s, sem,
):
    rows = odd_ref.shape[0] - 2 * REACH
    cols = 2 * half
    far = half - 2 * EDGE
    is_first = lax.axis_index("sec") == 0
    tile0 = half // LANES - 1
    tiles = cols // LANES - tile0
    to = slice(PAD + far, PAD + cols)
    before = [
        (pred_ref.at[:, far:cols, :], ref0_s.at[REACH : rows + REACH, to, :]),
        (pup_ref.at[:, far:cols, :], ref0_s.at[0:REACH, to, :]),
        (pdown_ref.at[:, far:cols, :], ref0_s.at[rows + REACH : rows + 2 * REACH, to, :]),
    ]

    @pl.when(is_first)
    def _():
        start_all(before, sem)

    flow0_ref[...] = jnp.zeros_like(flow0_ref)
    score_job(
        padded_query(odd_ref), padded_window(even_ref), m_s, s_s, cols // LANES, 0, ((REACH, rows - REACH),)
    )

    @pl.when(is_first)
    def _():
        zero_sides(ref0_s, cols)
        wait_all(before, sem)
        score_job(
            padded_query(even_ref, tile0), padded_window(ref0_s, None, tile0), m_s, s0_s, tiles, LANES - EDGE
        )
        flows_of(s0_s, off_ref.at[0, :, :, tile0 * LANES : cols], flow0_ref, tiles)


def own_scores_kernel(
    half, even_ref, odd_ref, up_ref, down_ref, off_ref, s_in, front_ref, pred_ref,
    s_s, flow_ref, ref_next, halo_next, halo_s, m_s, sem, next_sem, ref_sem,
):
    rows = odd_ref.shape[0] - 2 * REACH
    cols = 2 * half
    width = front_ref.shape[1]
    far = cols - width
    is_first = lax.axis_index("sec") == 0
    halos = [
        (up_ref.at[:, 0:cols, :], halo_s.at[0:REACH, PAD : PAD + cols, :]),
        (down_ref.at[:, 0:cols, :], halo_s.at[REACH : 2 * REACH, PAD : PAD + cols, :]),
    ]
    start_all(halos, sem)
    to = slice(PAD + far, PAD + cols)
    beyond = [
        (up_ref.at[:, cols : cols + width, :], halo_next.at[0:REACH, to, :]),
        (down_ref.at[:, cols : cols + width, :], halo_next.at[REACH : 2 * REACH, to, :]),
    ]
    start_all(beyond, next_sem)
    inside = ref_next.at[REACH : rows + REACH, PAD : PAD + width, :]
    before = [(pred_ref.at[:, 0:width, :], inside)]
    passed = [(front_ref, inside)]

    @pl.when(is_first)
    def _():
        start_all(before, ref_sem)

    @pl.when(jnp.logical_not(is_first))
    def _():
        start_all(passed, ref_sem)

    zero_sides(halo_s, cols)
    zero_sides(halo_next, cols)
    ref_next[:, PAD - EDGE : PAD, :] = jnp.zeros((rows + 2 * REACH, EDGE, LANES), BF16)
    wait_all(halos, sem)
    score_job(
        padded_query(odd_ref), padded_window(even_ref, halo_s), m_s, s_s, cols // LANES, 0,
        ((0, REACH), (rows - REACH, rows)),
    )
    flows_of(s_s, off_ref.at[1], flow_ref, cols // LANES)
    wait_all(beyond, next_sem)

    @pl.when(is_first)
    def _():
        wait_all(before, ref_sem)

    @pl.when(jnp.logical_not(is_first))
    def _():
        wait_all(passed, ref_sem)


def front_scores_kernel(
    half, even_ref, ref_in, fup_ref, fdown_ref, pup_ref, pdown_ref, off_ref, flow0_ref,
    ref_s, flow_ref, s_s, m_s, sem,
):
    rows = even_ref.shape[0] - 2 * REACH
    cols = 2 * half
    width = fup_ref.shape[1]
    is_first = lax.axis_index("sec") == 0
    above = ref_s.at[0:REACH, PAD : PAD + width, :]
    below = ref_s.at[rows + REACH : rows + 2 * REACH, PAD : PAD + width, :]
    before = [(pup_ref.at[:, 0:width, :], above), (pdown_ref.at[:, 0:width, :], below)]
    passed = [(fup_ref, above), (fdown_ref, below)]

    @pl.when(is_first)
    def _():
        start_all(before, sem)
        wait_all(before, sem)

    @pl.when(jnp.logical_not(is_first))
    def _():
        start_all(passed, sem)
        wait_all(passed, sem)

    tiles = half // LANES
    score_job(padded_query(even_ref), padded_window(ref_s), m_s, s_s, tiles)
    flow_ref[:, :, half:cols] = flow0_ref[:, :, LANES:]
    flows_of(s_s, off_ref.at[0], flow_ref, tiles)


def pairs_out(pack_ref, at, tops, bottoms):
    for n, (top, bottom) in enumerate(zip(tops, bottoms)):
        pack_ref[at + 16 * n : at + 16 * n + 16, :] = jnp.concatenate([top, bottom], 0).astype(BF16)
    return at + 16 * len(tops)


def back_scores_kernel(
    half, back_ref, odd_ref, halo_ref, mask_ref, flow1_ref, flow_ref,
    flow2_ref, pack_ref, s_s, m_s,
):
    rows = odd_ref.shape[0] - 2 * REACH
    cols = 2 * half
    tile0 = half // LANES - 1
    tiles = cols // LANES - tile0
    width = (back_ref.shape[0] - 4 * rows * tiles) // rows
    far = cols - width

    def query_of(r, k, low):
        at = (k + tile0) * LANES + low - far + r * width
        return back_ref[pl.ds(pl.multiple_of(at, 16), LANES - low), :]

    score_job(query_of, padded_window(odd_ref, halo_ref, tile0), m_s, s_s, tiles, LANES - EDGE)

    def body(k, carry):
        lanes = pl.ds(pl.multiple_of(k * LANES, LANES), LANES)
        at = pl.multiple_of(k * 4 * rows + rows * width, 4 * rows)
        extra = back_ref[pl.ds(at, 4 * rows), :].astype(F32)
        fy, fx = flow_tile(s_s, extra[:rows], extra[rows : 2 * rows], lanes)
        flow2_ref[0, :, lanes] = fy
        flow2_ref[1, :, lanes] = fx
        flow2_ref[2, :, lanes] = extra[2 * rows : 3 * rows]
        return carry

    lax.fori_loop(0, tiles, body, 0)

    def tiles_of(ref, count):
        return [ref[:, n * LANES : (n + 1) * LANES] for n in range(count)]

    n = 0
    for ref, count in ((flow1_ref, cols // LANES), (flow_ref, cols // LANES), (flow2_ref, flow2_ref.shape[2] // LANES)):
        n = pairs_out(pack_ref, n, tiles_of(ref.at[0], count), tiles_of(ref.at[1], count))
    masks = []
    for ref, count in ((mask_ref.at[1], cols // LANES), (mask_ref.at[0], cols // LANES), (flow2_ref.at[2], flow2_ref.shape[2] // LANES)):
        masks += [m.astype(F32) for m in tiles_of(ref, count)]
    if len(masks) % 2:
        masks.append(masks[-1])
    pairs_out(pack_ref, n, masks[0::2], masks[1::2])


def relax_kernel(
    half, up_ref, down_ref, flow1_ref, flow3_ref, flow2_ref, mask_ref, f1_ref, f3_ref, msg_ref,
    field_s, pull_s, keep_s,
):
    rows, cols = flow1_ref.shape[1:]
    deep = rows + 2 * ITERS
    place = lax.axis_index("tile")
    count = lax.axis_size("tile")
    glob = place * rows + lax.broadcasted_iota(jnp.int32, (deep, LANES), 0) - ITERS
    inside = ((glob >= 0) & (glob < rows * count)).astype(F32)
    widths = (cols, cols, flow2_ref.shape[2])
    tiles = [w // LANES for w in widths]
    flows = (flow1_ref, flow3_ref, flow2_ref)
    own_masks = (mask_ref.at[1], mask_ref.at[0], flow2_ref.at[2])
    starts = [0, tiles[0], tiles[0] + tiles[1]]
    mask_at = 16 * sum(tiles)
    for job in range(3):
        for k in range(tiles[job]):
            lanes = slice(k * LANES, (k + 1) * LANES)
            at = 16 * (starts[job] + k)
            m_at = mask_at + 8 * (starts[job] + k)
            half_at = m_at // 16 * 16
            sub = slice(m_at - half_at, m_at - half_at + 8)
            upper = up_ref[at : at + 16, :].astype(F32)
            lower = down_ref[at : at + 16, :].astype(F32)
            m_up = up_ref[half_at : half_at + 16, :].astype(F32)[sub]
            m_down = down_ref[half_at : half_at + 16, :].astype(F32)[sub]
            weight = stiffness * jnp.concatenate(
                [m_up, own_masks[job][:, lanes].astype(F32), m_down], 0
            )
            keep_s[job, :, lanes] = (step_size - step_size * weight) * inside
            for c in range(2):
                flow = jnp.concatenate(
                    [upper[8 * c : 8 * c + 8], flows[job][c, :, lanes], lower[8 * c : 8 * c + 8]], 0
                )
                pull = step_size * weight * flow * inside
                pull_s[job, c, :, lanes] = pull
                field_s[job, c, :, lanes] = pull
    step = step_size * inside

    def body(n, carry):
        for job in range(3):
            for c in range(2):
                old = [field_s[job, c, :, k * LANES : (k + 1) * LANES] for k in range(tiles[job])]
                lane = lax.broadcasted_iota(jnp.int32, (deep, LANES), 1)
                nxt = [pltpu.roll(x, LANES - 1, 1) for x in old]
                prv = [pltpu.roll(x, 1, 1) for x in old]
                zero = jnp.zeros_like(old[0])
                for k in range(tiles[job]):
                    lanes = slice(k * LANES, (k + 1) * LANES)
                    right = jnp.where(lane == LANES - 1, nxt[k + 1] if k + 1 < tiles[job] else zero, nxt[k])
                    left = jnp.where(lane == 0, prv[k - 1] if k else zero, prv[k])
                    around = pltpu.roll(old[k], 1, 0) + pltpu.roll(old[k], deep - 1, 0) + left + right
                    field_s[job, c, :, lanes] = (
                        keep_s[job, :, lanes] * old[k] + step * around + pull_s[job, c, :, lanes]
                    )
        return carry

    lax.fori_loop(0, ITERS - 1, body, 0)
    is_first = lax.axis_index("sec") == 0
    seam = half - EDGE // 2
    mine = slice(ITERS, ITERS + rows)
    lead = half - LANES
    for c in range(2):
        for k in range(tiles[0]):
            lanes = slice(k * LANES, (k + 1) * LANES)
            col = lax.broadcasted_iota(jnp.int32, (rows, LANES), 1) + k * LANES
            one = field_s[0, c, mine, lanes]
            front = field_s[1, c, mine, lanes]
            if (k + 1) * LANES > seam:
                front = jnp.where((col < seam) | is_first, front, 0.0)
            total = one + front
            if k * LANES >= lead:
                back = field_s[2, c, mine, k * LANES - lead : (k + 1) * LANES - lead]
                total = total + jnp.where(col >= seam, back, 0.0)
            f1_ref[c, :, lanes] = one
            f3_ref[c, :, lanes] = front
            msg_ref[c, :, lanes] = total.astype(msg_ref.dtype)


def shards(pixels, pred, offsets, mask, base_shift, w_hidden, w_feature, feat_gain):
    secs, rows, cols, patch = pixels.shape
    hid, feat = w_feature.shape
    assert secs == 2 and rows == ITERS and feat == LANES and cols % (2 * LANES) == 0
    half = cols // 2
    width = half + 2 * EDGE
    span = half + LANES
    deep = rows + 2 * REACH
    tail = 4 * rows * (span // LANES)
    full = cols + 2 * PAD
    gain = feat_gain.reshape(1, feat)
    shape = jax.ShapeDtypeStruct
    padded = shape((deep, full, feat), BF16)
    pre = pltpu.VMEM((2, 2 * width, feat), F32)

    dma = pltpu.SemaphoreType.DMA

    def call(kernel, ins, in_specs, outs, scratch, cost, limit, aliases=None):
        return pl.pallas_call(
            functools.partial(kernel, half),
            out_shape=outs,
            in_specs=in_specs,
            out_specs=tuple(VMEM for _ in outs),
            scratch_shapes=scratch,
            input_output_aliases=aliases or {},
            compiler_params=params(limit),
            cost_estimate=cost,
        )(*ins)

    def encode_cost(kind):
        return flops_of(len(pieces_of(kind, rows, 0)) * width, patch, hid, feat)

    def in_place(value):
        return pltpu.with_memory_space_constraint(value, pltpu.HBM)

    edges = shape((REACH, cols, feat), BF16)
    front, odd, wh, wf, gain, top, bottom = call(
        encode_front_kernel,
        (in_place(pixels), in_place(w_hidden), in_place(w_feature), in_place(gain), in_place(pred)), [HBM] * 5,
        (
            shape((rows, width, feat), BF16), padded,
            shape(w_hidden.shape, BF16), shape(w_feature.shape, BF16), shape(gain.shape, F32), edges, edges,
        ),
        [pltpu.VMEM((rows, width, patch), BF16), pre, dma((rows,)), dma((5,))],
        encode_cost("front"), 12,
    )
    weights = (pixels, wh, wf, gain)
    front_in = hop(front, "sec", 1)
    pup = hop_plane(bottom, 1)
    pdown = hop_plane(top, -1)
    pack = shape((REACH, cols + width, feat), BF16)
    odd, even, back, up, down = call(
        encode_border_kernel,
        (*weights, odd, offsets, mask), [VMEM] * 7,
        (padded, padded, shape((rows * width + tail, feat), BF16), pack, pack),
        [pre], encode_cost("border"), 10, {4: 0},
    )
    up_in = hop(up, "tile", 1)
    down_in = hop(down, "tile", -1)
    even, back = call(
        encode_back_kernel, (*weights, even, back), [VMEM] * 6,
        (padded, shape(back.shape, BF16)), [pre], encode_cost("back"), 10, {4: 0, 5: 1},
    )
    back_in = hop(back, "sec", -1)
    odd, even = call(
        encode_inner_kernel, (*weights, odd, even), [VMEM] * 6,
        (padded, padded), [pre], encode_cost("inner"), 10, {4: 0, 5: 1},
    )

    bands = SEG * (2 * REACH + 1)
    nodes = rows * cols

    def score_cost(part):
        return pl.CostEstimate(
            flops=int(part * nodes * 2560 * LANES), bytes_accessed=int(part * nodes * 512), transcendentals=0
        )

    halo = pltpu.VMEM((2 * REACH, full, feat), BF16)
    turning = pltpu.VMEM((2, rows, LANES, LANES), F32)
    turning4 = pltpu.VMEM((4, rows, LANES, LANES), F32)
    whole = pltpu.VMEM((deep, full, feat), BF16)
    flow0_shape = shape((2, rows, span), F32)
    scores, flow0 = call(
        near_scores_kernel, (even, odd, in_place(pred), pup, pdown, offsets),
        [VMEM] * 2 + [HBM] + [VMEM] * 3, (shape((rows, bands, cols), F32), flow0_shape),
        [whole, pltpu.VMEM((rows, bands, span), F32), turning4, dma((3,))], score_cost(0.5), 18,
    )
    fup_in = hop(front_in[rows - REACH :], "tile", 1)
    fdown_in = hop(front_in[:REACH], "tile", -1)
    ref_shape = shape((deep, half + 3 * PAD, feat), BF16)
    _, flow1, ref, beyond = call(
        own_scores_kernel, (even, odd, up_in, down_in, offsets, scores, front_in, in_place(pred)),
        [VMEM] * 7 + [HBM],
        (shape(scores.shape, F32), shape((2, rows, cols), F32), ref_shape, shape((2 * REACH, full, feat), BF16)),
        [halo, turning4, dma((2,)), dma((2,)), dma((1,))], score_cost(0.5), 14, {5: 0},
    )
    _, flow3 = call(
        front_scores_kernel, (even, ref, fup_in, fdown_in, pup, pdown, offsets, flow0),
        [VMEM] * 8, (ref_shape, shape((2, rows, cols), F32)),
        [pltpu.VMEM((rows, bands, half), F32), turning, dma((2,))], score_cost(0.5), 12, {1: 0},
    )

    tiles = 2 * (cols // LANES) + span // LANES
    pack_rows = 16 * tiles + 16 * ((tiles + 1) // 2)
    flow2, pack = call(
        back_scores_kernel, (back_in, odd, beyond, mask, flow1, flow3), [VMEM] * 6,
        (shape((3, rows, span), F32), shape((pack_rows, LANES), BF16)),
        [pltpu.VMEM((rows, bands, span), F32), turning], score_cost(0.55), 12,
    )
    pack_up = hop(pack, "tile", 1)
    pack_down = hop(pack, "tile", -1)

    wide = rows + 2 * ITERS
    f1, f3, msg = pl.pallas_call(
        functools.partial(relax_kernel, half),
        out_shape=(shape((2, rows, cols), F32), shape((2, rows, cols), F32), shape((2, rows, cols), BF16)),
        in_specs=[VMEM] * 6,
        out_specs=(VMEM,) * 3,
        scratch_shapes=[
            pltpu.VMEM((3, 2, wide, cols), F32),
            pltpu.VMEM((3, 2, wide, cols), F32),
            pltpu.VMEM((3, wide, cols), F32),
        ],
        compiler_params=params(12),
        cost_estimate=pl.CostEstimate(flops=nodes * 24 * 12 * 8, bytes_accessed=nodes * 40, transcendentals=0),
        name="relax",
    )(pack_up, pack_down, flow1, flow3, flow2, mask)

    prefix = base_shift
    for steps in range(1, lax.axis_size("sec")):
        prefix = prefix + hop(msg, "sec", steps).astype(F32)
    first = prefix + f3
    return jnp.stack([first, first + f1], axis=0)


def solution(mesh):
    in_specs = (
        P("sec", "tile", None, None),
        P("tile", None, None),
        P("sec", None, "tile", None),
        P("sec", "tile", None),
        P(None, "tile", None),
        P(),
        P(),
        P(),
    )
    out_specs = P("sec", None, "tile", None)
    return jax.shard_map(shards, mesh=mesh, in_specs=in_specs, out_specs=out_specs, check_vma=False)
```

```python
import functools

import jax
import jax.numpy as jnp
from jax import lax
from jax.experimental import pallas as pl
from jax.experimental.pallas import tpu as pltpu
from jax.sharding import PartitionSpec as P


ITERS = 8
REACH = 2
LANES = 128
BASE = 16
PAD = LANES
SEG = 16
EDGE = 16

epsilon = 1e-05
step_size = 0.2
stiffness = 0.5

F32 = jnp.float32
BF16 = jnp.bfloat16
HBM = pl.BlockSpec(memory_space=pltpu.HBM)
VMEM = pl.BlockSpec(memory_space=pltpu.VMEM)


def hop(value, axis, steps):
    count = lax.axis_size(axis)
    pairs = [(i, i + steps) for i in range(count) if 0 <= i + steps < count]
    return lax.ppermute(value, axis, pairs)


def swap(value, first, plane=False):
    tiles = lax.axis_size("tile")
    stride = lax.axis_size("sec") if plane else 1
    pairs = []
    for i in range(first, tiles - 1, 2):
        pairs += [(i * stride, (i + 1) * stride), ((i + 1) * stride, i * stride)]
    return lax.ppermute(value, ("tile", "sec") if plane else "tile", pairs)


def sides(rows):
    last = rows - REACH
    facing = jnp.where(lax.rem(lax.axis_index("tile"), 2) == 0, last, 0)
    return facing, last - facing


def params(limit):
    return pltpu.CompilerParams(vmem_limit_bytes=limit * 1024 * 1024)


def matmuls(pix, wh, wf):
    hidden = jnp.maximum(jnp.dot(pix, wh, preferred_element_type=F32), 0.0).astype(BF16)
    return jnp.dot(hidden, wf, preferred_element_type=F32)


def normed(pre, gain):
    mean = jnp.mean(pre * pre, axis=-1, keepdims=True)
    return (pre * lax.rsqrt(mean + epsilon) * gain).astype(BF16)


def encode_steps(pix_of, count, width, store, wh_ref, wf_ref, gain_ref, pre_s):
    steps = count // 2

    def finish(n):
        value = normed(pre_s[n % 2], gain_ref[...])
        store(2 * n, value[:width])
        store(2 * n + 1, value[width:])

    for n in range(steps):
        pre_s[n % 2] = matmuls(pix_of(2 * n), wh_ref[...], wf_ref[...])
        if n:
            finish(n - 1)
    finish(steps - 1)


def inner_rows(rows):
    return list(range(REACH, rows - REACH))


def pieces_of(kind, rows, far):
    inner = inner_rows(rows)
    if kind == "front":
        return [(1, r, 0) for r in range(rows)]
    if kind == "back":
        return [(0, r, far) for r in inner]
    return [(0, r, 0) for r in inner] + [(1, r, far) for r in inner]


def pixel_pair(pix_ref, pieces, n, width):
    rows = [pix_ref[sec, row, col0 : col0 + width, :] for sec, row, col0 in pieces[n : n + 2]]
    return jnp.concatenate(rows, 0)


def zero_sides(ref, cols):
    side = jnp.zeros((ref.shape[0], EDGE, ref.shape[2]), BF16)
    ref[:, PAD - EDGE : PAD, :] = side
    ref[:, PAD + cols : PAD + cols + EDGE, :] = side


def put_left(ref, row, value, half):
    ref[row + REACH, PAD : PAD + half, :] = value[:half]


def put_right(ref, row, value, half):
    ref[row + REACH, PAD + half : PAD + 2 * half, :] = value[value.shape[0] - half :]


def encode_front_kernel(
    half, pix_ref, wh_in, wf_in, gain_in, pred_ref,
    front_ref, odd_ref, wh_ref, wf_ref, gain_ref, pred_a_ref, pred_b_ref,
    pix_s, pre_s, sem, more_sem,
):
    rows, cols = pix_ref.shape[1:3]
    width = front_ref.shape[1]
    pieces = pieces_of("front", rows, cols - width)
    loads = [
        (pix_ref.at[sec, row, col0 : col0 + width, :], pix_s.at[n])
        for n, (sec, row, col0) in enumerate(pieces)
    ]
    copies = copies_of(loads, sem)
    constants = copies_of([(wh_in, wh_ref), (wf_in, wf_ref), (gain_in, gain_ref)], more_sem)
    side_a, side_b = sides(rows)
    edges = [(pred_ref.at[pl.ds(side_a, REACH)], pred_a_ref), (pred_ref.at[pl.ds(side_b, REACH)], pred_b_ref)]
    edge_sem = more_sem.at[len(constants) :]
    is_first = lax.axis_index("sec") == 0
    for copy in copies[:2] + constants + copies[2:4]:
        copy.start()

    @pl.when(is_first)
    def _():
        start_all(edges, edge_sem)

    zero_sides(odd_ref, cols)
    for copy in constants:
        copy.wait()

    def pix_of(n):
        for copy in copies[n + 4 : n + 6]:
            copy.start()
        copies[n].wait()
        copies[n + 1].wait()
        return pix_s[n : n + 2].reshape(2 * width, pix_s.shape[2])

    def store(n, value):
        front_ref[n] = value
        put_left(odd_ref, n, value, half)

    encode_steps(pix_of, len(pieces), width, store, wh_ref, wf_ref, gain_ref, pre_s)

    @pl.when(is_first)
    def _():
        wait_all(edges, edge_sem)


def encode_border_kernel(
    half, pix_ref, wh_ref, wf_ref, gain_ref, odd_in, off_ref, mask_ref,
    odd_ref, even_ref, back_ref, pack_a_ref, pack_b_ref, pre_s,
):
    rows, cols = pix_ref.shape[1:3]
    width = pack_a_ref.shape[1] - cols
    side_a, side_b = sides(rows)
    border = [side_a + r for r in range(REACH)] + [side_b + r for r in range(REACH)]
    far = cols - width
    pieces = [(0, r, far) for r in border] + [(0, r, 0) for r in border] + [(1, r, far) for r in border]
    zero_sides(even_ref, cols)
    first = half // LANES - 1
    for tile in range(cols // LANES - first):
        lanes = slice((first + tile) * LANES, (first + tile + 1) * LANES)
        extra = jnp.concatenate(
            [off_ref[0, 0, :, lanes], off_ref[0, 1, :, lanes], mask_ref[0, :, lanes], mask_ref[0, :, lanes]], 0
        )
        at = rows * width + tile * 4 * rows
        back_ref[at : at + 4 * rows, :] = extra.astype(F32).astype(BF16)

    def store(n, value):
        part, m = divmod(n, len(border))
        row = border[m]
        pack = pack_a_ref if m < REACH else pack_b_ref
        if part == 0:
            back_ref[pl.ds(pl.multiple_of(row * width, 16), width), :] = value
            put_right(even_ref, row, value, half)
            pack[m % REACH, half:cols, :] = value[width - half :]
        elif part == 1:
            put_left(even_ref, row, value, half)
            pack[m % REACH, 0:half, :] = value[:half]
        else:
            put_right(odd_ref, row, value, half)
            pack[m % REACH, cols : cols + width, :] = value

    encode_steps(
        lambda n: pixel_pair(pix_ref, pieces, n, width), len(pieces), width, store, wh_ref, wf_ref, gain_ref, pre_s
    )


def encode_back_kernel(half, pix_ref, wh_ref, wf_ref, gain_ref, even_in, back_in, even_ref, back_ref, pre_s):
    rows, cols = pix_ref.shape[1:3]
    width = pre_s.shape[1] // 2
    inner = inner_rows(rows)
    pieces = pieces_of("back", rows, cols - width)

    def store(n, value):
        back_ref[inner[n] * width : (inner[n] + 1) * width, :] = value
        put_right(even_ref, inner[n], value, half)

    encode_steps(
        lambda n: pixel_pair(pix_ref, pieces, n, width), len(pieces), width, store, wh_ref, wf_ref, gain_ref, pre_s
    )


def encode_inner_kernel(half, pix_ref, wh_ref, wf_ref, gain_ref, odd_in, even_in, odd_ref, even_ref, pre_s):
    rows, cols = pix_ref.shape[1:3]
    width = pre_s.shape[1] // 2
    inner = inner_rows(rows)
    pieces = pieces_of("inner", rows, cols - width)

    def store(n, value):
        part, m = divmod(n, len(inner))
        if part == 0:
            put_left(even_ref, inner[m], value, half)
        else:
            put_right(odd_ref, inner[m], value, half)

    encode_steps(
        lambda n: pixel_pair(pix_ref, pieces, n, width), len(pieces), width, store, wh_ref, wf_ref, gain_ref, pre_s
    )


def flops_of(nodes, patch, hid, feat):
    return pl.CostEstimate(
        flops=2 * nodes * hid * (patch + feat), bytes_accessed=nodes * 2 * (patch + feat), transcendentals=nodes
    )


def align(band, first, lift, row):
    band = pltpu.roll(band, (2 * LANES - first - BASE + 2 + lift) % LANES, 1)
    return jnp.where((row & 4) != 0, pltpu.roll(band, LANES - 4, 1), band)


def settle(band, row):
    for shift in (2, 1):
        band = jnp.where((row & shift) != 0, pltpu.roll(band, LANES - shift, 1), band)
    return band


def score_columns(query_of, window_of, rows, m_s, s_s, k, low):
    span = 2 * REACH + 1
    tall = LANES - low
    lane = lax.broadcasted_iota(jnp.int32, (8, LANES), 1)
    for rp in range(rows[0], rows[1] + 2 * REACH):
        j = rp % span
        window = window_of(rp, k, SEG * j)
        first = max(rp - 2 * REACH, rows[0])
        last = min(rp, rows[1] - 1)
        parts = [query_of(r, k, low) for r in range(first, last + 1)]
        query = jnp.concatenate(parts, 0) if len(parts) > 1 else parts[0]
        product = lax.dot_general(
            query, window, (((1,), (1,)), ((), ())), preferred_element_type=F32
        )
        for r in range(first, last + 1):
            for i in range(low // 8, LANES // 8):
                at = (r - first) * tall + 8 * i - low
                s = 8 * i + BASE - 4 + SEG * j
                near = product[at : at + 8, :LANES]
                far = product[at : at + 8, LANES:]
                if s + SEG <= LANES:
                    value, mask = near, (lane >= s) & (lane < s + SEG)
                elif s >= LANES:
                    value, mask = far, (lane >= s - LANES) & (lane < s + SEG - LANES)
                else:
                    value = jnp.where(lane >= s, near, far)
                    mask = (lane >= s) | (lane < s + SEG - LANES)
                dst = m_s.at[r, 8 * i : 8 * i + 8, :]
                if rp == r:
                    dst[...] = value
                else:
                    pltpu.store(dst, value, mask=mask)
        if rp > rows[0] + 2 * REACH and rp % 2:
            score_turn(m_s, s_s, rp - 2 * REACH - 1, k, low)


def score_turn(m_s, s_s, r, k, low):
    span = 2 * REACH + 1
    lane = lax.broadcasted_iota(jnp.int32, (8, LANES), 1)
    row = lax.broadcasted_iota(jnp.int32, (8, LANES), 0)
    groups = [jnp.zeros((8, LANES), F32)] * (low // 8)
    for i in range(low // 8, LANES // 8):
        one = align(m_s[r, 8 * i : 8 * i + 8, :], 8 * i, 0, row)
        two = align(m_s[r + 1, 8 * i : 8 * i + 8, :], 8 * i, 8, row)
        groups.append(settle(jnp.where((lane & 8) != 0, two, one), row))
    turned = jnp.concatenate(groups, 0).T
    lanes = pl.ds(pl.multiple_of(k * LANES, LANES), LANES)
    for n in range(2):
        for j in range(span):
            a = (j - r - n) % span
            at = SEG * j + 8 * n
            s_s[r + n, SEG * a : SEG * a + 8, lanes] = turned[at : at + 8]


def score_job(query_of, window_of, m_s, s_s, tiles, low=0, blocks=None):
    blocks = blocks or ((0, s_s.shape[0]),)
    first = 1 if low else 0

    def columns(m, k, low):
        for rows in blocks:
            score_columns(query_of, window_of, rows, m_s.at[m], s_s, k, low)

    if low:
        columns(0, 0, low)
    step = m_s.shape[0]
    whole, odd = (tiles - first) // step, (tiles - first) % step

    def body(n, carry):
        for m in range(step):
            columns(m, step * n + m + first, 0)
        return carry

    lax.fori_loop(0, whole, body, 0)
    for m in range(odd):
        columns(m, tiles - odd + m, 0)


def padded_query(ref, tile0=0):
    def query_of(r, k, low):
        at = pl.multiple_of((k + tile0) * LANES + PAD + low, 16)
        return ref[r + REACH, pl.ds(at, LANES - low), :]

    return query_of


def padded_window(ref, halo=None, tile0=0):
    rows = ref.shape[0] - 2 * REACH

    def window_of(rp, k, shift):
        at = pl.multiple_of((k + tile0) * LANES + (PAD - BASE) - shift, 16)
        if halo is not None and rp < REACH:
            return halo[rp, pl.ds(at, 2 * LANES), :]
        if halo is not None and rp >= rows + REACH:
            return halo[rp - rows, pl.ds(at, 2 * LANES), :]
        return ref[rp, pl.ds(at, 2 * LANES), :]

    return window_of


def flow_tile(s_s, oy, ox, lanes):
    y_low, y_high, x_low, x_high = oy < 0, oy > 0, ox < 0, ox > 0
    feat = F32(1.0 / LANES)
    by_row = {}
    for i in range(3):
        for b in range(5):
            v = [s_s[:, SEG * (i + d) + b, lanes] for d in range(3)]
            by_row[i, b] = jnp.where(y_low, v[0], jnp.where(y_high, v[2], v[1]))
    total = jnp.ones_like(oy)
    sum_y = jnp.zeros_like(oy)
    sum_x = jnp.zeros_like(oy)
    for i in range(3):
        for j in range(3):
            near = jnp.where(
                x_low, by_row[i, j], jnp.where(x_high, by_row[i, j + 2], by_row[i, j + 1])
            )
            near = near * feat
            weight = near * near
            total = total + weight
            if i != 1:
                sum_y = sum_y + weight * (i - 1)
            if j != 1:
                sum_x = sum_x + weight * (j - 1)
    return oy + sum_y / total, ox + sum_x / total


def flows_of(s_s, off_ref, flow_ref, tiles):
    def body(k, carry):
        lanes = pl.ds(pl.multiple_of(k * LANES, LANES), LANES)
        fy, fx = flow_tile(s_s, off_ref[0, :, lanes].astype(F32), off_ref[1, :, lanes].astype(F32), lanes)
        flow_ref[0, :, lanes] = fy
        flow_ref[1, :, lanes] = fx
        return carry

    lax.fori_loop(0, tiles, body, 0)


def copies_of(pairs, sem):
    return [pltpu.make_async_copy(src, dst, sem.at[n]) for n, (src, dst) in enumerate(pairs)]


def start_all(pairs, sem):
    for copy in copies_of(pairs, sem):
        copy.start()


def wait_all(pairs, sem):
    for copy in copies_of(pairs, sem):
        copy.wait()


def pick_kernel(half, front_ref, a_ref, b_ref):
    side_a, side_b = sides(front_ref.shape[0])
    for r in range(REACH):
        a_ref[r] = front_ref[side_a + r]
        b_ref[r] = front_ref[side_b + r]


def beyond_rows(rows):
    side_a, side_b = sides(rows)
    below = rows + REACH
    return jnp.where(side_a > 0, below, 0), jnp.where(side_b > 0, below, 0)


def near_scores_kernel(
    half, even_ref, odd_ref, pred_ref, pred_a_ref, pred_b_ref, off_ref,
    s_s, flow0_ref, ref0_s, s0_s, m_s, sem,
):
    rows = odd_ref.shape[0] - 2 * REACH
    cols = 2 * half
    far = half - 2 * EDGE
    is_first = lax.axis_index("sec") == 0
    tile0 = half // LANES - 1
    tiles = cols // LANES - tile0
    to = slice(PAD + far, PAD + cols)
    beyond_a, beyond_b = beyond_rows(rows)
    before = [
        (pred_ref.at[:, far:cols, :], ref0_s.at[REACH : rows + REACH, to, :]),
        (pred_a_ref.at[:, far:cols, :], ref0_s.at[pl.ds(beyond_a, REACH), to, :]),
        (pred_b_ref.at[:, far:cols, :], ref0_s.at[pl.ds(beyond_b, REACH), to, :]),
    ]

    @pl.when(is_first)
    def _():
        start_all(before, sem)

    flow0_ref[...] = jnp.zeros_like(flow0_ref)
    score_job(
        padded_query(odd_ref), padded_window(even_ref), m_s, s_s, cols // LANES, 0, ((REACH, rows - REACH),)
    )

    @pl.when(is_first)
    def _():
        zero_sides(ref0_s, cols)
        wait_all(before, sem)
        score_job(
            padded_query(even_ref, tile0), padded_window(ref0_s, None, tile0), m_s, s0_s, tiles, LANES - EDGE
        )
        flows_of(s0_s, off_ref.at[0, :, :, tile0 * LANES : cols], flow0_ref, tiles)


def own_scores_kernel(
    half, even_ref, odd_ref, pack_a_ref, pack_b_ref, off_ref, s_in, front_ref, pred_ref,
    s_s, flow_ref, ref_next, halo_next, halo_s, m_s, sem, next_sem, ref_sem,
):
    rows = odd_ref.shape[0] - 2 * REACH
    cols = 2 * half
    width = front_ref.shape[1]
    far = cols - width
    is_first = lax.axis_index("sec") == 0
    side_a, _ = sides(rows)
    half_a = jnp.where(side_a > 0, REACH, 0)
    half_b = REACH - half_a
    halos = [
        (pack_a_ref.at[:, 0:cols, :], halo_s.at[pl.ds(half_a, REACH), PAD : PAD + cols, :]),
        (pack_b_ref.at[:, 0:cols, :], halo_s.at[pl.ds(half_b, REACH), PAD : PAD + cols, :]),
    ]
    start_all(halos, sem)
    to = slice(PAD + far, PAD + cols)
    beyond = [
        (pack_a_ref.at[:, cols : cols + width, :], halo_next.at[pl.ds(half_a, REACH), to, :]),
        (pack_b_ref.at[:, cols : cols + width, :], halo_next.at[pl.ds(half_b, REACH), to, :]),
    ]
    start_all(beyond, next_sem)
    inside = ref_next.at[REACH : rows + REACH, PAD : PAD + width, :]
    before = [(pred_ref.at[:, 0:width, :], inside)]
    passed = [(front_ref, inside)]

    @pl.when(is_first)
    def _():
        start_all(before, ref_sem)

    @pl.when(jnp.logical_not(is_first))
    def _():
        start_all(passed, ref_sem)

    zero_sides(halo_s, cols)
    zero_sides(halo_next, cols)
    ref_next[:, PAD - EDGE : PAD, :] = jnp.zeros((rows + 2 * REACH, EDGE, LANES), BF16)
    wait_all(halos, sem)
    score_job(
        padded_query(odd_ref), padded_window(even_ref, halo_s), m_s, s_s, cols // LANES, 0,
        ((0, REACH), (rows - REACH, rows)),
    )
    flows_of(s_s, off_ref.at[1], flow_ref, cols // LANES)
    wait_all(beyond, next_sem)

    @pl.when(is_first)
    def _():
        wait_all(before, ref_sem)

    @pl.when(jnp.logical_not(is_first))
    def _():
        wait_all(passed, ref_sem)


def front_scores_kernel(
    half, even_ref, ref_in, front_a_ref, front_b_ref, pred_a_ref, pred_b_ref, off_ref, flow0_ref,
    ref_s, flow_ref, s_s, m_s, sem,
):
    rows = even_ref.shape[0] - 2 * REACH
    cols = 2 * half
    width = front_a_ref.shape[1]
    is_first = lax.axis_index("sec") == 0
    beyond_a, beyond_b = beyond_rows(rows)
    to_a = ref_s.at[pl.ds(beyond_a, REACH), PAD : PAD + width, :]
    to_b = ref_s.at[pl.ds(beyond_b, REACH), PAD : PAD + width, :]
    before = [(pred_a_ref.at[:, 0:width, :], to_a), (pred_b_ref.at[:, 0:width, :], to_b)]
    passed = [(front_a_ref, to_a), (front_b_ref, to_b)]

    @pl.when(is_first)
    def _():
        start_all(before, sem)
        wait_all(before, sem)

    @pl.when(jnp.logical_not(is_first))
    def _():
        start_all(passed, sem)
        wait_all(passed, sem)

    tiles = half // LANES
    score_job(padded_query(even_ref), padded_window(ref_s), m_s, s_s, tiles)
    flow_ref[:, :, half:cols] = flow0_ref[:, :, LANES:]
    flows_of(s_s, off_ref.at[0], flow_ref, tiles)


def pairs_out(pack_ref, at, tops, bottoms):
    for n, (top, bottom) in enumerate(zip(tops, bottoms)):
        pack_ref[at + 16 * n : at + 16 * n + 16, :] = jnp.concatenate([top, bottom], 0).astype(BF16)
    return at + 16 * len(tops)


def back_scores_kernel(
    half, back_ref, odd_ref, halo_ref, mask_ref, flow1_ref, flow_ref,
    flow2_ref, pack_ref, s_s, m_s,
):
    rows = odd_ref.shape[0] - 2 * REACH
    cols = 2 * half
    tile0 = half // LANES - 1
    tiles = cols // LANES - tile0
    width = (back_ref.shape[0] - 4 * rows * tiles) // rows
    far = cols - width

    def query_of(r, k, low):
        at = (k + tile0) * LANES + low - far + r * width
        return back_ref[pl.ds(pl.multiple_of(at, 16), LANES - low), :]

    score_job(query_of, padded_window(odd_ref, halo_ref, tile0), m_s, s_s, tiles, LANES - EDGE)

    def body(k, carry):
        lanes = pl.ds(pl.multiple_of(k * LANES, LANES), LANES)
        at = pl.multiple_of(k * 4 * rows + rows * width, 4 * rows)
        extra = back_ref[pl.ds(at, 4 * rows), :].astype(F32)
        fy, fx = flow_tile(s_s, extra[:rows], extra[rows : 2 * rows], lanes)
        flow2_ref[0, :, lanes] = fy
        flow2_ref[1, :, lanes] = fx
        flow2_ref[2, :, lanes] = extra[2 * rows : 3 * rows]
        return carry

    lax.fori_loop(0, tiles, body, 0)

    def tiles_of(ref, count):
        return [ref[:, n * LANES : (n + 1) * LANES] for n in range(count)]

    n = 0
    for ref, count in ((flow1_ref, cols // LANES), (flow_ref, cols // LANES), (flow2_ref, flow2_ref.shape[2] // LANES)):
        n = pairs_out(pack_ref, n, tiles_of(ref.at[0], count), tiles_of(ref.at[1], count))
    masks = []
    for ref, count in ((mask_ref.at[1], cols // LANES), (mask_ref.at[0], cols // LANES), (flow2_ref.at[2], flow2_ref.shape[2] // LANES)):
        masks += [m.astype(F32) for m in tiles_of(ref, count)]
    if len(masks) % 2:
        masks.append(masks[-1])
    pairs_out(pack_ref, n, masks[0::2], masks[1::2])


def relax_kernel(
    half, pack_a_ref, pack_b_ref, flow1_ref, flow3_ref, flow2_ref, mask_ref, f1_ref, f3_ref, msg_ref,
    field_s, pull_s, keep_s,
):
    rows, cols = flow1_ref.shape[1:]
    deep = rows + 2 * ITERS
    place = lax.axis_index("tile")
    count = lax.axis_size("tile")
    glob = place * rows + lax.broadcasted_iota(jnp.int32, (deep, LANES), 0) - ITERS
    a_below = lax.rem(place, 2) == 0
    inside = ((glob >= 0) & (glob < rows * count)).astype(F32)
    widths = (cols, cols, flow2_ref.shape[2])
    tiles = [w // LANES for w in widths]
    flows = (flow1_ref, flow3_ref, flow2_ref)
    own_masks = (mask_ref.at[1], mask_ref.at[0], flow2_ref.at[2])
    starts = [0, tiles[0], tiles[0] + tiles[1]]
    mask_at = 16 * sum(tiles)
    for job in range(3):
        for k in range(tiles[job]):
            lanes = slice(k * LANES, (k + 1) * LANES)
            at = 16 * (starts[job] + k)
            m_at = mask_at + 8 * (starts[job] + k)
            half_at = m_at // 16 * 16
            sub = slice(m_at - half_at, m_at - half_at + 8)
            side_a = pack_a_ref[at : at + 16, :].astype(F32)
            side_b = pack_b_ref[at : at + 16, :].astype(F32)
            m_a = pack_a_ref[half_at : half_at + 16, :].astype(F32)[sub]
            m_b = pack_b_ref[half_at : half_at + 16, :].astype(F32)[sub]
            upper, lower = jnp.where(a_below, side_b, side_a), jnp.where(a_below, side_a, side_b)
            m_up, m_down = jnp.where(a_below, m_b, m_a), jnp.where(a_below, m_a, m_b)
            weight = stiffness * jnp.concatenate(
                [m_up, own_masks[job][:, lanes].astype(F32), m_down], 0
            )
            keep_s[job, :, lanes] = (step_size - step_size * weight) * inside
            for c in range(2):
                flow = jnp.concatenate(
                    [upper[8 * c : 8 * c + 8], flows[job][c, :, lanes], lower[8 * c : 8 * c + 8]], 0
                )
                pull = step_size * weight * flow * inside
                pull_s[job, c, :, lanes] = pull
                field_s[job, c, :, lanes] = pull
    step = step_size * inside

    def body(n, carry):
        for job in range(3):
            for c in range(2):
                old = [field_s[job, c, :, k * LANES : (k + 1) * LANES] for k in range(tiles[job])]
                lane = lax.broadcasted_iota(jnp.int32, (deep, LANES), 1)
                nxt = [pltpu.roll(x, LANES - 1, 1) for x in old]
                prv = [pltpu.roll(x, 1, 1) for x in old]
                zero = jnp.zeros_like(old[0])
                for k in range(tiles[job]):
                    lanes = slice(k * LANES, (k + 1) * LANES)
                    right = jnp.where(lane == LANES - 1, nxt[k + 1] if k + 1 < tiles[job] else zero, nxt[k])
                    left = jnp.where(lane == 0, prv[k - 1] if k else zero, prv[k])
                    around = pltpu.roll(old[k], 1, 0) + pltpu.roll(old[k], deep - 1, 0) + left + right
                    field_s[job, c, :, lanes] = (
                        keep_s[job, :, lanes] * old[k] + step * around + pull_s[job, c, :, lanes]
                    )
        return carry

    lax.fori_loop(0, ITERS - 1, body, 0)
    is_first = lax.axis_index("sec") == 0
    seam = half - EDGE // 2
    mine = slice(ITERS, ITERS + rows)
    lead = half - LANES
    for c in range(2):
        for k in range(tiles[0]):
            lanes = slice(k * LANES, (k + 1) * LANES)
            col = lax.broadcasted_iota(jnp.int32, (rows, LANES), 1) + k * LANES
            one = field_s[0, c, mine, lanes]
            front = field_s[1, c, mine, lanes]
            if (k + 1) * LANES > seam:
                front = jnp.where((col < seam) | is_first, front, 0.0)
            total = one + front
            if k * LANES >= lead:
                back = field_s[2, c, mine, k * LANES - lead : (k + 1) * LANES - lead]
                total = total + jnp.where(col >= seam, back, 0.0)
            f1_ref[c, :, lanes] = one
            f3_ref[c, :, lanes] = front
            msg_ref[c, :, lanes] = total.astype(msg_ref.dtype)


def shards(pixels, pred, offsets, mask, base_shift, w_hidden, w_feature, feat_gain):
    secs, rows, cols, patch = pixels.shape
    hid, feat = w_feature.shape
    assert secs == 2 and rows == ITERS and feat == LANES and cols % (2 * LANES) == 0
    half = cols // 2
    width = half + 2 * EDGE
    span = half + LANES
    deep = rows + 2 * REACH
    tail = 4 * rows * (span // LANES)
    full = cols + 2 * PAD
    gain = feat_gain.reshape(1, feat)
    shape = jax.ShapeDtypeStruct
    padded = shape((deep, full, feat), BF16)
    pre = pltpu.VMEM((2, 2 * width, feat), F32)

    dma = pltpu.SemaphoreType.DMA

    def call(kernel, ins, in_specs, outs, scratch, cost, limit, aliases=None):
        return pl.pallas_call(
            functools.partial(kernel, half),
            out_shape=outs,
            in_specs=in_specs,
            out_specs=tuple(VMEM for _ in outs),
            scratch_shapes=scratch,
            input_output_aliases=aliases or {},
            compiler_params=params(limit),
            cost_estimate=cost,
        )(*ins)

    def encode_cost(kind):
        return flops_of(len(pieces_of(kind, rows, 0)) * width, patch, hid, feat)

    def in_place(value):
        return pltpu.with_memory_space_constraint(value, pltpu.HBM)

    edges = shape((REACH, cols, feat), BF16)
    front, odd, wh, wf, gain, pred_a, pred_b = call(
        encode_front_kernel,
        (in_place(pixels), in_place(w_hidden), in_place(w_feature), in_place(gain), in_place(pred)), [HBM] * 5,
        (
            shape((rows, width, feat), BF16), padded,
            shape(w_hidden.shape, BF16), shape(w_feature.shape, BF16), shape(gain.shape, F32), edges, edges,
        ),
        [pltpu.VMEM((rows, width, patch), BF16), pre, dma((rows,)), dma((5,))],
        encode_cost("front"), 12,
    )
    weights = (pixels, wh, wf, gain)
    front_in = hop(front, "sec", 1)
    pred_a = swap(pred_a, 0, True)
    pred_b = swap(pred_b, 1, True)
    pack = shape((REACH, cols + width, feat), BF16)
    odd, even, back, pack_a, pack_b = call(
        encode_border_kernel,
        (*weights, odd, offsets, mask), [VMEM] * 7,
        (padded, padded, shape((rows * width + tail, feat), BF16), pack, pack),
        [pre], flops_of(6 * REACH * width, patch, hid, feat), 10, {4: 0},
    )
    pack_b = swap(pack_b, 1)
    pack_a = swap(pack_a, 0)
    even, back = call(
        encode_back_kernel, (*weights, even, back), [VMEM] * 6,
        (padded, shape(back.shape, BF16)), [pre], encode_cost("back"), 10, {4: 0, 5: 1},
    )
    back_in = hop(back, "sec", -1)
    odd, even = call(
        encode_inner_kernel, (*weights, odd, even), [VMEM] * 6,
        (padded, padded), [pre], encode_cost("inner"), 10, {4: 0, 5: 1},
    )

    bands = SEG * (2 * REACH + 1)
    nodes = rows * cols

    def score_cost(part):
        return pl.CostEstimate(
            flops=int(part * nodes * 2560 * LANES), bytes_accessed=int(part * nodes * 512), transcendentals=0
        )

    halo = pltpu.VMEM((2 * REACH, full, feat), BF16)
    turning = pltpu.VMEM((2, rows, LANES, LANES), F32)
    turning4 = pltpu.VMEM((4, rows, LANES, LANES), F32)
    whole = pltpu.VMEM((deep, full, feat), BF16)
    flow0_shape = shape((2, rows, span), F32)
    scores, flow0 = call(
        near_scores_kernel, (even, odd, in_place(pred), pred_a, pred_b, offsets),
        [VMEM] * 2 + [HBM] + [VMEM] * 3, (shape((rows, bands, cols), F32), flow0_shape),
        [whole, pltpu.VMEM((rows, bands, span), F32), turning4, dma((3,))], score_cost(0.5), 18,
    )
    edge = shape((REACH, width, feat), BF16)
    front_a, front_b = call(
        pick_kernel, (front_in,), [VMEM], (edge, edge), [],
        pl.CostEstimate(flops=0, bytes_accessed=8 * REACH * width * feat, transcendentals=0), 4,
    )
    front_b = swap(front_b, 1)
    front_a = swap(front_a, 0)
    ref_shape = shape((deep, half + 3 * PAD, feat), BF16)
    _, flow1, ref, beyond = call(
        own_scores_kernel, (even, odd, pack_a, pack_b, offsets, scores, front_in, in_place(pred)),
        [VMEM] * 7 + [HBM],
        (shape(scores.shape, F32), shape((2, rows, cols), F32), ref_shape, shape((2 * REACH, full, feat), BF16)),
        [halo, turning4, dma((2,)), dma((2,)), dma((1,))], score_cost(0.5), 14, {5: 0},
    )
    _, flow3 = call(
        front_scores_kernel, (even, ref, front_a, front_b, pred_a, pred_b, offsets, flow0),
        [VMEM] * 8, (ref_shape, shape((2, rows, cols), F32)),
        [pltpu.VMEM((rows, bands, half), F32), turning, dma((2,))], score_cost(0.5), 12, {1: 0},
    )

    tiles = 2 * (cols // LANES) + span // LANES
    pack_rows = 16 * tiles + 16 * ((tiles + 1) // 2)
    flow2, pack = call(
        back_scores_kernel, (back_in, odd, beyond, mask, flow1, flow3), [VMEM] * 6,
        (shape((3, rows, span), F32), shape((pack_rows, LANES), BF16)),
        [pltpu.VMEM((rows, bands, span), F32), turning], score_cost(0.55), 12,
    )
    flows_b = swap(pack, 1)
    flows_a = swap(pack, 0)

    wide = rows + 2 * ITERS
    f1, f3, msg = pl.pallas_call(
        functools.partial(relax_kernel, half),
        out_shape=(shape((2, rows, cols), F32), shape((2, rows, cols), F32), shape((2, rows, cols), BF16)),
        in_specs=[VMEM] * 6,
        out_specs=(VMEM,) * 3,
        scratch_shapes=[
            pltpu.VMEM((3, 2, wide, cols), F32),
            pltpu.VMEM((3, 2, wide, cols), F32),
            pltpu.VMEM((3, wide, cols), F32),
        ],
        compiler_params=params(12),
        cost_estimate=pl.CostEstimate(flops=nodes * 24 * 12 * 8, bytes_accessed=nodes * 40, transcendentals=0),
        name="relax",
    )(flows_a, flows_b, flow1, flow3, flow2, mask)

    prefix = base_shift
    for steps in range(1, lax.axis_size("sec")):
        prefix = prefix + hop(msg, "sec", steps).astype(F32)
    first = prefix + f3
    return jnp.stack([first, first + f1], axis=0)


def solution(mesh):
    in_specs = (
        P("sec", "tile", None, None),
        P("tile", None, None),
        P("sec", None, "tile", None),
        P("sec", "tile", None),
        P(None, "tile", None),
        P(),
        P(),
        P(),
    )
    out_specs = P("sec", None, "tile", None)
    return jax.shard_map(shards, mesh=mesh, in_specs=in_specs, out_specs=out_specs, check_vma=False)
```

```python
import functools

import jax
import jax.numpy as jnp
from jax import lax
from jax.experimental import pallas as pl
from jax.experimental.pallas import tpu as pltpu
from jax.sharding import PartitionSpec as P


ITERS = 8
REACH = 2
LANES = 128
BASE = 16
PAD = LANES
SEG = 16
EDGE = 16

epsilon = 1e-05
step_size = 0.2
stiffness = 0.5

F32 = jnp.float32
BF16 = jnp.bfloat16
HBM = pl.BlockSpec(memory_space=pltpu.HBM)
VMEM = pl.BlockSpec(memory_space=pltpu.VMEM)


def hop(value, axis, steps):
    count = lax.axis_size(axis)
    pairs = [(i, i + steps) for i in range(count) if 0 <= i + steps < count]
    return lax.ppermute(value, axis, pairs)


def swap(value, first, plane=False):
    tiles = lax.axis_size("tile")
    stride = lax.axis_size("sec") if plane else 1
    pairs = []
    for i in range(first, tiles - 1, 2):
        pairs += [(i * stride, (i + 1) * stride), ((i + 1) * stride, i * stride)]
    return lax.ppermute(value, ("tile", "sec") if plane else "tile", pairs)


def sides(rows):
    last = rows - REACH
    facing = jnp.where(lax.rem(lax.axis_index("tile"), 2) == 0, last, 0)
    return facing, last - facing


def params(limit):
    return pltpu.CompilerParams(vmem_limit_bytes=limit * 1024 * 1024)


def matmuls(pix, wh, wf):
    hidden = jnp.maximum(jnp.dot(pix, wh, preferred_element_type=F32), 0.0).astype(BF16)
    return jnp.dot(hidden, wf, preferred_element_type=F32)


def normed(pre, gain):
    mean = jnp.mean(pre * pre, axis=-1, keepdims=True)
    return (pre * lax.rsqrt(mean + epsilon) * gain).astype(BF16)


def encode_steps(pix_of, count, width, store, wh_ref, wf_ref, gain_ref, pre_s):
    steps = count // 2

    def finish(n):
        value = normed(pre_s[n % 2], gain_ref[...])
        store(2 * n, value[:width])
        store(2 * n + 1, value[width:])

    for n in range(steps):
        pre_s[n % 2] = matmuls(pix_of(2 * n), wh_ref[...], wf_ref[...])
        if n:
            finish(n - 1)
    finish(steps - 1)


def inner_rows(rows):
    return list(range(REACH, rows - REACH))


def pieces_of(kind, rows, far):
    inner = inner_rows(rows)
    if kind == "front":
        return [(1, r, 0) for r in range(rows)]
    return [(0, r, 0) for r in inner] + [(1, r, far) for r in inner]


def pixel_pair(pix_ref, pieces, n, width):
    rows = [pix_ref[sec, row, col0 : col0 + width, :] for sec, row, col0 in pieces[n : n + 2]]
    return jnp.concatenate(rows, 0)


def zero_sides(ref, cols):
    side = jnp.zeros((ref.shape[0], EDGE, ref.shape[2]), BF16)
    ref[:, PAD - EDGE : PAD, :] = side
    ref[:, PAD + cols : PAD + cols + EDGE, :] = side


def put_left(ref, row, value, half):
    ref[row + REACH, PAD : PAD + half, :] = value[:half]


def put_right(ref, row, value, half):
    ref[row + REACH, PAD + half : PAD + 2 * half, :] = value[value.shape[0] - half :]


def encode_front_kernel(
    half, pix_ref, wh_in, wf_in, gain_in, pred_ref,
    front_ref, odd_ref, wh_ref, wf_ref, gain_ref, pred_a_ref, pred_b_ref,
    pix_s, pre_s, sem, more_sem,
):
    rows, cols = pix_ref.shape[1:3]
    width = pix_s.shape[1]
    lean = front_ref.shape[1]
    pieces = pieces_of("front", rows, cols - width)
    loads = [
        (pix_ref.at[sec, row, col0 : col0 + width, :], pix_s.at[n])
        for n, (sec, row, col0) in enumerate(pieces)
    ]
    copies = copies_of(loads, sem)
    constants = copies_of([(wh_in, wh_ref), (wf_in, wf_ref), (gain_in, gain_ref)], more_sem)
    side_a, side_b = sides(rows)
    edges = [(pred_ref.at[pl.ds(side_a, REACH)], pred_a_ref), (pred_ref.at[pl.ds(side_b, REACH)], pred_b_ref)]
    edge_sem = more_sem.at[len(constants) :]
    is_first = lax.axis_index("sec") == 0
    for copy in copies[:2] + constants + copies[2:4]:
        copy.start()

    @pl.when(is_first)
    def _():
        start_all(edges, edge_sem)

    zero_sides(odd_ref, cols)
    for copy in constants:
        copy.wait()

    def pix_of(n):
        for copy in copies[n + 4 : n + 6]:
            copy.start()
        copies[n].wait()
        copies[n + 1].wait()
        return pix_s[n : n + 2].reshape(2 * width, pix_s.shape[2])

    def store(n, value):
        front_ref[n] = value[:lean]
        put_left(odd_ref, n, value, half)

    encode_steps(pix_of, len(pieces), width, store, wh_ref, wf_ref, gain_ref, pre_s)

    @pl.when(is_first)
    def _():
        wait_all(edges, edge_sem)


def encode_border_kernel(
    half, pix_ref, wh_ref, wf_ref, gain_ref, odd_in, off_ref, mask_ref,
    odd_ref, even_ref, back_ref, pack_a_ref, pack_b_ref, pre_s,
):
    rows, cols = pix_ref.shape[1:3]
    width = pack_a_ref.shape[1] - cols
    side_a, side_b = sides(rows)
    border = [side_a + r for r in range(REACH)] + [side_b + r for r in range(REACH)]
    far = cols - width
    lean = width - EDGE
    inner = inner_rows(rows)
    pieces = [(0, r, far) for r in border] + [(0, r, 0) for r in border] + [(1, r, far) for r in border]
    pieces += [(0, r, far) for r in inner]
    zero_sides(even_ref, cols)
    first = half // LANES - 1
    for tile in range(cols // LANES - first):
        lanes = slice((first + tile) * LANES, (first + tile + 1) * LANES)
        extra = jnp.concatenate(
            [off_ref[0, 0, :, lanes], off_ref[0, 1, :, lanes], mask_ref[0, :, lanes], mask_ref[0, :, lanes]], 0
        )
        at = rows * lean + tile * 4 * rows
        back_ref[at : at + 4 * rows, :] = extra.astype(F32).astype(BF16)

    def store(n, value):
        part, m = divmod(n, len(border))
        row = border[m] if part < 3 else inner[n - 3 * len(border)]
        pack = pack_a_ref if m < REACH else pack_b_ref
        if part == 0 or part > 2:
            back_ref[pl.ds(pl.multiple_of(row * lean, 16), lean), :] = value[EDGE:]
        if part > 2:
            put_right(even_ref, row, value, half)
        elif part == 0:
            put_right(even_ref, row, value, half)
            pack[m % REACH, half:cols, :] = value[width - half :]
        elif part == 1:
            put_left(even_ref, row, value, half)
            pack[m % REACH, 0:half, :] = value[:half]
        else:
            put_right(odd_ref, row, value, half)
            pack[m % REACH, cols : cols + width, :] = value

    encode_steps(
        lambda n: pixel_pair(pix_ref, pieces, n, width), len(pieces), width, store, wh_ref, wf_ref, gain_ref, pre_s
    )


def encode_inner_kernel(half, pix_ref, wh_ref, wf_ref, gain_ref, odd_in, even_in, odd_ref, even_ref, pre_s):
    rows, cols = pix_ref.shape[1:3]
    width = pre_s.shape[1] // 2
    inner = inner_rows(rows)
    pieces = pieces_of("inner", rows, cols - width)

    def store(n, value):
        part, m = divmod(n, len(inner))
        if part == 0:
            put_left(even_ref, inner[m], value, half)
        else:
            put_right(odd_ref, inner[m], value, half)

    encode_steps(
        lambda n: pixel_pair(pix_ref, pieces, n, width), len(pieces), width, store, wh_ref, wf_ref, gain_ref, pre_s
    )


def flops_of(nodes, patch, hid, feat):
    return pl.CostEstimate(
        flops=2 * nodes * hid * (patch + feat), bytes_accessed=nodes * 2 * (patch + feat), transcendentals=nodes
    )


def align(band, first, lift, row):
    band = pltpu.roll(band, (2 * LANES - first - BASE + 2 + lift) % LANES, 1)
    return jnp.where((row & 4) != 0, pltpu.roll(band, LANES - 4, 1), band)


def settle(band, row):
    for shift in (2, 1):
        band = jnp.where((row & shift) != 0, pltpu.roll(band, LANES - shift, 1), band)
    return band


def score_columns(query_of, window_of, rows, m_s, s_s, k, low):
    span = 2 * REACH + 1
    tall = LANES - low
    lane = lax.broadcasted_iota(jnp.int32, (8, LANES), 1)
    for rp in range(rows[0], rows[1] + 2 * REACH):
        j = rp % span
        window = window_of(rp, k, SEG * j)
        first = max(rp - 2 * REACH, rows[0])
        last = min(rp, rows[1] - 1)
        parts = [query_of(r, k, low) for r in range(first, last + 1)]
        query = jnp.concatenate(parts, 0) if len(parts) > 1 else parts[0]
        product = lax.dot_general(
            query, window, (((1,), (1,)), ((), ())), preferred_element_type=F32
        )
        for r in range(first, last + 1):
            for i in range(low // 8, LANES // 8):
                at = (r - first) * tall + 8 * i - low
                s = 8 * i + BASE - 4 + SEG * j
                near = product[at : at + 8, :LANES]
                far = product[at : at + 8, LANES:]
                if s + SEG <= LANES:
                    value, mask = near, (lane >= s) & (lane < s + SEG)
                elif s >= LANES:
                    value, mask = far, (lane >= s - LANES) & (lane < s + SEG - LANES)
                else:
                    value = jnp.where(lane >= s, near, far)
                    mask = (lane >= s) | (lane < s + SEG - LANES)
                dst = m_s.at[r, 8 * i : 8 * i + 8, :]
                if rp == r:
                    dst[...] = value
                else:
                    pltpu.store(dst, value, mask=mask)
        if rp > rows[0] + 2 * REACH and rp % 2:
            score_turn(m_s, s_s, rp - 2 * REACH - 1, k, low)


def score_turn(m_s, s_s, r, k, low):
    span = 2 * REACH + 1
    lane = lax.broadcasted_iota(jnp.int32, (8, LANES), 1)
    row = lax.broadcasted_iota(jnp.int32, (8, LANES), 0)
    groups = [jnp.zeros((8, LANES), F32)] * (low // 8)
    for i in range(low // 8, LANES // 8):
        one = align(m_s[r, 8 * i : 8 * i + 8, :], 8 * i, 0, row)
        two = align(m_s[r + 1, 8 * i : 8 * i + 8, :], 8 * i, 8, row)
        groups.append(settle(jnp.where((lane & 8) != 0, two, one), row))
    turned = jnp.concatenate(groups, 0).T
    lanes = pl.ds(pl.multiple_of(k * LANES, LANES), LANES)
    for n in range(2):
        for j in range(span):
            a = (j - r - n) % span
            at = SEG * j + 8 * n
            s_s[r + n, SEG * a : SEG * a + 8, lanes] = turned[at : at + 8]


def score_job(query_of, window_of, m_s, s_s, tiles, low=0, blocks=None):
    blocks = blocks or ((0, s_s.shape[0]),)
    first = 1 if low else 0

    def columns(m, k, low):
        for rows in blocks:
            score_columns(query_of, window_of, rows, m_s.at[m], s_s, k, low)

    if low:
        columns(0, 0, low)
    step = m_s.shape[0]
    whole, odd = (tiles - first) // step, (tiles - first) % step

    def body(n, carry):
        for m in range(step):
            columns(m, step * n + m + first, 0)
        return carry

    lax.fori_loop(0, whole, body, 0)
    for m in range(odd):
        columns(m, tiles - odd + m, 0)


def padded_query(ref, tile0=0):
    def query_of(r, k, low):
        at = pl.multiple_of((k + tile0) * LANES + PAD + low, 16)
        return ref[r + REACH, pl.ds(at, LANES - low), :]

    return query_of


def padded_window(ref, halo=None, tile0=0):
    rows = ref.shape[0] - 2 * REACH

    def window_of(rp, k, shift):
        at = pl.multiple_of((k + tile0) * LANES + (PAD - BASE) - shift, 16)
        if halo is not None and rp < REACH:
            return halo[rp, pl.ds(at, 2 * LANES), :]
        if halo is not None and rp >= rows + REACH:
            return halo[rp - rows, pl.ds(at, 2 * LANES), :]
        return ref[rp, pl.ds(at, 2 * LANES), :]

    return window_of


def flow_tile(s_s, oy, ox, lanes):
    y_low, y_high, x_low, x_high = oy < 0, oy > 0, ox < 0, ox > 0
    feat = F32(1.0 / LANES)
    by_row = {}
    for i in range(3):
        for b in range(5):
            v = [s_s[:, SEG * (i + d) + b, lanes] for d in range(3)]
            by_row[i, b] = jnp.where(y_low, v[0], jnp.where(y_high, v[2], v[1]))
    total = jnp.ones_like(oy)
    sum_y = jnp.zeros_like(oy)
    sum_x = jnp.zeros_like(oy)
    for i in range(3):
        for j in range(3):
            near = jnp.where(
                x_low, by_row[i, j], jnp.where(x_high, by_row[i, j + 2], by_row[i, j + 1])
            )
            near = near * feat
            weight = near * near
            total = total + weight
            if i != 1:
                sum_y = sum_y + weight * (i - 1)
            if j != 1:
                sum_x = sum_x + weight * (j - 1)
    return oy + sum_y / total, ox + sum_x / total


def flows_of(s_s, off_ref, flow_ref, tiles):
    def body(k, carry):
        lanes = pl.ds(pl.multiple_of(k * LANES, LANES), LANES)
        fy, fx = flow_tile(s_s, off_ref[0, :, lanes].astype(F32), off_ref[1, :, lanes].astype(F32), lanes)
        flow_ref[0, :, lanes] = fy
        flow_ref[1, :, lanes] = fx
        return carry

    lax.fori_loop(0, tiles, body, 0)


def copies_of(pairs, sem):
    return [pltpu.make_async_copy(src, dst, sem.at[n]) for n, (src, dst) in enumerate(pairs)]


def start_all(pairs, sem):
    for copy in copies_of(pairs, sem):
        copy.start()


def wait_all(pairs, sem):
    for copy in copies_of(pairs, sem):
        copy.wait()


def pick_kernel(half, front_ref, a_ref, b_ref):
    side_a, side_b = sides(front_ref.shape[0])
    for r in range(REACH):
        a_ref[r] = front_ref[side_a + r]
        b_ref[r] = front_ref[side_b + r]


def beyond_rows(rows):
    side_a, side_b = sides(rows)
    below = rows + REACH
    return jnp.where(side_a > 0, below, 0), jnp.where(side_b > 0, below, 0)


def near_scores_kernel(
    half, even_ref, odd_ref, pred_ref, pred_a_ref, pred_b_ref, off_ref,
    s_s, flow0_ref, ref0_s, s0_s, m_s, sem,
):
    rows = odd_ref.shape[0] - 2 * REACH
    cols = 2 * half
    far = half - 2 * EDGE
    is_first = lax.axis_index("sec") == 0
    tile0 = half // LANES - 1
    tiles = cols // LANES - tile0
    to = slice(PAD + far, PAD + cols)
    beyond_a, beyond_b = beyond_rows(rows)
    before = [
        (pred_ref.at[:, far:cols, :], ref0_s.at[REACH : rows + REACH, to, :]),
        (pred_a_ref.at[:, far:cols, :], ref0_s.at[pl.ds(beyond_a, REACH), to, :]),
        (pred_b_ref.at[:, far:cols, :], ref0_s.at[pl.ds(beyond_b, REACH), to, :]),
    ]

    @pl.when(is_first)
    def _():
        start_all(before, sem)

    flow0_ref[...] = jnp.zeros_like(flow0_ref)
    score_job(
        padded_query(odd_ref), padded_window(even_ref), m_s, s_s, cols // LANES, 0, ((REACH, rows - REACH),)
    )

    @pl.when(is_first)
    def _():
        zero_sides(ref0_s, cols)
        wait_all(before, sem)
        score_job(
            padded_query(even_ref, tile0), padded_window(ref0_s, None, tile0), m_s, s0_s, tiles, LANES - EDGE
        )
        flows_of(s0_s, off_ref.at[0, :, :, tile0 * LANES : cols], flow0_ref, tiles)


def own_scores_kernel(
    half, even_ref, odd_ref, pack_a_ref, pack_b_ref, off_ref, s_in, front_ref, pred_ref,
    s_s, flow_ref, ref_next, halo_next, halo_s, m_s, sem, next_sem, ref_sem,
):
    rows = odd_ref.shape[0] - 2 * REACH
    cols = 2 * half
    width = pack_a_ref.shape[1] - cols
    lean = front_ref.shape[1]
    far = cols - width
    is_first = lax.axis_index("sec") == 0
    side_a, _ = sides(rows)
    half_a = jnp.where(side_a > 0, REACH, 0)
    half_b = REACH - half_a
    halos = [
        (pack_a_ref.at[:, 0:cols, :], halo_s.at[pl.ds(half_a, REACH), PAD : PAD + cols, :]),
        (pack_b_ref.at[:, 0:cols, :], halo_s.at[pl.ds(half_b, REACH), PAD : PAD + cols, :]),
    ]
    start_all(halos, sem)
    to = slice(PAD + far, PAD + cols)
    beyond = [
        (pack_a_ref.at[:, cols : cols + width, :], halo_next.at[pl.ds(half_a, REACH), to, :]),
        (pack_b_ref.at[:, cols : cols + width, :], halo_next.at[pl.ds(half_b, REACH), to, :]),
    ]
    start_all(beyond, next_sem)
    left = slice(PAD, PAD + lean)
    inside = ref_next.at[REACH : rows + REACH, left, :]
    before = [(pred_ref.at[:, 0:lean, :], inside)]
    passed = [(front_ref, inside)]

    @pl.when(is_first)
    def _():
        start_all(before, ref_sem)

    @pl.when(jnp.logical_not(is_first))
    def _():
        start_all(passed, ref_sem)

    zero_sides(halo_s, cols)
    zero_sides(halo_next, cols)
    ref_next[:, PAD - EDGE : PAD, :] = jnp.zeros((rows + 2 * REACH, EDGE, LANES), BF16)
    wait_all(halos, sem)
    score_job(
        padded_query(odd_ref), padded_window(even_ref, halo_s), m_s, s_s, cols // LANES, 0,
        ((0, REACH), (rows - REACH, rows)),
    )
    flows_of(s_s, off_ref.at[1], flow_ref, cols // LANES)
    wait_all(beyond, next_sem)

    @pl.when(is_first)
    def _():
        wait_all(before, ref_sem)

    @pl.when(jnp.logical_not(is_first))
    def _():
        wait_all(passed, ref_sem)


def front_scores_kernel(
    half, even_ref, ref_in, front_a_ref, front_b_ref, pred_a_ref, pred_b_ref, off_ref, flow0_ref,
    ref_s, flow_ref, s_s, m_s, sem,
):
    rows = even_ref.shape[0] - 2 * REACH
    cols = 2 * half
    width = front_a_ref.shape[1]
    is_first = lax.axis_index("sec") == 0
    beyond_a, beyond_b = beyond_rows(rows)
    to_a = ref_s.at[pl.ds(beyond_a, REACH), PAD : PAD + width, :]
    to_b = ref_s.at[pl.ds(beyond_b, REACH), PAD : PAD + width, :]
    before = [(pred_a_ref.at[:, 0:width, :], to_a), (pred_b_ref.at[:, 0:width, :], to_b)]
    passed = [(front_a_ref, to_a), (front_b_ref, to_b)]

    @pl.when(is_first)
    def _():
        start_all(before, sem)
        wait_all(before, sem)

    @pl.when(jnp.logical_not(is_first))
    def _():
        start_all(passed, sem)
        wait_all(passed, sem)

    tiles = half // LANES
    score_job(padded_query(even_ref), padded_window(ref_s), m_s, s_s, tiles)
    flow_ref[:, :, half:cols] = flow0_ref[:, :, LANES:]
    flows_of(s_s, off_ref.at[0], flow_ref, tiles)


def pairs_out(pack_ref, at, tops, bottoms):
    for n, (top, bottom) in enumerate(zip(tops, bottoms)):
        pack_ref[at + 16 * n : at + 16 * n + 16, :] = jnp.concatenate([top, bottom], 0).astype(BF16)
    return at + 16 * len(tops)


def back_scores_kernel(
    half, back_ref, odd_ref, halo_ref, mask_ref, flow1_ref, flow_ref,
    flow2_ref, pack_ref, s_s, m_s,
):
    rows = odd_ref.shape[0] - 2 * REACH
    cols = 2 * half
    tile0 = half // LANES - 1
    tiles = cols // LANES - tile0
    width = (back_ref.shape[0] - 4 * rows * tiles) // rows
    far = cols - width

    def query_of(r, k, low):
        at = (k + tile0) * LANES + low - far + r * width
        return back_ref[pl.ds(pl.multiple_of(at, 16), LANES - low), :]

    score_job(query_of, padded_window(odd_ref, halo_ref, tile0), m_s, s_s, tiles, LANES - EDGE)

    def body(k, carry):
        lanes = pl.ds(pl.multiple_of(k * LANES, LANES), LANES)
        at = pl.multiple_of(k * 4 * rows + rows * width, 4 * rows)
        extra = back_ref[pl.ds(at, 4 * rows), :].astype(F32)
        fy, fx = flow_tile(s_s, extra[:rows], extra[rows : 2 * rows], lanes)
        flow2_ref[0, :, lanes] = fy
        flow2_ref[1, :, lanes] = fx
        flow2_ref[2, :, lanes] = extra[2 * rows : 3 * rows]
        return carry

    lax.fori_loop(0, tiles, body, 0)

    def tiles_of(ref, count):
        return [ref[:, n * LANES : (n + 1) * LANES] for n in range(count)]

    n = 0
    for ref, count in ((flow1_ref, cols // LANES), (flow_ref, cols // LANES), (flow2_ref, flow2_ref.shape[2] // LANES)):
        n = pairs_out(pack_ref, n, tiles_of(ref.at[0], count), tiles_of(ref.at[1], count))
    masks = []
    for ref, count in ((mask_ref.at[1], cols // LANES), (mask_ref.at[0], cols // LANES), (flow2_ref.at[2], flow2_ref.shape[2] // LANES)):
        masks += [m.astype(F32) for m in tiles_of(ref, count)]
    if len(masks) % 2:
        masks.append(masks[-1])
    pairs_out(pack_ref, n, masks[0::2], masks[1::2])


def relax_kernel(
    half, pack_a_ref, pack_b_ref, flow1_ref, flow3_ref, flow2_ref, mask_ref, f1_ref, f3_ref, msg_ref,
    field_s, pull_s, keep_s,
):
    rows, cols = flow1_ref.shape[1:]
    deep = rows + 2 * ITERS
    place = lax.axis_index("tile")
    count = lax.axis_size("tile")
    glob = place * rows + lax.broadcasted_iota(jnp.int32, (deep, LANES), 0) - ITERS
    a_below = lax.rem(place, 2) == 0
    inside = ((glob >= 0) & (glob < rows * count)).astype(F32)
    widths = (cols, cols, flow2_ref.shape[2])
    tiles = [w // LANES for w in widths]
    flows = (flow1_ref, flow3_ref, flow2_ref)
    own_masks = (mask_ref.at[1], mask_ref.at[0], flow2_ref.at[2])
    starts = [0, tiles[0], tiles[0] + tiles[1]]
    mask_at = 16 * sum(tiles)
    for job in range(3):
        for k in range(tiles[job]):
            lanes = slice(k * LANES, (k + 1) * LANES)
            at = 16 * (starts[job] + k)
            m_at = mask_at + 8 * (starts[job] + k)
            half_at = m_at // 16 * 16
            sub = slice(m_at - half_at, m_at - half_at + 8)
            side_a = pack_a_ref[at : at + 16, :].astype(F32)
            side_b = pack_b_ref[at : at + 16, :].astype(F32)
            m_a = pack_a_ref[half_at : half_at + 16, :].astype(F32)[sub]
            m_b = pack_b_ref[half_at : half_at + 16, :].astype(F32)[sub]
            upper, lower = jnp.where(a_below, side_b, side_a), jnp.where(a_below, side_a, side_b)
            m_up, m_down = jnp.where(a_below, m_b, m_a), jnp.where(a_below, m_a, m_b)
            weight = stiffness * jnp.concatenate(
                [m_up, own_masks[job][:, lanes].astype(F32), m_down], 0
            )
            keep_s[job, :, lanes] = (step_size - step_size * weight) * inside
            for c in range(2):
                flow = jnp.concatenate(
                    [upper[8 * c : 8 * c + 8], flows[job][c, :, lanes], lower[8 * c : 8 * c + 8]], 0
                )
                pull = step_size * weight * flow * inside
                pull_s[job, c, :, lanes] = pull
                field_s[job, c, :, lanes] = pull
    step = step_size * inside

    def body(n, carry):
        for job in range(3):
            for c in range(2):
                old = [field_s[job, c, :, k * LANES : (k + 1) * LANES] for k in range(tiles[job])]
                lane = lax.broadcasted_iota(jnp.int32, (deep, LANES), 1)
                nxt = [pltpu.roll(x, LANES - 1, 1) for x in old]
                prv = [pltpu.roll(x, 1, 1) for x in old]
                zero = jnp.zeros_like(old[0])
                for k in range(tiles[job]):
                    lanes = slice(k * LANES, (k + 1) * LANES)
                    right = jnp.where(lane == LANES - 1, nxt[k + 1] if k + 1 < tiles[job] else zero, nxt[k])
                    left = jnp.where(lane == 0, prv[k - 1] if k else zero, prv[k])
                    around = pltpu.roll(old[k], 1, 0) + pltpu.roll(old[k], deep - 1, 0) + left + right
                    field_s[job, c, :, lanes] = (
                        keep_s[job, :, lanes] * old[k] + step * around + pull_s[job, c, :, lanes]
                    )
        return carry

    lax.fori_loop(0, ITERS - 1, body, 0)
    is_first = lax.axis_index("sec") == 0
    seam = half - EDGE // 2
    mine = slice(ITERS, ITERS + rows)
    lead = half - LANES
    for c in range(2):
        for k in range(tiles[0]):
            lanes = slice(k * LANES, (k + 1) * LANES)
            col = lax.broadcasted_iota(jnp.int32, (rows, LANES), 1) + k * LANES
            one = field_s[0, c, mine, lanes]
            front = field_s[1, c, mine, lanes]
            if (k + 1) * LANES > seam:
                front = jnp.where((col < seam) | is_first, front, 0.0)
            total = one + front
            if k * LANES >= lead:
                back = field_s[2, c, mine, k * LANES - lead : (k + 1) * LANES - lead]
                total = total + jnp.where(col >= seam, back, 0.0)
            f1_ref[c, :, lanes] = one
            f3_ref[c, :, lanes] = front
            msg_ref[c, :, lanes] = total.astype(msg_ref.dtype)


def shards(pixels, pred, offsets, mask, base_shift, w_hidden, w_feature, feat_gain):
    secs, rows, cols, patch = pixels.shape
    hid, feat = w_feature.shape
    assert secs == 2 and rows == ITERS and feat == LANES and cols % (2 * LANES) == 0
    half = cols // 2
    width = half + 2 * EDGE
    lean = width - EDGE
    span = half + LANES
    deep = rows + 2 * REACH
    tail = 4 * rows * (span // LANES)
    full = cols + 2 * PAD
    gain = feat_gain.reshape(1, feat)
    shape = jax.ShapeDtypeStruct
    padded = shape((deep, full, feat), BF16)
    pre = pltpu.VMEM((2, 2 * width, feat), F32)

    dma = pltpu.SemaphoreType.DMA

    def call(kernel, ins, in_specs, outs, scratch, cost, limit, aliases=None):
        return pl.pallas_call(
            functools.partial(kernel, half),
            out_shape=outs,
            in_specs=in_specs,
            out_specs=tuple(VMEM for _ in outs),
            scratch_shapes=scratch,
            input_output_aliases=aliases or {},
            compiler_params=params(limit),
            cost_estimate=cost,
        )(*ins)

    def encode_cost(kind):
        return flops_of(len(pieces_of(kind, rows, 0)) * width, patch, hid, feat)

    def in_place(value):
        return pltpu.with_memory_space_constraint(value, pltpu.HBM)

    edges = shape((REACH, cols, feat), BF16)
    front, odd, wh, wf, gain, pred_a, pred_b = call(
        encode_front_kernel,
        (in_place(pixels), in_place(w_hidden), in_place(w_feature), in_place(gain), in_place(pred)), [HBM] * 5,
        (
            shape((rows, lean, feat), BF16), padded,
            shape(w_hidden.shape, BF16), shape(w_feature.shape, BF16), shape(gain.shape, F32), edges, edges,
        ),
        [pltpu.VMEM((rows, width, patch), BF16), pre, dma((rows,)), dma((5,))],
        encode_cost("front"), 12,
    )
    weights = (pixels, wh, wf, gain)
    front_in = hop(front, "sec", 1)
    pred_a = swap(pred_a, 0, True)
    pred_b = swap(pred_b, 1, True)
    pack = shape((REACH, cols + width, feat), BF16)
    odd, even, back, pack_a, pack_b = call(
        encode_border_kernel,
        (*weights, odd, offsets, mask), [VMEM] * 7,
        (padded, padded, shape((rows * lean + tail, feat), BF16), pack, pack),
        [pre], flops_of((rows + 4 * REACH) * width, patch, hid, feat), 10, {4: 0},
    )
    pack_b = swap(pack_b, 1)
    pack_a = swap(pack_a, 0)
    back_in = hop(back, "sec", -1)
    odd, even = call(
        encode_inner_kernel, (*weights, odd, even), [VMEM] * 6,
        (padded, padded), [pre], encode_cost("inner"), 10, {4: 0, 5: 1},
    )

    bands = SEG * (2 * REACH + 1)
    nodes = rows * cols

    def score_cost(part):
        return pl.CostEstimate(
            flops=int(part * nodes * 2560 * LANES), bytes_accessed=int(part * nodes * 512), transcendentals=0
        )

    halo = pltpu.VMEM((2 * REACH, full, feat), BF16)
    turning = pltpu.VMEM((2, rows, LANES, LANES), F32)
    turning4 = pltpu.VMEM((4, rows, LANES, LANES), F32)
    whole = pltpu.VMEM((deep, full, feat), BF16)
    flow0_shape = shape((2, rows, span), F32)
    scores, flow0 = call(
        near_scores_kernel, (even, odd, in_place(pred), pred_a, pred_b, offsets),
        [VMEM] * 2 + [HBM] + [VMEM] * 3, (shape((rows, bands, cols), F32), flow0_shape),
        [whole, pltpu.VMEM((rows, bands, span), F32), turning4, dma((3,))], score_cost(0.5), 18,
    )
    edge = shape((REACH, lean, feat), BF16)
    front_a, front_b = call(
        pick_kernel, (front_in,), [VMEM], (edge, edge), [],
        pl.CostEstimate(flops=0, bytes_accessed=8 * REACH * width * feat, transcendentals=0), 4,
    )
    front_b = swap(front_b, 1)
    front_a = swap(front_a, 0)
    ref_shape = shape((deep, half + 3 * PAD, feat), BF16)
    _, flow1, ref, beyond = call(
        own_scores_kernel, (even, odd, pack_a, pack_b, offsets, scores, front_in, in_place(pred)),
        [VMEM] * 7 + [HBM],
        (shape(scores.shape, F32), shape((2, rows, cols), F32), ref_shape, shape((2 * REACH, full, feat), BF16)),
        [halo, turning4, dma((2,)), dma((2,)), dma((1,))], score_cost(0.5), 14, {5: 0},
    )
    _, flow3 = call(
        front_scores_kernel, (even, ref, front_a, front_b, pred_a, pred_b, offsets, flow0),
        [VMEM] * 8, (ref_shape, shape((2, rows, cols), F32)),
        [pltpu.VMEM((rows, bands, half), F32), turning, dma((2,))], score_cost(0.5), 12, {1: 0},
    )

    tiles = 2 * (cols // LANES) + span // LANES
    pack_rows = 16 * tiles + 16 * ((tiles + 1) // 2)
    flow2, pack = call(
        back_scores_kernel, (back_in, odd, beyond, mask, flow1, flow3), [VMEM] * 6,
        (shape((3, rows, span), F32), shape((pack_rows, LANES), BF16)),
        [pltpu.VMEM((rows, bands, span), F32), turning], score_cost(0.55), 12,
    )
    flows_b = swap(pack, 1)
    flows_a = swap(pack, 0)

    wide = rows + 2 * ITERS
    f1, f3, msg = pl.pallas_call(
        functools.partial(relax_kernel, half),
        out_shape=(shape((2, rows, cols), F32), shape((2, rows, cols), F32), shape((2, rows, cols), BF16)),
        in_specs=[VMEM] * 6,
        out_specs=(VMEM,) * 3,
        scratch_shapes=[
            pltpu.VMEM((3, 2, wide, cols), F32),
            pltpu.VMEM((3, 2, wide, cols), F32),
            pltpu.VMEM((3, wide, cols), F32),
        ],
        compiler_params=params(12),
        cost_estimate=pl.CostEstimate(flops=nodes * 24 * 12 * 8, bytes_accessed=nodes * 40, transcendentals=0),
        name="relax",
    )(flows_a, flows_b, flow1, flow3, flow2, mask)

    prefix = base_shift
    for steps in range(1, lax.axis_size("sec")):
        prefix = prefix + hop(msg, "sec", steps).astype(F32)
    first = prefix + f3
    return jnp.stack([first, first + f1], axis=0)


def solution(mesh):
    in_specs = (
        P("sec", "tile", None, None),
        P("tile", None, None),
        P("sec", None, "tile", None),
        P("sec", "tile", None),
        P(None, "tile", None),
        P(),
        P(),
        P(),
    )
    out_specs = P("sec", None, "tile", None)
    return jax.shard_map(shards, mesh=mesh, in_specs=in_specs, out_specs=out_specs, check_vma=False)
```

```python
import functools

import jax
import jax.numpy as jnp
from jax import lax
from jax.experimental import pallas as pl
from jax.experimental.pallas import tpu as pltpu
from jax.sharding import PartitionSpec as P


ITERS = 8
REACH = 2
LANES = 128
BASE = 16
PAD = LANES
SEG = 16
EDGE = 16

epsilon = 1e-05
step_size = 0.2
stiffness = 0.5

F32 = jnp.float32
BF16 = jnp.bfloat16
HBM = pl.BlockSpec(memory_space=pltpu.HBM)
VMEM = pl.BlockSpec(memory_space=pltpu.VMEM)


def hop(value, axis, steps):
    count = lax.axis_size(axis)
    pairs = [(i, i + steps) for i in range(count) if 0 <= i + steps < count]
    return lax.ppermute(value, axis, pairs)


def swap(value, first, plane=False):
    tiles = lax.axis_size("tile")
    stride = lax.axis_size("sec") if plane else 1
    pairs = []
    for i in range(first, tiles - 1, 2):
        pairs += [(i * stride, (i + 1) * stride), ((i + 1) * stride, i * stride)]
    return lax.ppermute(value, ("tile", "sec") if plane else "tile", pairs)


def sides(rows):
    last = rows - REACH
    facing = jnp.where(lax.rem(lax.axis_index("tile"), 2) == 0, last, 0)
    return facing, last - facing


def params(limit):
    return pltpu.CompilerParams(vmem_limit_bytes=limit * 1024 * 1024)


def matmuls(pix, wh, wf):
    hidden = jnp.maximum(jnp.dot(pix, wh, preferred_element_type=F32), 0.0).astype(BF16)
    return jnp.dot(hidden, wf, preferred_element_type=F32)


def normed(pre, gain):
    mean = jnp.mean(pre * pre, axis=-1, keepdims=True)
    return (pre * lax.rsqrt(mean + epsilon) * gain).astype(BF16)


def encode_steps(pix_of, count, width, store, wh_ref, wf_ref, gain_ref, pre_s):
    steps = count // 2

    def finish(n):
        value = normed(pre_s[n % 2], gain_ref[...])
        store(2 * n, value[:width])
        store(2 * n + 1, value[width:])

    for n in range(steps):
        pre_s[n % 2] = matmuls(pix_of(2 * n), wh_ref[...], wf_ref[...])
        if n:
            finish(n - 1)
    finish(steps - 1)


def inner_rows(rows):
    return list(range(REACH, rows - REACH))


def pieces_of(kind, rows, far):
    inner = inner_rows(rows)
    if kind == "front":
        return [(1, r, 0) for r in range(rows)]
    return [(0, r, 0) for r in inner] + [(1, r, far) for r in inner]


def pixel_pair(pix_ref, pieces, n, width):
    rows = [pix_ref[sec, row, col0 : col0 + width, :] for sec, row, col0 in pieces[n : n + 2]]
    return jnp.concatenate(rows, 0)


def zero_sides(ref, cols):
    side = jnp.zeros((ref.shape[0], EDGE, ref.shape[2]), BF16)
    ref[:, PAD - EDGE : PAD, :] = side
    ref[:, PAD + cols : PAD + cols + EDGE, :] = side


def put_left(ref, row, value, half):
    ref[row + REACH, PAD : PAD + half, :] = value[:half]


def put_right(ref, row, value, half):
    ref[row + REACH, PAD + half : PAD + 2 * half, :] = value[value.shape[0] - half :]


def encode_front_kernel(
    half, pix_ref, wh_in, wf_in, gain_in, pred_ref,
    front_ref, odd_ref, wh_ref, wf_ref, gain_ref, pred_a_ref, pred_b_ref,
    pix_s, pre_s, sem, more_sem,
):
    rows, cols = pix_ref.shape[1:3]
    width = pix_s.shape[1]
    lean = front_ref.shape[1]
    pieces = pieces_of("front", rows, cols - width)
    loads = [
        (pix_ref.at[sec, row, col0 : col0 + width, :], pix_s.at[n])
        for n, (sec, row, col0) in enumerate(pieces)
    ]
    copies = copies_of(loads, sem)
    constants = copies_of([(wh_in, wh_ref), (wf_in, wf_ref), (gain_in, gain_ref)], more_sem)
    side_a, side_b = sides(rows)
    edges = [(pred_ref.at[pl.ds(side_a, REACH)], pred_a_ref), (pred_ref.at[pl.ds(side_b, REACH)], pred_b_ref)]
    edge_sem = more_sem.at[len(constants) :]
    is_first = lax.axis_index("sec") == 0
    for copy in copies[:2] + constants + copies[2:4]:
        copy.start()

    @pl.when(is_first)
    def _():
        start_all(edges, edge_sem)

    zero_sides(odd_ref, cols)
    for copy in constants:
        copy.wait()

    def pix_of(n):
        for copy in copies[n + 4 : n + 6]:
            copy.start()
        copies[n].wait()
        copies[n + 1].wait()
        return pix_s[n : n + 2].reshape(2 * width, pix_s.shape[2])

    def store(n, value):
        front_ref[n] = value[:lean]
        put_left(odd_ref, n, value, half)

    encode_steps(pix_of, len(pieces), width, store, wh_ref, wf_ref, gain_ref, pre_s)

    @pl.when(is_first)
    def _():
        wait_all(edges, edge_sem)


def encode_border_kernel(
    half, pix_ref, wh_ref, wf_ref, gain_ref, odd_in, off_ref, mask_ref,
    odd_ref, even_ref, back_ref, pack_a_ref, pack_b_ref, pre_s,
):
    rows, cols = pix_ref.shape[1:3]
    width = pack_a_ref.shape[1] - cols
    side_a, side_b = sides(rows)
    border = [side_a + r for r in range(REACH)] + [side_b + r for r in range(REACH)]
    far = cols - width
    lean = width - EDGE
    inner = inner_rows(rows)
    pieces = [(0, r, far) for r in border] + [(0, r, 0) for r in border] + [(1, r, far) for r in border]
    pieces += [(0, r, far) for r in inner]
    zero_sides(even_ref, cols)
    first = half // LANES - 1
    for tile in range(cols // LANES - first):
        lanes = slice((first + tile) * LANES, (first + tile + 1) * LANES)
        extra = jnp.concatenate(
            [off_ref[0, 0, :, lanes], off_ref[0, 1, :, lanes], mask_ref[0, :, lanes], mask_ref[0, :, lanes]], 0
        )
        at = rows * lean + tile * 4 * rows
        back_ref[at : at + 4 * rows, :] = extra.astype(F32).astype(BF16)

    def store(n, value):
        part, m = divmod(n, len(border))
        row = border[m] if part < 3 else inner[n - 3 * len(border)]
        pack = pack_a_ref if m < REACH else pack_b_ref
        if part == 0 or part > 2:
            back_ref[pl.ds(pl.multiple_of(row * lean, 16), lean), :] = value[EDGE:]
        if part > 2:
            put_right(even_ref, row, value, half)
        elif part == 0:
            put_right(even_ref, row, value, half)
            pack[m % REACH, half:cols, :] = value[width - half :]
        elif part == 1:
            put_left(even_ref, row, value, half)
            pack[m % REACH, 0:half, :] = value[:half]
        else:
            put_right(odd_ref, row, value, half)
            pack[m % REACH, cols : cols + width, :] = value

    encode_steps(
        lambda n: pixel_pair(pix_ref, pieces, n, width), len(pieces), width, store, wh_ref, wf_ref, gain_ref, pre_s
    )


def encode_inner_kernel(half, pix_ref, wh_ref, wf_ref, gain_ref, odd_in, even_in, odd_ref, even_ref, pre_s):
    rows, cols = pix_ref.shape[1:3]
    width = pre_s.shape[1] // 2
    inner = inner_rows(rows)
    pieces = pieces_of("inner", rows, cols - width)

    def store(n, value):
        part, m = divmod(n, len(inner))
        if part == 0:
            put_left(even_ref, inner[m], value, half)
        else:
            put_right(odd_ref, inner[m], value, half)

    encode_steps(
        lambda n: pixel_pair(pix_ref, pieces, n, width), len(pieces), width, store, wh_ref, wf_ref, gain_ref, pre_s
    )


def flops_of(nodes, patch, hid, feat):
    return pl.CostEstimate(
        flops=2 * nodes * hid * (patch + feat), bytes_accessed=nodes * 2 * (patch + feat), transcendentals=nodes
    )


def align(band, first, lift, row):
    band = pltpu.roll(band, (2 * LANES - first - BASE + 2 + lift) % LANES, 1)
    return jnp.where((row & 4) != 0, pltpu.roll(band, LANES - 4, 1), band)


def settle(band, row):
    for shift in (2, 1):
        band = jnp.where((row & shift) != 0, pltpu.roll(band, LANES - shift, 1), band)
    return band


def score_columns(query_of, window_of, rows, m_s, s_s, k, low):
    span = 2 * REACH + 1
    tall = LANES - low
    lane = lax.broadcasted_iota(jnp.int32, (8, LANES), 1)
    for rp in range(rows[0], rows[1] + 2 * REACH):
        j = rp % span
        window = window_of(rp, k, SEG * j)
        first = max(rp - 2 * REACH, rows[0])
        last = min(rp, rows[1] - 1)
        parts = [query_of(r, k, low) for r in range(first, last + 1)]
        query = jnp.concatenate(parts, 0) if len(parts) > 1 else parts[0]
        product = lax.dot_general(
            query, window, (((1,), (1,)), ((), ())), preferred_element_type=F32
        )
        for r in range(first, last + 1):
            for i in range(low // 8, LANES // 8):
                at = (r - first) * tall + 8 * i - low
                s = 8 * i + BASE - 4 + SEG * j
                near = product[at : at + 8, :LANES]
                far = product[at : at + 8, LANES:]
                if s + SEG <= LANES:
                    value, mask = near, (lane >= s) & (lane < s + SEG)
                elif s >= LANES:
                    value, mask = far, (lane >= s - LANES) & (lane < s + SEG - LANES)
                else:
                    value = jnp.where(lane >= s, near, far)
                    mask = (lane >= s) | (lane < s + SEG - LANES)
                dst = m_s.at[r, 8 * i : 8 * i + 8, :]
                if rp == r:
                    dst[...] = value
                else:
                    pltpu.store(dst, value, mask=mask)
        if rp > rows[0] + 2 * REACH and rp % 2:
            score_turn(m_s, s_s, rp - 2 * REACH - 1, k, low)


def score_turn(m_s, s_s, r, k, low):
    span = 2 * REACH + 1
    lane = lax.broadcasted_iota(jnp.int32, (8, LANES), 1)
    row = lax.broadcasted_iota(jnp.int32, (8, LANES), 0)
    groups = [jnp.zeros((8, LANES), F32)] * (low // 8)
    for i in range(low // 8, LANES // 8):
        one = align(m_s[r, 8 * i : 8 * i + 8, :], 8 * i, 0, row)
        two = align(m_s[r + 1, 8 * i : 8 * i + 8, :], 8 * i, 8, row)
        groups.append(settle(jnp.where((lane & 8) != 0, two, one), row))
    turned = jnp.concatenate(groups, 0).T
    lanes = pl.ds(pl.multiple_of(k * LANES, LANES), LANES)
    for n in range(2):
        for j in range(span):
            a = (j - r - n) % span
            at = SEG * j + 8 * n
            s_s[r + n, SEG * a : SEG * a + 8, lanes] = turned[at : at + 8]


def score_job(query_of, window_of, m_s, s_s, tiles, low=0, blocks=None):
    blocks = blocks or ((0, s_s.shape[0]),)
    first = 1 if low else 0

    def columns(m, k, low):
        for rows in blocks:
            score_columns(query_of, window_of, rows, m_s.at[m], s_s, k, low)

    if low:
        columns(0, 0, low)
    step = m_s.shape[0]
    whole, odd = (tiles - first) // step, (tiles - first) % step

    def body(n, carry):
        for m in range(step):
            columns(m, step * n + m + first, 0)
        return carry

    lax.fori_loop(0, whole, body, 0)
    for m in range(odd):
        columns(m, tiles - odd + m, 0)


def padded_query(ref, tile0=0):
    def query_of(r, k, low):
        at = pl.multiple_of((k + tile0) * LANES + PAD + low, 16)
        return ref[r + REACH, pl.ds(at, LANES - low), :]

    return query_of


def padded_window(ref, halo=None, tile0=0):
    rows = ref.shape[0] - 2 * REACH

    def window_of(rp, k, shift):
        at = pl.multiple_of((k + tile0) * LANES + (PAD - BASE) - shift, 16)
        if halo is not None and rp < REACH:
            return halo[rp, pl.ds(at, 2 * LANES), :]
        if halo is not None and rp >= rows + REACH:
            return halo[rp - rows, pl.ds(at, 2 * LANES), :]
        return ref[rp, pl.ds(at, 2 * LANES), :]

    return window_of


def flow_tile(s_s, oy, ox, lanes):
    y_low, y_high, x_low, x_high = oy < 0, oy > 0, ox < 0, ox > 0
    feat = F32(1.0 / LANES)
    by_row = {}
    for i in range(3):
        for b in range(5):
            v = [s_s[:, SEG * (i + d) + b, lanes] for d in range(3)]
            by_row[i, b] = jnp.where(y_low, v[0], jnp.where(y_high, v[2], v[1]))
    total = jnp.ones_like(oy)
    sum_y = jnp.zeros_like(oy)
    sum_x = jnp.zeros_like(oy)
    for i in range(3):
        for j in range(3):
            near = jnp.where(
                x_low, by_row[i, j], jnp.where(x_high, by_row[i, j + 2], by_row[i, j + 1])
            )
            near = near * feat
            weight = near * near
            total = total + weight
            if i != 1:
                sum_y = sum_y + weight * (i - 1)
            if j != 1:
                sum_x = sum_x + weight * (j - 1)
    return oy + sum_y / total, ox + sum_x / total


def flows_of(s_s, off_ref, flow_ref, tiles):
    def body(k, carry):
        lanes = pl.ds(pl.multiple_of(k * LANES, LANES), LANES)
        fy, fx = flow_tile(s_s, off_ref[0, :, lanes].astype(F32), off_ref[1, :, lanes].astype(F32), lanes)
        flow_ref[0, :, lanes] = fy
        flow_ref[1, :, lanes] = fx
        return carry

    lax.fori_loop(0, tiles, body, 0)


def copies_of(pairs, sem):
    return [pltpu.make_async_copy(src, dst, sem.at[n]) for n, (src, dst) in enumerate(pairs)]


def start_all(pairs, sem):
    for copy in copies_of(pairs, sem):
        copy.start()


def wait_all(pairs, sem):
    for copy in copies_of(pairs, sem):
        copy.wait()


def pick_kernel(half, front_ref, a_ref, b_ref):
    side_a, side_b = sides(front_ref.shape[0])
    for r in range(REACH):
        a_ref[r] = front_ref[side_a + r]
        b_ref[r] = front_ref[side_b + r]


def beyond_rows(rows):
    side_a, side_b = sides(rows)
    below = rows + REACH
    return jnp.where(side_a > 0, below, 0), jnp.where(side_b > 0, below, 0)


def near_scores_kernel(
    half, even_ref, odd_ref, pred_ref, pred_a_ref, pred_b_ref, off_ref,
    s_s, flow0_ref, ref0_s, s0_s, m_s, sem,
):
    rows = odd_ref.shape[0] - 2 * REACH
    cols = 2 * half
    far = half - 2 * EDGE
    is_first = lax.axis_index("sec") == 0
    tile0 = half // LANES - 1
    tiles = cols // LANES - tile0
    to = slice(PAD + far, PAD + cols)
    beyond_a, beyond_b = beyond_rows(rows)
    before = [
        (pred_ref.at[:, far:cols, :], ref0_s.at[REACH : rows + REACH, to, :]),
        (pred_a_ref.at[:, far:cols, :], ref0_s.at[pl.ds(beyond_a, REACH), to, :]),
        (pred_b_ref.at[:, far:cols, :], ref0_s.at[pl.ds(beyond_b, REACH), to, :]),
    ]

    @pl.when(is_first)
    def _():
        start_all(before, sem)

    flow0_ref[...] = jnp.zeros_like(flow0_ref)
    score_job(
        padded_query(odd_ref), padded_window(even_ref), m_s, s_s, cols // LANES, 0, ((REACH, rows - REACH),)
    )

    @pl.when(is_first)
    def _():
        zero_sides(ref0_s, cols)
        wait_all(before, sem)
        score_job(
            padded_query(even_ref, tile0), padded_window(ref0_s, None, tile0), m_s, s0_s, tiles, LANES - EDGE
        )
        flows_of(s0_s, off_ref.at[0, :, :, tile0 * LANES : cols], flow0_ref, tiles)


def own_scores_kernel(
    half, even_ref, odd_ref, pack_a_ref, pack_b_ref, off_ref, s_in, front_ref, pred_ref,
    s_s, flow_ref, ref_next, halo_next, halo_s, m_s, sem, next_sem, ref_sem,
):
    rows = odd_ref.shape[0] - 2 * REACH
    cols = 2 * half
    width = pack_a_ref.shape[1] - cols
    lean = front_ref.shape[1]
    far = cols - width
    is_first = lax.axis_index("sec") == 0
    side_a, _ = sides(rows)
    half_a = jnp.where(side_a > 0, REACH, 0)
    half_b = REACH - half_a
    halos = [
        (pack_a_ref.at[:, 0:cols, :], halo_s.at[pl.ds(half_a, REACH), PAD : PAD + cols, :]),
        (pack_b_ref.at[:, 0:cols, :], halo_s.at[pl.ds(half_b, REACH), PAD : PAD + cols, :]),
    ]
    start_all(halos, sem)
    to = slice(PAD + far, PAD + cols)
    beyond = [
        (pack_a_ref.at[:, cols : cols + width, :], halo_next.at[pl.ds(half_a, REACH), to, :]),
        (pack_b_ref.at[:, cols : cols + width, :], halo_next.at[pl.ds(half_b, REACH), to, :]),
    ]
    start_all(beyond, next_sem)
    left = slice(PAD, PAD + lean)
    inside = ref_next.at[REACH : rows + REACH, left, :]
    before = [(pred_ref.at[:, 0:lean, :], inside)]
    passed = [(front_ref, inside)]

    @pl.when(is_first)
    def _():
        start_all(before, ref_sem)

    @pl.when(jnp.logical_not(is_first))
    def _():
        start_all(passed, ref_sem)

    zero_sides(halo_s, cols)
    zero_sides(halo_next, cols)
    ref_next[:, PAD - EDGE : PAD, :] = jnp.zeros((rows + 2 * REACH, EDGE, LANES), BF16)
    wait_all(halos, sem)
    score_job(
        padded_query(odd_ref), padded_window(even_ref, halo_s), m_s, s_s, cols // LANES, 0,
        ((0, REACH), (rows - REACH, rows)),
    )
    flows_of(s_s, off_ref.at[1], flow_ref, cols // LANES)
    wait_all(beyond, next_sem)

    @pl.when(is_first)
    def _():
        wait_all(before, ref_sem)

    @pl.when(jnp.logical_not(is_first))
    def _():
        wait_all(passed, ref_sem)


def front_scores_kernel(
    half, even_ref, ref_in, front_a_ref, front_b_ref, pred_a_ref, pred_b_ref, off_ref, flow0_ref,
    ref_s, flow_ref, s_s, m_s, sem,
):
    rows = even_ref.shape[0] - 2 * REACH
    cols = 2 * half
    width = front_a_ref.shape[1]
    is_first = lax.axis_index("sec") == 0
    beyond_a, beyond_b = beyond_rows(rows)
    to_a = ref_s.at[pl.ds(beyond_a, REACH), PAD : PAD + width, :]
    to_b = ref_s.at[pl.ds(beyond_b, REACH), PAD : PAD + width, :]
    before = [(pred_a_ref.at[:, 0:width, :], to_a), (pred_b_ref.at[:, 0:width, :], to_b)]
    passed = [(front_a_ref, to_a), (front_b_ref, to_b)]

    @pl.when(is_first)
    def _():
        start_all(before, sem)
        wait_all(before, sem)

    @pl.when(jnp.logical_not(is_first))
    def _():
        start_all(passed, sem)
        wait_all(passed, sem)

    tiles = half // LANES
    score_job(padded_query(even_ref), padded_window(ref_s), m_s, s_s, tiles)
    flow_ref[:, :, half:cols] = flow0_ref[:, :, LANES:]
    flows_of(s_s, off_ref.at[0], flow_ref, tiles)


def pairs_out(pack_ref, at, tops, bottoms):
    for n, (top, bottom) in enumerate(zip(tops, bottoms)):
        pack_ref[at + 16 * n : at + 16 * n + 16, :] = jnp.concatenate([top, bottom], 0).astype(BF16)
    return at + 16 * len(tops)


def back_scores_kernel(
    half, back_ref, odd_ref, halo_ref, mask_ref, flow1_ref, flow_ref,
    flow2_ref, pack_ref, s_s, m_s,
):
    rows = odd_ref.shape[0] - 2 * REACH
    cols = 2 * half
    tile0 = half // LANES - 1
    tiles = cols // LANES - tile0
    width = (back_ref.shape[0] - 4 * rows * tiles) // rows
    far = cols - width

    def query_of(r, k, low):
        at = (k + tile0) * LANES + low - far + r * width
        return back_ref[pl.ds(pl.multiple_of(at, 16), LANES - low), :]

    score_job(query_of, padded_window(odd_ref, halo_ref, tile0), m_s, s_s, tiles, LANES - EDGE)

    def body(k, carry):
        lanes = pl.ds(pl.multiple_of(k * LANES, LANES), LANES)
        at = pl.multiple_of(k * 4 * rows + rows * width, 4 * rows)
        extra = back_ref[pl.ds(at, 4 * rows), :].astype(F32)
        fy, fx = flow_tile(s_s, extra[:rows], extra[rows : 2 * rows], lanes)
        flow2_ref[0, :, lanes] = fy
        flow2_ref[1, :, lanes] = fx
        flow2_ref[2, :, lanes] = extra[2 * rows : 3 * rows]
        return carry

    lax.fori_loop(0, tiles, body, 0)

    def tiles_of(ref, count):
        return [ref[:, n * LANES : (n + 1) * LANES] for n in range(count)]

    n = 0
    for ref, count in ((flow1_ref, cols // LANES), (flow_ref, cols // LANES), (flow2_ref, flow2_ref.shape[2] // LANES)):
        n = pairs_out(pack_ref, n, tiles_of(ref.at[0], count), tiles_of(ref.at[1], count))
    masks = []
    for ref, count in ((mask_ref.at[1], cols // LANES), (mask_ref.at[0], cols // LANES), (flow2_ref.at[2], flow2_ref.shape[2] // LANES)):
        masks += [m.astype(F32) for m in tiles_of(ref, count)]
    if len(masks) % 2:
        masks.append(masks[-1])
    pairs_out(pack_ref, n, masks[0::2], masks[1::2])


def relax_kernel(
    half, pack_a_ref, pack_b_ref, flow1_ref, flow3_ref, flow2_ref, mask_ref, f1_ref, f3_ref, msg_ref,
    field_s, pull_s, keep_s,
):
    rows, cols = flow1_ref.shape[1:]
    deep = rows + 2 * ITERS
    place = lax.axis_index("tile")
    count = lax.axis_size("tile")
    glob = place * rows + lax.broadcasted_iota(jnp.int32, (deep, LANES), 0) - ITERS
    a_below = lax.rem(place, 2) == 0
    inside = ((glob >= 0) & (glob < rows * count)).astype(F32)
    widths = (cols, cols, flow2_ref.shape[2])
    tiles = [w // LANES for w in widths]
    flows = (flow1_ref, flow3_ref, flow2_ref)
    own_masks = (mask_ref.at[1], mask_ref.at[0], flow2_ref.at[2])
    starts = [0, tiles[0], tiles[0] + tiles[1]]
    mask_at = 16 * sum(tiles)
    for job in range(3):
        for k in range(tiles[job]):
            lanes = slice(k * LANES, (k + 1) * LANES)
            at = 16 * (starts[job] + k)
            m_at = mask_at + 8 * (starts[job] + k)
            half_at = m_at // 16 * 16
            sub = slice(m_at - half_at, m_at - half_at + 8)
            side_a = pack_a_ref[at : at + 16, :].astype(F32)
            side_b = pack_b_ref[at : at + 16, :].astype(F32)
            m_a = pack_a_ref[half_at : half_at + 16, :].astype(F32)[sub]
            m_b = pack_b_ref[half_at : half_at + 16, :].astype(F32)[sub]
            upper, lower = jnp.where(a_below, side_b, side_a), jnp.where(a_below, side_a, side_b)
            m_up, m_down = jnp.where(a_below, m_b, m_a), jnp.where(a_below, m_a, m_b)
            weight = stiffness * jnp.concatenate(
                [m_up, own_masks[job][:, lanes].astype(F32), m_down], 0
            )
            keep_s[job, :, lanes] = (step_size - step_size * weight) * inside
            for c in range(2):
                flow = jnp.concatenate(
                    [upper[8 * c : 8 * c + 8], flows[job][c, :, lanes], lower[8 * c : 8 * c + 8]], 0
                )
                pull = step_size * weight * flow * inside
                pull_s[job, c, :, lanes] = pull
                field_s[job, c, :, lanes] = pull
    step = step_size * inside

    def body(n, carry):
        for job in range(3):
            for c in range(2):
                old = [field_s[job, c, :, k * LANES : (k + 1) * LANES] for k in range(tiles[job])]
                lane = lax.broadcasted_iota(jnp.int32, (deep, LANES), 1)
                nxt = [pltpu.roll(x, LANES - 1, 1) for x in old]
                prv = [pltpu.roll(x, 1, 1) for x in old]
                zero = jnp.zeros_like(old[0])
                for k in range(tiles[job]):
                    lanes = slice(k * LANES, (k + 1) * LANES)
                    right = jnp.where(lane == LANES - 1, nxt[k + 1] if k + 1 < tiles[job] else zero, nxt[k])
                    left = jnp.where(lane == 0, prv[k - 1] if k else zero, prv[k])
                    around = pltpu.roll(old[k], 1, 0) + pltpu.roll(old[k], deep - 1, 0) + left + right
                    field_s[job, c, :, lanes] = (
                        keep_s[job, :, lanes] * old[k] + step * around + pull_s[job, c, :, lanes]
                    )
        return carry

    lax.fori_loop(0, ITERS - 1, body, 0)
    is_first = lax.axis_index("sec") == 0
    seam = half - EDGE // 2
    mine = slice(ITERS, ITERS + rows)
    lead = half - LANES
    for c in range(2):
        for k in range(tiles[0]):
            lanes = slice(k * LANES, (k + 1) * LANES)
            col = lax.broadcasted_iota(jnp.int32, (rows, LANES), 1) + k * LANES
            one = field_s[0, c, mine, lanes]
            front = field_s[1, c, mine, lanes]
            if (k + 1) * LANES > seam:
                front = jnp.where((col < seam) | is_first, front, 0.0)
            total = one + front
            if k * LANES >= lead:
                back = field_s[2, c, mine, k * LANES - lead : (k + 1) * LANES - lead]
                total = total + jnp.where(col >= seam, back, 0.0)
            f1_ref[c, :, lanes] = one
            f3_ref[c, :, lanes] = front
            msg_ref[c, :, lanes] = total.astype(msg_ref.dtype)


def shards(pixels, pred, offsets, mask, base_shift, w_hidden, w_feature, feat_gain):
    secs, rows, cols, patch = pixels.shape
    hid, feat = w_feature.shape
    assert secs == 2 and rows == ITERS and feat == LANES and cols % (2 * LANES) == 0
    half = cols // 2
    width = half + 2 * EDGE
    lean = width - EDGE
    span = half + LANES
    deep = rows + 2 * REACH
    tail = 4 * rows * (span // LANES)
    full = cols + 2 * PAD
    gain = feat_gain.reshape(1, feat)
    shape = jax.ShapeDtypeStruct
    padded = shape((deep, full, feat), BF16)
    pre = pltpu.VMEM((2, 2 * width, feat), F32)

    dma = pltpu.SemaphoreType.DMA

    def call(kernel, ins, in_specs, outs, scratch, cost, limit, aliases=None):
        return pl.pallas_call(
            functools.partial(kernel, half),
            out_shape=outs,
            in_specs=in_specs,
            out_specs=tuple(VMEM for _ in outs),
            scratch_shapes=scratch,
            input_output_aliases=aliases or {},
            compiler_params=params(limit),
            cost_estimate=cost,
        )(*ins)

    def encode_cost(kind):
        return flops_of(len(pieces_of(kind, rows, 0)) * width, patch, hid, feat)

    def in_place(value):
        return pltpu.with_memory_space_constraint(value, pltpu.HBM)

    edges = shape((REACH, cols, feat), BF16)
    front, odd, wh, wf, gain, pred_a, pred_b = call(
        encode_front_kernel,
        (in_place(pixels), in_place(w_hidden), in_place(w_feature), in_place(gain), in_place(pred)), [HBM] * 5,
        (
            shape((rows, lean, feat), BF16), padded,
            shape(w_hidden.shape, BF16), shape(w_feature.shape, BF16), shape(gain.shape, F32), edges, edges,
        ),
        [pltpu.VMEM((rows, width, patch), BF16), pre, dma((rows,)), dma((5,))],
        encode_cost("front"), 12,
    )
    weights = (pixels, wh, wf, gain)
    front_in = hop(front, "sec", 1)
    pred_a = swap(pred_a, 0, True)
    pred_b = swap(pred_b, 1, True)
    pack = shape((REACH, cols + width, feat), BF16)
    odd, even, back, pack_a, pack_b = call(
        encode_border_kernel,
        (*weights, odd, offsets, mask), [VMEM] * 7,
        (padded, padded, shape((rows * lean + tail, feat), BF16), pack, pack),
        [pre], flops_of((rows + 4 * REACH) * width, patch, hid, feat), 10, {4: 0},
    )
    pack_b = swap(pack_b, 1)
    pack_a = swap(pack_a, 0)
    back_in = hop(back, "sec", -1)
    odd, even = call(
        encode_inner_kernel, (*weights, odd, even), [VMEM] * 6,
        (padded, padded), [pre], encode_cost("inner"), 10, {4: 0, 5: 1},
    )

    bands = SEG * (2 * REACH + 1)
    nodes = rows * cols

    def score_cost(part):
        return pl.CostEstimate(
            flops=int(part * nodes * 2560 * LANES), bytes_accessed=int(part * nodes * 512), transcendentals=0
        )

    halo = pltpu.VMEM((2 * REACH, full, feat), BF16)
    turning4 = pltpu.VMEM((4, rows, LANES, LANES), F32)
    whole = pltpu.VMEM((deep, full, feat), BF16)
    flow0_shape = shape((2, rows, span), F32)
    scores, flow0 = call(
        near_scores_kernel, (even, odd, in_place(pred), pred_a, pred_b, offsets),
        [VMEM] * 2 + [HBM] + [VMEM] * 3, (shape((rows, bands, cols), F32), flow0_shape),
        [whole, pltpu.VMEM((rows, bands, span), F32), turning4, dma((3,))], score_cost(0.5), 18,
    )
    edge = shape((REACH, lean, feat), BF16)
    front_a, front_b = call(
        pick_kernel, (front_in,), [VMEM], (edge, edge), [],
        pl.CostEstimate(flops=0, bytes_accessed=8 * REACH * width * feat, transcendentals=0), 4,
    )
    front_b = swap(front_b, 1)
    front_a = swap(front_a, 0)
    ref_shape = shape((deep, half + 3 * PAD, feat), BF16)
    _, flow1, ref, beyond = call(
        own_scores_kernel, (even, odd, pack_a, pack_b, offsets, scores, front_in, in_place(pred)),
        [VMEM] * 7 + [HBM],
        (shape(scores.shape, F32), shape((2, rows, cols), F32), ref_shape, shape((2 * REACH, full, feat), BF16)),
        [halo, turning4, dma((2,)), dma((2,)), dma((1,))], score_cost(0.5), 14, {5: 0},
    )
    _, flow3 = call(
        front_scores_kernel, (even, ref, front_a, front_b, pred_a, pred_b, offsets, flow0),
        [VMEM] * 8, (ref_shape, shape((2, rows, cols), F32)),
        [pltpu.VMEM((rows, bands, half), F32), turning4, dma((2,))], score_cost(0.5), 14, {1: 0},
    )

    tiles = 2 * (cols // LANES) + span // LANES
    pack_rows = 16 * tiles + 16 * ((tiles + 1) // 2)
    flow2, pack = call(
        back_scores_kernel, (back_in, odd, beyond, mask, flow1, flow3), [VMEM] * 6,
        (shape((3, rows, span), F32), shape((pack_rows, LANES), BF16)),
        [pltpu.VMEM((rows, bands, span), F32), turning4], score_cost(0.55), 14,
    )
    flows_b = swap(pack, 1)
    flows_a = swap(pack, 0)

    wide = rows + 2 * ITERS
    f1, f3, msg = pl.pallas_call(
        functools.partial(relax_kernel, half),
        out_shape=(shape((2, rows, cols), F32), shape((2, rows, cols), F32), shape((2, rows, cols), BF16)),
        in_specs=[VMEM] * 6,
        out_specs=(VMEM,) * 3,
        scratch_shapes=[
            pltpu.VMEM((3, 2, wide, cols), F32),
            pltpu.VMEM((3, 2, wide, cols), F32),
            pltpu.VMEM((3, wide, cols), F32),
        ],
        compiler_params=params(12),
        cost_estimate=pl.CostEstimate(flops=nodes * 24 * 12 * 8, bytes_accessed=nodes * 40, transcendentals=0),
        name="relax",
    )(flows_a, flows_b, flow1, flow3, flow2, mask)

    prefix = base_shift
    for steps in range(1, lax.axis_size("sec")):
        prefix = prefix + hop(msg, "sec", steps).astype(F32)
    first = prefix + f3
    return jnp.stack([first, first + f1], axis=0)


def solution(mesh):
    in_specs = (
        P("sec", "tile", None, None),
        P("tile", None, None),
        P("sec", None, "tile", None),
        P("sec", "tile", None),
        P(None, "tile", None),
        P(),
        P(),
        P(),
    )
    out_specs = P("sec", None, "tile", None)
    return jax.shard_map(shards, mesh=mesh, in_specs=in_specs, out_specs=out_specs, check_vma=False)
```
